32 devices in a mesh: ctx: 8 (over z, core), fsdp: 4 (over y, x).
Axes of the slice: x: 2, y: 2, z: 4, core: 2. Of those that a mesh axis runs over, the one named last changes fastest.
Arguments:
- tokens: bfloat16 [2, 4, 1024, 2048], P(None, 'fsdp', 'ctx'), may hold values from -6 to 6
- cotangent: bfloat16 [2, 4, 1024, 2048], P(None, 'fsdp', 'ctx'), may hold values from -6 to 6
- w_query: bfloat16 [2048, 2048], P('fsdp'), may hold values from -0.125 to 0.125
- w_key: bfloat16 [2048, 2048], P('fsdp'), may hold values from -0.125 to 0.125
- w_value: bfloat16 [2048, 4096], P('fsdp'), may hold values from -0.125 to 0.125
- w_gate: bfloat16 [2048, 4096], P('fsdp'), may hold values from -0.125 to 0.125
- w_out: bfloat16 [4096, 2048], P('fsdp'), may hold values from -0.125 to 0.125
- w_up: bfloat16 [2048, 4096], P('fsdp'), may hold values from -0.125 to 0.125
- w_down: bfloat16 [4096, 2048], P('fsdp'), may hold values from -0.125 to 0.125
- norm_gains: float32 [2, 2048], replicated, may hold values from 0.5 to 1.5
- norm_biases: float32 [2, 2048], replicated, may hold values from -1.8 to 1.8
- block_deal: int32 [16], replicated, may hold values from 0 to 15, each once
- doc_lengths: int32 [2, 4, 4], P(None, 'fsdp'), may hold values from 1 to 512, 1024 in all within a row
Outputs:
- output: bfloat16 [2, 4, 1024, 2048], P(None, 'fsdp', 'ctx')
- grad_tokens: float32 [2, 4, 1024, 2048], P(None, 'fsdp', 'ctx')
- grad_w_query: float32 [2048, 2048], P(('ctx', 'fsdp'))
- grad_w_key: float32 [2048, 2048], P(('ctx', 'fsdp'))
- grad_w_value: float32 [2048, 4096], P(('ctx', 'fsdp'))
- grad_w_gate: float32 [2048, 4096], P(('ctx', 'fsdp'))
- grad_w_out: float32 [4096, 2048], P(('ctx', 'fsdp'))
- grad_w_up: float32 [2048, 4096], P(('ctx', 'fsdp'))
- grad_w_down: float32 [4096, 2048], P(('ctx', 'fsdp'))
- grad_norm_gains: float32 [2, 2048], P(None, ('ctx', 'fsdp'))
- grad_norm_biases: float32 [2, 2048], P(None, ('ctx', 'fsdp'))
The draws below stay inside these ranges and needn't reach their ends.
Inputs may be any that keep to these rules, and one draw needn't show every extreme that they name: block_deal[b] is the position, in blocks of 64 tokens, of the b-th stored block of every sequence; each position once. `doc_lengths`: the lengths of the 4 documents of one sequence in order; they sum to 1024 and the longest is 512.
All inputs are finite; a program needn't handle non-finite values.
Results may differ from the reference program's by a relative error of at most 0.014.
The reference program's roundings to bfloat16 on the way count: a program that leaves them out, or rounds other values in their place, can miss the bound.
Values may be sent and summed in bfloat16 or wider, within the bound.
No kernel may reach another device: no remote copies, remote signals or barrier semaphores. Data moves between devices by JAX's collectives and lax.ppermute only.
A program may use at most 960 MiB of HBM per device.

```python
import math
import jax
import jax.numpy as jnp
import numpy as np
from jax import lax

D = 2048
HEADS = 8
DK = 256
DV = 512
FF = 4096
MICRO = 2
DOCS = 4
QW = 2048
VW = 4096
SEQ = 1024
LANES = 4
BLOCK = 64
NBLOCK = 16
MOST_DOC = 512


def level_of(rng, shape, cuts, least, high):
    def one(dim, blocks):
        steps = jax.random.uniform(jax.random.fold_in(jax.random.fold_in(rng, 6), dim), (blocks,), jnp.float32, least / len(cuts), high / len(cuts))
        return jnp.repeat(jnp.exp(steps), shape[dim] // blocks).reshape((-1,) + (1,) * (len(shape) - dim - 1))

    loudness = one(*cuts[0])
    for cut in cuts[1:]:
        loudness = loudness * one(*cut)
    return loudness


def length_profile(number_of, total, limit, skew):
    loads = [(1 << 20) // math.isqrt(standing ** skew) + 1 for standing in range(2, number_of + 1)]
    rest, holding = total - limit - (number_of - 1), [1] * (number_of - 1)
    while rest > 0:
        candidates = [i for i in range(number_of - 1) if holding[i] < limit]
        mass, budget = sum([loads[i] for i in candidates]), rest
        for i in candidates:
            more = min(limit - holding[i], max(1, budget * loads[i] // mass), rest)
            holding[i] = holding[i] + more
            rest = rest - more
    return np.array([limit] + holding)


def uneven_parts(own_key, amount, total, most, slope):
    if amount == 2:
        one = jax.random.randint(own_key, (), max(1, total - most), min(most, total - 1) + 1)
        return jnp.stack([one, total - one])
    tallies = jnp.asarray(length_profile(amount, total, most, slope), jnp.int32)
    couples = (amount - 1) // 2
    source_of, sink = tallies[1:1 + 2 * couples:2], tallies[2:2 + 2 * couples:2]
    slack = jnp.minimum(source_of - 1, most - sink)
    passed = jax.random.randint(jax.random.fold_in(own_key, 1), (couples,), 0, 1 << 20) % (slack + 1)
    tallies = tallies.at[1:1 + 2 * couples:2].set(source_of - passed).at[2:2 + 2 * couples:2].set(sink + passed)
    return tallies[jax.random.permutation(jax.random.fold_in(own_key, 2), amount)]


def gaussian(stream_key, shape, scale, reach, cuts=(), kind=jnp.bfloat16):
    factor_of = level_of(stream_key, shape, cuts, -0.22, 0.18) if cuts else 1.0
    array = jax.random.normal(stream_key, shape, jnp.float32) * scale * factor_of
    return jnp.minimum(jnp.maximum(array, -reach), reach).astype(kind)


def setup_inputs(seed: int = 0) -> dict:
    arg_keys = jax.random.split(jax.random.key(seed), 14)
    tokens = gaussian(arg_keys[0], (MICRO, LANES, SEQ, D), 1.0, 6.0, ((1, 4), (2, 8)))
    cotangent = gaussian(arg_keys[1], (MICRO, LANES, SEQ, D), 1.0, 6.0, ((1, 4), (2, 8)))
    w_query = gaussian(arg_keys[2], (D, QW), D ** -0.5, 0.125, ((0, 4),))
    w_key = gaussian(arg_keys[3], (D, QW), D ** -0.5, 0.125, ((0, 4),))
    w_value = gaussian(arg_keys[4], (D, VW), D ** -0.5, 0.125, ((0, 4),))
    w_gate = gaussian(arg_keys[5], (D, VW), D ** -0.5, 0.125, ((0, 4),))
    w_out = gaussian(arg_keys[6], (VW, D), (VW // 2) ** -0.5, 0.125, ((0, 4),))
    w_up = gaussian(arg_keys[7], (D, FF), D ** -0.5, 0.125, ((0, 4),))
    w_down = gaussian(arg_keys[8], (FF, D), (FF // 2) ** -0.5, 0.125, ((0, 4),))
    norm_gains = jnp.clip(1.0 + 0.1 * jax.random.normal(arg_keys[9], (2, D), jnp.float32), 0.5, 1.5)
    norm_biases = gaussian(arg_keys[10], (2, D), 0.3, 1.8, (), jnp.float32)
    block_deal = jax.random.permutation(arg_keys[11], NBLOCK).astype(jnp.int32)
    doc_lengths = jax.vmap(lambda own: uneven_parts(own, DOCS, SEQ, MOST_DOC, 0))(jax.random.split(arg_keys[12], MICRO * LANES)).reshape((MICRO, LANES, DOCS)).astype(jnp.int32)
    return dict(tokens=tokens, cotangent=cotangent, w_query=w_query, w_key=w_key, w_value=w_value, w_gate=w_gate, w_out=w_out, w_up=w_up, w_down=w_down, norm_gains=norm_gains, norm_biases=norm_biases, block_deal=block_deal, doc_lengths=doc_lengths)


epsilon = 1e-05
group_floor = 1.0

@jax.custom_vjp
def low(v):
    return lax.optimization_barrier(v.astype(jnp.bfloat16)).astype(jnp.float32)

@jax.custom_vjp
def low_back(v):
    return v

def low_keep(v):
    return (low(v), None)

def low_pass(kept, grad):
    return (grad,)

def back_keep(v):
    return (v, None)

def back_low(kept, grad):
    return (low(grad),)
low.defvjp(low_keep, low_pass)
low_back.defvjp(back_keep, back_low)

def product(left, right):
    return jnp.dot(left, right, precision=lax.Precision.HIGHEST, preferred_element_type=jnp.float32)

def layer_norm(values, gain_row, offset):
    center = lax.optimization_barrier(jnp.mean(values, axis=-1, keepdims=True))
    centred = values - center
    spread = lax.optimization_barrier(jnp.mean(centred * centred, axis=-1, keepdims=True))
    return centred * lax.rsqrt(spread + epsilon) * gain_row + offset

def gated_mix(gate_pre, retained):
    number = retained.shape[0]
    grouped = retained.reshape(number, -1, DV)
    center = lax.optimization_barrier(jnp.mean(grouped, axis=-1, keepdims=True))
    centred = grouped - center
    spread = lax.optimization_barrier(jnp.mean(centred * centred, axis=-1, keepdims=True))
    normed = (centred * lax.rsqrt(spread + group_floor)).reshape(number, -1)
    return jax.nn.silu(gate_pre) * normed

def forward(rows_in, params, key_pos, key_doc):
    w_query, w_key, w_value, w_gate, w_out, w_up, w_down, norm_gains, norm_biases = params
    length_all = rows_in.shape[0]
    normed_one = low(layer_norm(rows_in, norm_gains[0], norm_biases[0]))
    query_all = low(low_back(product(normed_one, w_query)))
    key_all = low(low_back(product(normed_one, w_key)))
    value_all = low(low_back(product(normed_one, w_value)))
    gate_pre = low_back(product(normed_one, w_gate))
    keeping = (key_pos[:, None] >= key_pos[None, :]) & (key_doc[:, None] == key_doc[None, :])
    spacing = jnp.where(keeping, (key_pos[:, None] - key_pos[None, :]).astype(jnp.float32), jnp.zeros((), jnp.float32))
    scaling = jnp.asarray(DK ** (-0.5), jnp.float32)
    head_ids = jnp.arange(HEADS, dtype=jnp.int32).astype(jnp.float32)
    decay_log = jnp.log1p(-jnp.exp2(-5.0 - head_ids))

    def one_head(inputs):
        head_query, head_key, head_value, head_rate = inputs
        scores = low_back(product(head_query, head_key.T))
        table = jnp.where(keeping, jnp.exp(head_rate * spacing) * scaling, jnp.zeros((), jnp.float32))
        attend = low(scores * table)
        return low_back(product(attend, head_value))
    checked_head = jax.checkpoint(one_head)

    def head_step(carry, inputs):
        return (carry, checked_head(inputs))
    split_query = query_all.reshape(length_all, HEADS, DK).transpose(1, 0, 2)
    split_key = key_all.reshape(length_all, HEADS, DK).transpose(1, 0, 2)
    split_value = value_all.reshape(length_all, HEADS, DV).transpose(1, 0, 2)
    unused, retained = lax.scan(head_step, jnp.zeros((), jnp.float32), (split_query, split_key, split_value, decay_log))
    retained = retained.transpose(1, 0, 2).reshape(length_all, VW)
    mixed = low(gated_mix(gate_pre, retained))
    attn_out = low_back(product(mixed, w_out))
    hidden = rows_in + attn_out
    normed_two = low(layer_norm(hidden, norm_gains[1], norm_biases[1]))
    up_pre = low_back(product(normed_two, w_up))
    active = low(jax.nn.gelu(up_pre, approximate=False))
    ffn_out = low_back(product(active, w_down))
    return hidden + ffn_out

def reference(tokens, cotangent, w_query, w_key, w_value, w_gate, w_out, w_up, w_down, norm_gains, norm_biases, block_deal, doc_lengths):
    stored = jnp.arange(SEQ, dtype=jnp.int32)
    block_of = (stored // BLOCK).astype(jnp.int32)
    key_pos = (block_deal.astype(jnp.int32)[block_of] * BLOCK + stored % BLOCK).astype(jnp.int32)
    flat_rows = tokens.reshape(MICRO * LANES, SEQ, D).astype(jnp.float32)
    flat_cot = cotangent.reshape(MICRO * LANES, SEQ, D).astype(jnp.float32)
    flat_sizes = doc_lengths.reshape(MICRO * LANES, DOCS).astype(jnp.int32)
    params = tuple((weight_arr.astype(jnp.float32) for weight_arr in (w_query, w_key, w_value, w_gate, w_out, w_up, w_down, norm_gains, norm_biases)))
    zeros_all = tuple((jnp.zeros_like(weight_arr) for weight_arr in params))

    def one_sequence(totals, inputs):
        rows_in, cot_rows, sizes_now = inputs
        starts = (jnp.cumsum(sizes_now, dtype=jnp.int32) - sizes_now).astype(jnp.int32)
        hits = (key_pos[:, None] >= starts[None, :]).astype(jnp.int32)
        key_doc = (lax.optimization_barrier(jnp.sum(hits, axis=1, dtype=jnp.int32)) - 1).astype(jnp.int32)

        def apply_layer(rows_arg, params_arg):
            return forward(rows_arg, params_arg, key_pos, key_doc)
        result, pull_back = jax.vjp(apply_layer, rows_in, params)
        grad_rows, grad_params = pull_back(cot_rows)
        totals = tuple((running + extra for running, extra in zip(totals, grad_params)))
        return (totals, (result.astype(jnp.bfloat16), grad_rows))
    totals, (outputs, grad_rows) = lax.scan(one_sequence, zeros_all, (flat_rows, flat_cot, flat_sizes))
    grad_scale = float(MICRO * LANES * SEQ) ** (-0.5)
    totals = tuple((running * grad_scale for running in totals))
    output = outputs.reshape(MICRO, LANES, SEQ, D)
    grad_tokens = grad_rows.reshape(MICRO, LANES, SEQ, D)
    return (output, grad_tokens, totals[0], totals[1], totals[2], totals[3], totals[4], totals[5], totals[6], totals[7], totals[8])
```

```python
import jax
import jax.numpy as jnp
from jax import lax
from jax.sharding import PartitionSpec as P

HEADS = 8
DK = 256
DV = 512
FF = 4096
MICRO = 2
QW = 2048
VW = 4096
BLOCK = 64


epsilon = 1e-05
group_floor = 1.0


def layer_norm(values, gain_row, offset):
    center = jnp.mean(values, axis=-1, keepdims=True)
    centred = values - center
    spread = jnp.mean(centred * centred, axis=-1, keepdims=True)
    return centred * lax.rsqrt(spread + epsilon) * gain_row + offset


def gated_mix(gate_pre, retained):
    number = retained.shape[0]
    grouped = retained.reshape(number, -1, DV)
    center = jnp.mean(grouped, axis=-1, keepdims=True)
    centred = grouped - center
    spread = jnp.mean(centred * centred, axis=-1, keepdims=True)
    normed = (centred * lax.rsqrt(spread + group_floor)).reshape(number, -1)
    return jax.nn.silu(gate_pre) * normed


def smooth_act(values):
    return jax.nn.gelu(values, approximate=False)


def stored_positions(block_deal, full_length, block_size):
    stored = jnp.arange(full_length, dtype=jnp.int32)
    block_ids = stored // block_size
    slots_all = jnp.arange(block_deal.shape[0], dtype=jnp.int32)
    picked = jnp.sum(
        jnp.where(block_ids[:, None] == slots_all[None, :], block_deal[None, :], 0),
        axis=1,
        dtype=jnp.int32,
    )
    return picked * block_size + stored % block_size


def document_ids(positions, doc_sizes):
    starts = jnp.cumsum(doc_sizes, dtype=jnp.int32) - doc_sizes
    return (
        jnp.sum((positions[:, None] >= starts[None, :]).astype(jnp.int32), axis=1, dtype=jnp.int32)
        - 1
    )


def decay_table(query_pos, query_doc, key_pos, key_doc, decay_log, scaling):
    keeping = (query_pos[:, None] >= key_pos[None, :]) & (query_doc[:, None] == key_doc[None, :])
    spacing = jnp.where(keeping, (query_pos[:, None] - key_pos[None, :]).astype(jnp.float32), 0.0)
    factor = jnp.exp(decay_log[:, None, None] * spacing[None])
    return jnp.where(keeping[None], factor * scaling, 0.0)


def contract_rows(left, right):
    return lax.dot_general(
        left, right, (((1,), (1,)), ((), ())), preferred_element_type=jnp.float32
    )


def contract_cols(left, right):
    return lax.dot_general(
        left, right, (((0,), (0,)), ((), ())), preferred_element_type=jnp.float32
    )


def add_single(left, weight_piece):
    return jnp.dot(left, weight_piece, preferred_element_type=jnp.float32)


def back_rows(left, weight_piece):
    return contract_rows(left, weight_piece)


def weight_term(kept_acts, number):
    normed_one, grads_in, normed_two, grads_up, mixed_all, grads_attn, active_all, grads_ffn = (
        kept_acts
    )
    pieces = [
        contract_cols(normed_one, grads_in),
        contract_cols(normed_two, grads_up),
        contract_cols(mixed_all, grads_attn).reshape(number, -1),
        contract_cols(active_all, grads_ffn).reshape(number, -1),
    ]
    return jnp.concatenate(pieces, axis=1)


def body(
    tokens,
    cotangent,
    w_query,
    w_key,
    w_value,
    w_gate,
    w_out,
    w_up,
    w_down,
    norm_gains,
    norm_biases,
    block_deal,
    doc_lengths,
):
    ctx_size = lax.axis_size("ctx")
    tok_rows = tokens.shape[2]
    full_length = tok_rows * ctx_size
    model_width = tokens.shape[3]
    share_rows = model_width // lax.axis_size(("ctx", "fsdp"))
    grad_scale = float(MICRO * lax.axis_size("fsdp") * full_length) ** (-0.5)
    own_start = lax.axis_index("ctx") * tok_rows
    key_pos = stored_positions(block_deal, full_length, BLOCK)
    query_pos = lax.dynamic_slice_in_dim(key_pos, own_start, tok_rows)
    decay_log = jnp.log1p(-jnp.exp2(-5.0 - jnp.arange(HEADS).astype(jnp.float32)))
    scaling = DK ** (-0.5)
    out_list = []
    grad_list = []
    weight_sum = None
    gain_sum = jnp.zeros((2, model_width), jnp.float32)
    bias_sum = jnp.zeros((2, model_width), jnp.float32)
    for batch_index in range(MICRO):
        rows_in = tokens[batch_index, 0].astype(jnp.float32)
        grad_rows = cotangent[batch_index, 0].astype(jnp.float32)
        key_doc = document_ids(key_pos, doc_lengths[batch_index, 0])
        query_doc = lax.dynamic_slice_in_dim(key_doc, own_start, tok_rows)
        table = decay_table(query_pos, query_doc, key_pos, key_doc, decay_log, scaling)
        normed_one, norm_pull_one = jax.vjp(layer_norm, rows_in, norm_gains[0], norm_biases[0])
        low_one = normed_one.astype(jnp.bfloat16)
        pieces = (
            lax.all_gather(w_query, "fsdp", axis=0, tiled=True),
            lax.all_gather(w_key, "fsdp", axis=0, tiled=True),
            lax.all_gather(w_value, "fsdp", axis=0, tiled=True),
            lax.all_gather(w_gate, "fsdp", axis=0, tiled=True),
        )
        query_f, key_f, value_f, gate_pre = tuple(
            (
                jnp.dot(low_one, weight_piece, preferred_element_type=jnp.float32)
                for weight_piece in pieces
            )
        )
        query_low = query_f.astype(jnp.bfloat16)
        key_low = key_f.astype(jnp.bfloat16)
        value_low = value_f.astype(jnp.bfloat16)
        keys_all, values_all = (
            lax.all_gather(key_low, "ctx", axis=0, tiled=True),
            lax.all_gather(value_low, "ctx", axis=0, tiled=True),
        )
        query_heads = query_low.reshape(tok_rows, HEADS, DK)
        key_heads = keys_all.reshape(full_length, HEADS, DK)
        value_heads = values_all.reshape(full_length, HEADS, DV)
        scores = jnp.einsum(
            "thd,shd->hts", query_heads, key_heads, preferred_element_type=jnp.float32
        )
        attend = (scores * table).astype(jnp.bfloat16)
        retained = jnp.einsum(
            "hts,shd->thd", attend, value_heads, preferred_element_type=jnp.float32
        ).reshape(tok_rows, VW)
        mixed, mix_pull = jax.vjp(gated_mix, gate_pre, retained)
        mixed_low = mixed.astype(jnp.bfloat16)
        attn_out = add_single(mixed_low, lax.all_gather(w_out, "fsdp", axis=0, tiled=True))
        hidden = rows_in + attn_out
        normed_two, norm_pull_two = jax.vjp(layer_norm, hidden, norm_gains[1], norm_biases[1])
        low_two = normed_two.astype(jnp.bfloat16)
        up_pre = add_single(low_two, lax.all_gather(w_up, "fsdp", axis=0, tiled=True))
        active, act_pull = jax.vjp(smooth_act, up_pre)
        active_low = active.astype(jnp.bfloat16)
        ffn_out = add_single(active_low, lax.all_gather(w_down, "fsdp", axis=0, tiled=True))
        out_list.append((hidden + ffn_out).astype(jnp.bfloat16))
        grad_ffn = grad_rows.astype(jnp.bfloat16)
        grad_act = back_rows(grad_ffn, lax.all_gather(w_down, "fsdp", axis=0, tiled=True))
        grad_up = act_pull(grad_act)[0].astype(jnp.bfloat16)
        grad_norm_two = back_rows(grad_up, lax.all_gather(w_up, "fsdp", axis=0, tiled=True))
        grad_hidden_ln, grad_gain_two, grad_bias_two = norm_pull_two(grad_norm_two)
        grad_hidden = grad_rows + grad_hidden_ln
        grad_attn = grad_hidden.astype(jnp.bfloat16)
        grad_mixed = back_rows(grad_attn, lax.all_gather(w_out, "fsdp", axis=0, tiled=True))
        grad_gate_f, grad_ret_f = mix_pull(grad_mixed)
        grad_gate = grad_gate_f.astype(jnp.bfloat16)
        ret_low = grad_ret_f.astype(jnp.bfloat16)
        ret_heads = ret_low.reshape(tok_rows, HEADS, DV)
        grad_attend = jnp.einsum(
            "thd,shd->hts", ret_heads, value_heads, preferred_element_type=jnp.float32
        )
        grad_scores = (grad_attend * table).astype(jnp.bfloat16)
        grad_query = (
            jnp.einsum("hts,shd->thd", grad_scores, key_heads, preferred_element_type=jnp.float32)
            .reshape(tok_rows, QW)
            .astype(jnp.bfloat16)
        )
        key_part = jnp.einsum(
            "hts,thd->shd", grad_scores, query_heads, preferred_element_type=jnp.float32
        ).reshape(tok_rows * lax.axis_size("ctx"), QW)
        value_part = jnp.einsum(
            "hts,thd->shd", attend, ret_heads, preferred_element_type=jnp.float32
        ).reshape(tok_rows * lax.axis_size("ctx"), VW)
        key_value_sum = lax.psum_scatter(
            jnp.concatenate([key_part, value_part], axis=1).astype(jnp.bfloat16),
            "ctx",
            scatter_dimension=0,
            tiled=True,
        ).astype(jnp.float32)
        grad_key = key_value_sum[:, :QW].astype(jnp.bfloat16)
        grad_value = key_value_sum[:, QW:].astype(jnp.bfloat16)
        term_now = (
            contract_rows(grad_query, lax.all_gather(w_query, "fsdp", axis=0, tiled=True))
            + contract_rows(grad_key, lax.all_gather(w_key, "fsdp", axis=0, tiled=True))
            + contract_rows(grad_value, lax.all_gather(w_value, "fsdp", axis=0, tiled=True))
            + contract_rows(grad_gate, lax.all_gather(w_gate, "fsdp", axis=0, tiled=True))
        )
        grad_rows_ln, grad_gain_one, grad_bias_one = norm_pull_one(term_now)
        grad_list.append(grad_hidden + grad_rows_ln)
        gain_sum = gain_sum + jnp.stack([grad_gain_one, grad_gain_two])
        bias_sum = bias_sum + jnp.stack([grad_bias_one, grad_bias_two])
        kept_now = (
            low_one,
            jnp.concatenate([grad_query, grad_key, grad_value, grad_gate], axis=1),
            low_two,
            grad_up,
            mixed_low,
            grad_attn,
            active_low,
            grad_ffn,
        )
        term_sum = lax.psum_scatter(
            weight_term(kept_now, share_rows * lax.axis_size(("ctx", "fsdp"))),
            ("ctx", "fsdp"),
            scatter_dimension=0,
            tiled=True,
        )
        weight_sum = term_sum if weight_sum is None else weight_sum + term_sum
    weight_sum = weight_sum * grad_scale
    bounds = [QW, 2 * QW, 2 * QW + VW, 2 * QW + 2 * VW, 2 * QW + 2 * VW + FF, 2 * QW + 3 * VW + FF]
    g_query, g_key, g_value, g_gate, g_up, g_out_flat, g_down_flat = jnp.split(
        weight_sum, bounds, axis=1
    )
    g_out = g_out_flat.reshape(share_rows * (VW // model_width), model_width)
    g_down = g_down_flat.reshape(share_rows * (FF // model_width), model_width)
    gain_grads, bias_grads = (
        lax.psum_scatter(gain_sum, ("ctx", "fsdp"), scatter_dimension=1, tiled=True),
        lax.psum_scatter(bias_sum, ("ctx", "fsdp"), scatter_dimension=1, tiled=True),
    )
    gain_grads = gain_grads * grad_scale
    bias_grads = bias_grads * grad_scale
    output = jnp.stack(out_list)[:, None]
    grad_tokens = jnp.stack(grad_list)[:, None]
    return (
        output,
        grad_tokens,
        g_query,
        g_key,
        g_value,
        g_gate,
        g_out,
        g_up,
        g_down,
        gain_grads,
        bias_grads,
    )


def xy_swap(x, bit):
    return lax.ppermute(x, "fsdp", [(i, i ^ bit) for i in range(lax.axis_size("fsdp"))])


def core_swap(x):
    return lax.ppermute(x, "ctx", [(i, i ^ 1) for i in range(lax.axis_size("ctx"))])


def after(x, *earlier):
    return lax.optimization_barrier((x,) + tuple(earlier))[0]


def gather_first(x):
    return xy_swap(x, 1), xy_swap(x, 2)


def gather_second(x, first, second):
    half = x.shape[0] // 2
    low_part = xy_swap(first[:half], 2)
    high_part = xy_swap(second[half:], 1)
    return [x, first, second, jnp.concatenate([low_part, high_part], axis=0)]


def plane_gather(x):
    return gather_second(x, *gather_first(x))


def plane_reduce(blocks):
    half = blocks[0].shape[-1] // 2
    left = [b[..., :half] for b in blocks]
    right = [b[..., half:] for b in blocks]
    left_in = xy_swap(jnp.stack([left[1], left[3]]), 1).astype(jnp.float32)
    right_in = xy_swap(jnp.stack([right[2], right[3]]), 2).astype(jnp.float32)
    left_far = left[2].astype(jnp.float32) + left_in[1]
    right_far = right[1].astype(jnp.float32) + right_in[1]
    left_last = xy_swap(left_far.astype(jnp.bfloat16), 2).astype(jnp.float32)
    right_last = xy_swap(right_far.astype(jnp.bfloat16), 1).astype(jnp.float32)
    left_own = left[0].astype(jnp.float32) + left_in[0]
    right_own = right[0].astype(jnp.float32) + right_in[0]
    return jnp.concatenate([left_own + left_last, right_own + right_last], axis=-1)


def sum_everywhere(x):
    for axis in ("ctx", "fsdp"):
        size = lax.axis_size(axis)
        bit = 1
        while bit < size:
            x = x + lax.ppermute(x, axis, [(i, i ^ bit) for i in range(size)])
            bit *= 2
    return x


def in_rank_order(blocks, rank):
    odd = (rank % 2) == 1
    upper = (rank // 2) == 1
    one = [
        jnp.where(odd, blocks[1], blocks[0]),
        jnp.where(odd, blocks[0], blocks[1]),
        jnp.where(odd, blocks[3], blocks[2]),
        jnp.where(odd, blocks[2], blocks[3]),
    ]
    return [
        jnp.where(upper, one[2], one[0]),
        jnp.where(upper, one[3], one[1]),
        jnp.where(upper, one[0], one[2]),
        jnp.where(upper, one[1], one[3]),
    ]


def pick(x, index, size, axis):
    return lax.dynamic_slice_in_dim(x, index * size, size, axis)


def head_columns(w_query, w_key, w_value, w_gate, ctx_rank):
    return jnp.concatenate(
        [
            pick(w_query, ctx_rank, DK, 1),
            pick(w_key, ctx_rank, DK, 1),
            pick(w_value, ctx_rank, DV, 1),
            pick(w_gate, ctx_rank, DV, 1),
        ],
        axis=1,
    )


def out_quarter(w_out, ctx_rank, fsdp_rank, ctx_size, fsdp_size):
    held = pick(w_out, ctx_rank % 2, DV, 0)
    source = ctx_rank // 2
    rows = DV // fsdp_size
    own = pick(held, fsdp_rank, rows, 0)
    quarter = jnp.where(fsdp_rank == source, own, jnp.zeros_like(own))
    for bit in range(1, fsdp_size):
        pairs = [
            (c * fsdp_size + c // 2, c * fsdp_size + ((c // 2) ^ bit)) for c in range(ctx_size)
        ]
        came = lax.ppermute(pick(held, fsdp_rank ^ bit, rows, 0), ("ctx", "fsdp"), pairs)
        quarter = jnp.where((fsdp_rank ^ source) == bit, came, quarter)
    return quarter


def exchange(pieces_of):
    core = lax.axis_index("ctx") % 2
    return [xy_swap(pieces_of(bit, core), bit) for bit in (1, 2, 3)]


def exchanged(pieces_of, mine, axis, fsdp_rank):
    even = (lax.axis_index("ctx") % 2) == 0
    other = core_swap(jnp.stack(mine))
    blocks = [jnp.concatenate([pieces_of(0, 0), pieces_of(0, 1)], axis=axis)]
    for number in range(3):
        one, two = mine[number], other[number]
        pair = [jnp.where(even, one, two), jnp.where(even, two, one)]
        blocks.append(jnp.concatenate(pair, axis=axis))
    return jnp.concatenate(in_rank_order(blocks, fsdp_rank), axis=0)


def up_pieces(w_up, fsdp_rank, ctx_size, fsdp_size):
    rows = w_up.shape[0]
    unit = FF // (ctx_size * fsdp_size)
    half = ctx_size // 2
    view = w_up.reshape(rows, ctx_size, fsdp_size * unit)

    def piece(bit, part):
        place = (0, part * half, (fsdp_rank ^ bit) * unit)
        return lax.dynamic_slice(view, place, (rows, half, unit)).reshape(rows, half * unit)

    return piece


def down_pieces(w_down, fsdp_rank, ctx_size, fsdp_size):
    unit = FF // (ctx_size * fsdp_size)
    width = w_down.shape[1]
    view = w_down.reshape(2, fsdp_size * unit, width)

    def piece(bit, part):
        return lax.dynamic_slice(view, (part, (fsdp_rank ^ bit) * unit, 0), (1, unit, width))[0]

    return piece


def smooth_parts(values):
    share = 0.5 + 0.5 * lax.erf(values * (0.5**0.5))
    density = jnp.exp(-0.5 * values * values) * ((0.5 / jnp.pi) ** 0.5)
    return values * share, share + values * density


def one_table(pos, doc, rate, scaling):
    keeping = (pos[:, None] >= pos[None, :]) & (doc[:, None] == doc[None, :])
    spacing = jnp.where(keeping, (pos[:, None] - pos[None, :]).astype(jnp.float32), 0.0)
    return jnp.where(keeping, jnp.exp(rate * spacing) * scaling, 0.0)


def ctx_sum(x):
    return lax.psum_scatter(x, "ctx", scatter_dimension=0, tiled=True)


def body_heads(
    tokens,
    cotangent,
    w_query,
    w_key,
    w_value,
    w_gate,
    w_out,
    w_up,
    w_down,
    norm_gains,
    norm_biases,
    block_deal,
    doc_lengths,
):
    low = jnp.bfloat16
    ctx_size = lax.axis_size("ctx")
    fsdp_size = lax.axis_size("fsdp")
    tok_rows = tokens.shape[2]
    full_length = tok_rows * ctx_size
    width = tokens.shape[3]
    share = width // (ctx_size * fsdp_size)
    grad_scale = float(MICRO * fsdp_size * full_length) ** (-0.5)
    ctx_rank = lax.axis_index("ctx")
    fsdp_rank = lax.axis_index("fsdp")
    pos = stored_positions(block_deal, full_length, BLOCK)
    rate = jnp.log1p(-jnp.exp2(-5.0 - ctx_rank.astype(jnp.float32)))
    scaling = DK ** (-0.5)

    rows_in = [tokens[m, 0].astype(jnp.float32) for m in range(MICRO)]
    grad_rows = [cotangent[m, 0].astype(jnp.float32) for m in range(MICRO)]
    norm_one = [jax.vjp(layer_norm, rows_in[m], norm_gains[0], norm_biases[0]) for m in range(MICRO)]
    x_all = [
        lax.all_gather(norm_one[m][0].astype(low), "ctx", axis=0, tiled=True) for m in range(MICRO)
    ]
    own_in = head_columns(w_query, w_key, w_value, w_gate, ctx_rank)
    in_first = gather_first(own_in)
    in_blocks = gather_second(own_in, *in_first)
    w_in = jnp.concatenate(in_rank_order(in_blocks, fsdp_rank), axis=0)
    quarter = out_quarter(after(w_out, *in_first), ctx_rank, fsdp_rank, ctx_size, fsdp_size)
    quarter = after(quarter, in_blocks[3])
    out_first = gather_first(quarter)
    up_piece = up_pieces(after(w_up, quarter), fsdp_rank, ctx_size, fsdp_size)
    up_mine = exchange(up_piece)
    out_blocks = gather_second(quarter, *out_first)
    w_head = jnp.concatenate(in_rank_order(out_blocks, fsdp_rank), axis=0)
    down_piece = down_pieces(after(w_down, *up_mine), fsdp_rank, ctx_size, fsdp_size)
    down_mine = exchange(down_piece)
    cot_first = [None] * MICRO
    cot_in = [None] * MICRO
    earlier = down_mine
    for m in range(MICRO):
        cot_in[m] = after(cotangent[m, 0], *earlier)
        cot_first[m] = gather_first(cot_in[m])
        earlier = cot_first[m]
    up_own = exchanged(up_piece, up_mine, 1, fsdp_rank)
    down_own = exchanged(down_piece, down_mine, 0, fsdp_rank)

    kept = []
    attn_out = []
    for m in range(MICRO):
        doc = document_ids(pos, doc_lengths[m, 0])
        table = one_table(pos, doc, rate, scaling)
        joint = jnp.dot(x_all[m], w_in[:, : 2 * DK + DV], preferred_element_type=jnp.float32).astype(low)
        gate_pre = jnp.dot(x_all[m], w_in[:, 2 * DK + DV :], preferred_element_type=jnp.float32)
        query, key, value = joint[:, :DK], joint[:, DK : 2 * DK], joint[:, 2 * DK :]
        attend = (contract_rows(query, key) * table).astype(low)
        retained = add_single(attend, value)
        mixed, mix_pull = jax.vjp(gated_mix, gate_pre, retained)
        mixed_low = mixed.astype(low)
        part = add_single(mixed_low, w_head).astype(low)
        if m == 0:
            part = after(part, *x_all[1:], *up_mine)
        else:
            part = after(part, up_own, down_own)
        attn_out.append(ctx_sum(part))
        kept.append((table, query, key, value, attend, mix_pull, mixed_low))

    outs = [None] * MICRO
    grad_attn = []
    grad_hidden = []
    ffn_kept = []
    cot_all = []
    norm_two_terms = []
    for m in range(MICRO):
        hidden = rows_in[m] + attn_out[m].astype(jnp.float32)
        normed_two, pull_two = jax.vjp(layer_norm, hidden, norm_gains[1], norm_biases[1])
        two_own = after(normed_two.astype(low), *cot_first[m])
        two_all = jnp.concatenate(plane_gather(two_own), axis=0)
        cot_all.append(jnp.concatenate(gather_second(cot_in[m], *cot_first[m]), axis=0))
        active, slope = smooth_parts(add_single(two_all, up_own))
        active_low, slope = lax.optimization_barrier((active.astype(low), slope))
        grad_up = (back_rows(cot_all[m], down_own) * slope).astype(low)
        norm_part = back_rows(grad_up, up_own).astype(low)
        cut = [norm_part[j * tok_rows : (j + 1) * tok_rows] for j in range(fsdp_size)]
        grad_norm_two = plane_reduce(cut)
        grad_ln, gain_two, bias_two = pull_two(grad_norm_two)
        norm_two_terms.append((gain_two, bias_two))
        total = grad_rows[m] + grad_ln
        grad_hidden.append(total)
        grad_attn.append(total.astype(low))
        ffn_kept.append((two_all, grad_up, active_low, hidden))

    grad_all = [lax.all_gather(grad_attn[m], "ctx", axis=0, tiled=True) for m in range(MICRO)]

    both = lambda number: jnp.concatenate([ffn_kept[m][number] for m in range(MICRO)], axis=0)
    up_grad = contract_cols(both(0), both(1)).astype(low)
    down_grad = contract_cols(both(2), jnp.concatenate(cot_all, axis=0)).astype(low)
    for m in range(MICRO):
        ffn_part = add_single(after(ffn_kept[m][2], *grad_attn[: m + 1]), down_own).astype(low)
        cut = [ffn_part[j * tok_rows : (j + 1) * tok_rows] for j in range(fsdp_size)]
        outs[m] = (ffn_kept[m][3] + plane_reduce(cut)).astype(low)

    grads_in = []
    terms = []
    for m in range(MICRO):
        table, query, key, value, attend, mix_pull, mixed_low = kept[m]
        grad_mixed = back_rows(grad_all[m], w_head)
        grad_gate, grad_ret = mix_pull(grad_mixed)
        ret_low = grad_ret.astype(low)
        grad_scores = (contract_rows(ret_low, value) * table).astype(low)
        grad_query = add_single(grad_scores, key).astype(low)
        grad_key = contract_cols(grad_scores, query).astype(low)
        grad_value = contract_cols(attend, ret_low).astype(low)
        grad_in = jnp.concatenate([grad_query, grad_key, grad_value, grad_gate.astype(low)], axis=1)
        grads_in.append(grad_in)
        part = back_rows(grad_in, w_in).astype(low)
        if m == 0:
            part = after(part, *grad_all[1:])
        terms.append(part)
    sums = [ctx_sum(terms[m]) for m in range(MICRO)]
    up_sum = ctx_sum(after(up_grad, *terms))
    down_sum = ctx_sum(after(down_grad, up_sum))

    grad_tokens = []
    norm_one_terms = []
    for m in range(MICRO):
        grad_ln, gain_one, bias_one = norm_one[m][1](sums[m].astype(jnp.float32))
        norm_one_terms.append((gain_one, bias_one))
        grad_tokens.append(grad_hidden[m] + grad_ln)

    in_term = contract_cols(
        after(jnp.concatenate(x_all, axis=0), *terms), jnp.concatenate(grads_in, axis=0)
    ).astype(low)
    in_view = in_term.reshape(ctx_size, fsdp_size, share, -1)
    in_sum = plane_reduce([pick(in_view, fsdp_rank ^ j, 1, 1)[:, 0] for j in range(fsdp_size)])
    in_mine = lax.all_to_all(in_sum.astype(low), "ctx", split_axis=0, concat_axis=0, tiled=True)
    out_term = contract_cols(
        jnp.concatenate([kept[m][6] for m in range(MICRO)], axis=0),
        jnp.concatenate(grad_all, axis=0),
    ).astype(low)
    rows = DV // fsdp_size
    g_out = plane_reduce([pick(out_term, fsdp_rank ^ j, rows, 0) for j in range(fsdp_size)])

    def by_head(first, size):
        part = in_mine[:, :, first : first + size].transpose(1, 0, 2)
        return part.reshape(share, -1).astype(jnp.float32) * grad_scale

    g_query = by_head(0, DK)
    g_key = by_head(DK, DK)
    g_value = by_head(2 * DK, DV)
    g_gate = by_head(2 * DK + DV, DV)

    up_view = up_sum.reshape(fsdp_size, share, -1)
    pieces = [lax.dynamic_index_in_dim(up_view, fsdp_rank, 0, keepdims=False)]
    for bit in range(1, fsdp_size):
        pieces.append(
            xy_swap(lax.dynamic_index_in_dim(up_view, fsdp_rank ^ bit, 0, keepdims=False), bit)
        )
    pieces = [p.reshape(share, ctx_size, -1) for p in in_rank_order(pieces, fsdp_rank)]
    g_up = jnp.stack(pieces, axis=2).reshape(share, FF).astype(jnp.float32) * grad_scale

    gain_rows = [sum(t[0] for t in norm_one_terms), sum(t[0] for t in norm_two_terms)]
    bias_rows = [sum(t[1] for t in norm_one_terms), sum(t[1] for t in norm_two_terms)]
    norm_sums = sum_everywhere(jnp.stack(gain_rows + bias_rows))
    norm_sums = pick(norm_sums, ctx_rank * fsdp_size + fsdp_rank, share, 1) * grad_scale
    return (
        jnp.stack(outs)[:, None],
        jnp.stack(grad_tokens)[:, None],
        g_query,
        g_key,
        g_value,
        g_gate,
        g_out * grad_scale,
        g_up,
        down_sum.astype(jnp.float32) * grad_scale,
        norm_sums[:2],
        norm_sums[2:],
    )


def solution(mesh):
    in_specs = (
        P(None, "fsdp", "ctx", None),
        P(None, "fsdp", "ctx", None),
        P("fsdp", None),
        P("fsdp", None),
        P("fsdp", None),
        P("fsdp", None),
        P("fsdp", None),
        P("fsdp", None),
        P("fsdp", None),
        P(),
        P(),
        P(),
        P(None, "fsdp", None),
    )
    out_specs = (
        P(None, "fsdp", "ctx", None),
        P(None, "fsdp", "ctx", None),
        P(("ctx", "fsdp"), None),
        P(("ctx", "fsdp"), None),
        P(("ctx", "fsdp"), None),
        P(("ctx", "fsdp"), None),
        P(("ctx", "fsdp"), None),
        P(("ctx", "fsdp"), None),
        P(("ctx", "fsdp"), None),
        P(None, ("ctx", "fsdp")),
        P(None, ("ctx", "fsdp")),
    )
    by_heads = mesh.shape["ctx"] == HEADS and mesh.shape["fsdp"] == 4
    chosen = body_heads if by_heads else body
    return jax.shard_map(chosen, mesh=mesh, in_specs=in_specs, out_specs=out_specs, check_vma=False)
```

```python
import jax
import jax.numpy as jnp
from jax import lax
from jax.sharding import PartitionSpec as P

HEADS = 8
DK = 256
DV = 512
FF = 4096
MICRO = 2
QW = 2048
VW = 4096
BLOCK = 64


epsilon = 1e-05
group_floor = 1.0


def layer_norm(values, gain_row, offset):
    center = jnp.mean(values, axis=-1, keepdims=True)
    centred = values - center
    spread = jnp.mean(centred * centred, axis=-1, keepdims=True)
    return centred * lax.rsqrt(spread + epsilon) * gain_row + offset


def gated_mix(gate_pre, retained):
    number = retained.shape[0]
    grouped = retained.reshape(number, -1, DV)
    center = jnp.mean(grouped, axis=-1, keepdims=True)
    centred = grouped - center
    spread = jnp.mean(centred * centred, axis=-1, keepdims=True)
    normed = (centred * lax.rsqrt(spread + group_floor)).reshape(number, -1)
    return jax.nn.silu(gate_pre) * normed


def smooth_act(values):
    return jax.nn.gelu(values, approximate=False)


def stored_positions(block_deal, full_length, block_size):
    stored = jnp.arange(full_length, dtype=jnp.int32)
    block_ids = stored // block_size
    slots_all = jnp.arange(block_deal.shape[0], dtype=jnp.int32)
    picked = jnp.sum(
        jnp.where(block_ids[:, None] == slots_all[None, :], block_deal[None, :], 0),
        axis=1,
        dtype=jnp.int32,
    )
    return picked * block_size + stored % block_size


def document_ids(positions, doc_sizes):
    starts = jnp.cumsum(doc_sizes, dtype=jnp.int32) - doc_sizes
    return (
        jnp.sum((positions[:, None] >= starts[None, :]).astype(jnp.int32), axis=1, dtype=jnp.int32)
        - 1
    )


def decay_table(query_pos, query_doc, key_pos, key_doc, decay_log, scaling):
    keeping = (query_pos[:, None] >= key_pos[None, :]) & (query_doc[:, None] == key_doc[None, :])
    spacing = jnp.where(keeping, (query_pos[:, None] - key_pos[None, :]).astype(jnp.float32), 0.0)
    factor = jnp.exp(decay_log[:, None, None] * spacing[None])
    return jnp.where(keeping[None], factor * scaling, 0.0)


def contract_rows(left, right):
    return lax.dot_general(
        left, right, (((1,), (1,)), ((), ())), preferred_element_type=jnp.float32
    )


def contract_cols(left, right):
    return lax.dot_general(
        left, right, (((0,), (0,)), ((), ())), preferred_element_type=jnp.float32
    )


def add_single(left, weight_piece):
    return jnp.dot(left, weight_piece, preferred_element_type=jnp.float32)


def back_rows(left, weight_piece):
    return contract_rows(left, weight_piece)


def weight_term(kept_acts, number):
    normed_one, grads_in, normed_two, grads_up, mixed_all, grads_attn, active_all, grads_ffn = (
        kept_acts
    )
    pieces = [
        contract_cols(normed_one, grads_in),
        contract_cols(normed_two, grads_up),
        contract_cols(mixed_all, grads_attn).reshape(number, -1),
        contract_cols(active_all, grads_ffn).reshape(number, -1),
    ]
    return jnp.concatenate(pieces, axis=1)


def body(
    tokens,
    cotangent,
    w_query,
    w_key,
    w_value,
    w_gate,
    w_out,
    w_up,
    w_down,
    norm_gains,
    norm_biases,
    block_deal,
    doc_lengths,
):
    ctx_size = lax.axis_size("ctx")
    tok_rows = tokens.shape[2]
    full_length = tok_rows * ctx_size
    model_width = tokens.shape[3]
    share_rows = model_width // lax.axis_size(("ctx", "fsdp"))
    grad_scale = float(MICRO * lax.axis_size("fsdp") * full_length) ** (-0.5)
    own_start = lax.axis_index("ctx") * tok_rows
    key_pos = stored_positions(block_deal, full_length, BLOCK)
    query_pos = lax.dynamic_slice_in_dim(key_pos, own_start, tok_rows)
    decay_log = jnp.log1p(-jnp.exp2(-5.0 - jnp.arange(HEADS).astype(jnp.float32)))
    scaling = DK ** (-0.5)
    out_list = []
    grad_list = []
    weight_sum = None
    gain_sum = jnp.zeros((2, model_width), jnp.float32)
    bias_sum = jnp.zeros((2, model_width), jnp.float32)
    for batch_index in range(MICRO):
        rows_in = tokens[batch_index, 0].astype(jnp.float32)
        grad_rows = cotangent[batch_index, 0].astype(jnp.float32)
        key_doc = document_ids(key_pos, doc_lengths[batch_index, 0])
        query_doc = lax.dynamic_slice_in_dim(key_doc, own_start, tok_rows)
        table = decay_table(query_pos, query_doc, key_pos, key_doc, decay_log, scaling)
        normed_one, norm_pull_one = jax.vjp(layer_norm, rows_in, norm_gains[0], norm_biases[0])
        low_one = normed_one.astype(jnp.bfloat16)
        pieces = (
            lax.all_gather(w_query, "fsdp", axis=0, tiled=True),
            lax.all_gather(w_key, "fsdp", axis=0, tiled=True),
            lax.all_gather(w_value, "fsdp", axis=0, tiled=True),
            lax.all_gather(w_gate, "fsdp", axis=0, tiled=True),
        )
        query_f, key_f, value_f, gate_pre = tuple(
            (
                jnp.dot(low_one, weight_piece, preferred_element_type=jnp.float32)
                for weight_piece in pieces
            )
        )
        query_low = query_f.astype(jnp.bfloat16)
        key_low = key_f.astype(jnp.bfloat16)
        value_low = value_f.astype(jnp.bfloat16)
        keys_all, values_all = (
            lax.all_gather(key_low, "ctx", axis=0, tiled=True),
            lax.all_gather(value_low, "ctx", axis=0, tiled=True),
        )
        query_heads = query_low.reshape(tok_rows, HEADS, DK)
        key_heads = keys_all.reshape(full_length, HEADS, DK)
        value_heads = values_all.reshape(full_length, HEADS, DV)
        scores = jnp.einsum(
            "thd,shd->hts", query_heads, key_heads, preferred_element_type=jnp.float32
        )
        attend = (scores * table).astype(jnp.bfloat16)
        retained = jnp.einsum(
            "hts,shd->thd", attend, value_heads, preferred_element_type=jnp.float32
        ).reshape(tok_rows, VW)
        mixed, mix_pull = jax.vjp(gated_mix, gate_pre, retained)
        mixed_low = mixed.astype(jnp.bfloat16)
        attn_out = add_single(mixed_low, lax.all_gather(w_out, "fsdp", axis=0, tiled=True))
        hidden = rows_in + attn_out
        normed_two, norm_pull_two = jax.vjp(layer_norm, hidden, norm_gains[1], norm_biases[1])
        low_two = normed_two.astype(jnp.bfloat16)
        up_pre = add_single(low_two, lax.all_gather(w_up, "fsdp", axis=0, tiled=True))
        active, act_pull = jax.vjp(smooth_act, up_pre)
        active_low = active.astype(jnp.bfloat16)
        ffn_out = add_single(active_low, lax.all_gather(w_down, "fsdp", axis=0, tiled=True))
        out_list.append((hidden + ffn_out).astype(jnp.bfloat16))
        grad_ffn = grad_rows.astype(jnp.bfloat16)
        grad_act = back_rows(grad_ffn, lax.all_gather(w_down, "fsdp", axis=0, tiled=True))
        grad_up = act_pull(grad_act)[0].astype(jnp.bfloat16)
        grad_norm_two = back_rows(grad_up, lax.all_gather(w_up, "fsdp", axis=0, tiled=True))
        grad_hidden_ln, grad_gain_two, grad_bias_two = norm_pull_two(grad_norm_two)
        grad_hidden = grad_rows + grad_hidden_ln
        grad_attn = grad_hidden.astype(jnp.bfloat16)
        grad_mixed = back_rows(grad_attn, lax.all_gather(w_out, "fsdp", axis=0, tiled=True))
        grad_gate_f, grad_ret_f = mix_pull(grad_mixed)
        grad_gate = grad_gate_f.astype(jnp.bfloat16)
        ret_low = grad_ret_f.astype(jnp.bfloat16)
        ret_heads = ret_low.reshape(tok_rows, HEADS, DV)
        grad_attend = jnp.einsum(
            "thd,shd->hts", ret_heads, value_heads, preferred_element_type=jnp.float32
        )
        grad_scores = (grad_attend * table).astype(jnp.bfloat16)
        grad_query = (
            jnp.einsum("hts,shd->thd", grad_scores, key_heads, preferred_element_type=jnp.float32)
            .reshape(tok_rows, QW)
            .astype(jnp.bfloat16)
        )
        key_part = jnp.einsum(
            "hts,thd->shd", grad_scores, query_heads, preferred_element_type=jnp.float32
        ).reshape(tok_rows * lax.axis_size("ctx"), QW)
        value_part = jnp.einsum(
            "hts,thd->shd", attend, ret_heads, preferred_element_type=jnp.float32
        ).reshape(tok_rows * lax.axis_size("ctx"), VW)
        key_value_sum = lax.psum_scatter(
            jnp.concatenate([key_part, value_part], axis=1).astype(jnp.bfloat16),
            "ctx",
            scatter_dimension=0,
            tiled=True,
        ).astype(jnp.float32)
        grad_key = key_value_sum[:, :QW].astype(jnp.bfloat16)
        grad_value = key_value_sum[:, QW:].astype(jnp.bfloat16)
        term_now = (
            contract_rows(grad_query, lax.all_gather(w_query, "fsdp", axis=0, tiled=True))
            + contract_rows(grad_key, lax.all_gather(w_key, "fsdp", axis=0, tiled=True))
            + contract_rows(grad_value, lax.all_gather(w_value, "fsdp", axis=0, tiled=True))
            + contract_rows(grad_gate, lax.all_gather(w_gate, "fsdp", axis=0, tiled=True))
        )
        grad_rows_ln, grad_gain_one, grad_bias_one = norm_pull_one(term_now)
        grad_list.append(grad_hidden + grad_rows_ln)
        gain_sum = gain_sum + jnp.stack([grad_gain_one, grad_gain_two])
        bias_sum = bias_sum + jnp.stack([grad_bias_one, grad_bias_two])
        kept_now = (
            low_one,
            jnp.concatenate([grad_query, grad_key, grad_value, grad_gate], axis=1),
            low_two,
            grad_up,
            mixed_low,
            grad_attn,
            active_low,
            grad_ffn,
        )
        term_sum = lax.psum_scatter(
            weight_term(kept_now, share_rows * lax.axis_size(("ctx", "fsdp"))),
            ("ctx", "fsdp"),
            scatter_dimension=0,
            tiled=True,
        )
        weight_sum = term_sum if weight_sum is None else weight_sum + term_sum
    weight_sum = weight_sum * grad_scale
    bounds = [QW, 2 * QW, 2 * QW + VW, 2 * QW + 2 * VW, 2 * QW + 2 * VW + FF, 2 * QW + 3 * VW + FF]
    g_query, g_key, g_value, g_gate, g_up, g_out_flat, g_down_flat = jnp.split(
        weight_sum, bounds, axis=1
    )
    g_out = g_out_flat.reshape(share_rows * (VW // model_width), model_width)
    g_down = g_down_flat.reshape(share_rows * (FF // model_width), model_width)
    gain_grads, bias_grads = (
        lax.psum_scatter(gain_sum, ("ctx", "fsdp"), scatter_dimension=1, tiled=True),
        lax.psum_scatter(bias_sum, ("ctx", "fsdp"), scatter_dimension=1, tiled=True),
    )
    gain_grads = gain_grads * grad_scale
    bias_grads = bias_grads * grad_scale
    output = jnp.stack(out_list)[:, None]
    grad_tokens = jnp.stack(grad_list)[:, None]
    return (
        output,
        grad_tokens,
        g_query,
        g_key,
        g_value,
        g_gate,
        g_out,
        g_up,
        g_down,
        gain_grads,
        bias_grads,
    )


def xy_swap(x, bit):
    return lax.ppermute(x, "fsdp", [(i, i ^ bit) for i in range(lax.axis_size("fsdp"))])


def core_swap(x):
    return lax.ppermute(x, "ctx", [(i, i ^ 1) for i in range(lax.axis_size("ctx"))])


def after(x, *earlier):
    return lax.optimization_barrier((x,) + tuple(earlier))[0]


def gather_first(x):
    return xy_swap(x, 1), xy_swap(x, 2)


def gather_second(x, first, second):
    half = x.shape[0] // 2
    low_part = xy_swap(first[:half], 2)
    high_part = xy_swap(second[half:], 1)
    return [x, first, second, jnp.concatenate([low_part, high_part], axis=0)]


def plane_gather(x):
    return gather_second(x, *gather_first(x))


def plane_reduce(blocks):
    half = blocks[0].shape[-1] // 2
    left = [b[..., :half] for b in blocks]
    right = [b[..., half:] for b in blocks]
    left_in = xy_swap(jnp.stack([left[1], left[3]]), 1).astype(jnp.float32)
    right_in = xy_swap(jnp.stack([right[2], right[3]]), 2).astype(jnp.float32)
    left_far = left[2].astype(jnp.float32) + left_in[1]
    right_far = right[1].astype(jnp.float32) + right_in[1]
    left_last = xy_swap(left_far.astype(jnp.bfloat16), 2).astype(jnp.float32)
    right_last = xy_swap(right_far.astype(jnp.bfloat16), 1).astype(jnp.float32)
    left_own = left[0].astype(jnp.float32) + left_in[0]
    right_own = right[0].astype(jnp.float32) + right_in[0]
    return jnp.concatenate([left_own + left_last, right_own + right_last], axis=-1)


def sum_everywhere(x):
    for axis in ("ctx", "fsdp"):
        size = lax.axis_size(axis)
        bit = 1
        while bit < size:
            x = x + lax.ppermute(x, axis, [(i, i ^ bit) for i in range(size)])
            bit *= 2
    return x


def in_rank_order(blocks, rank):
    odd = (rank % 2) == 1
    upper = (rank // 2) == 1
    one = [
        jnp.where(odd, blocks[1], blocks[0]),
        jnp.where(odd, blocks[0], blocks[1]),
        jnp.where(odd, blocks[3], blocks[2]),
        jnp.where(odd, blocks[2], blocks[3]),
    ]
    return [
        jnp.where(upper, one[2], one[0]),
        jnp.where(upper, one[3], one[1]),
        jnp.where(upper, one[0], one[2]),
        jnp.where(upper, one[1], one[3]),
    ]


def pick(x, index, size, axis):
    return lax.dynamic_slice_in_dim(x, index * size, size, axis)


def head_columns(w_query, w_key, w_value, w_gate, ctx_rank):
    return jnp.concatenate(
        [
            pick(w_query, ctx_rank, DK, 1),
            pick(w_key, ctx_rank, DK, 1),
            pick(w_value, ctx_rank, DV, 1),
            pick(w_gate, ctx_rank, DV, 1),
        ],
        axis=1,
    )


def out_quarter_parts(w_out, ctx_rank, fsdp_rank, ctx_size, fsdp_size):
    held = pick(w_out, ctx_rank % 2, DV, 0)
    rows = DV // fsdp_size
    parts = [pick(held, fsdp_rank, rows, 0)]
    for bit in range(1, fsdp_size):
        pairs = [
            (c * fsdp_size + c // 2, c * fsdp_size + ((c // 2) ^ bit)) for c in range(ctx_size)
        ]
        parts.append(lax.ppermute(pick(held, fsdp_rank ^ bit, rows, 0), ("ctx", "fsdp"), pairs))
    return parts


def choose_quarter(parts, ctx_rank, fsdp_rank):
    quarter = parts[0]
    for bit in range(1, len(parts)):
        quarter = jnp.where((fsdp_rank ^ (ctx_rank // 2)) == bit, parts[bit], quarter)
    return quarter


def exchange(pieces_of):
    core = lax.axis_index("ctx") % 2
    return [xy_swap(pieces_of(bit, core), bit) for bit in (1, 2, 3)]


def exchanged(pieces_of, mine, axis, fsdp_rank):
    even = (lax.axis_index("ctx") % 2) == 0
    other = core_swap(jnp.stack(mine))
    blocks = [jnp.concatenate([pieces_of(0, 0), pieces_of(0, 1)], axis=axis)]
    for number in range(3):
        one, two = mine[number], other[number]
        pair = [jnp.where(even, one, two), jnp.where(even, two, one)]
        blocks.append(jnp.concatenate(pair, axis=axis))
    return jnp.concatenate(in_rank_order(blocks, fsdp_rank), axis=0)


def up_pieces(w_up, fsdp_rank, ctx_size, fsdp_size):
    rows = w_up.shape[0]
    unit = FF // (ctx_size * fsdp_size)
    half = ctx_size // 2
    view = w_up.reshape(rows, ctx_size, fsdp_size * unit)

    def piece(bit, part):
        place = (0, part * half, (fsdp_rank ^ bit) * unit)
        return lax.dynamic_slice(view, place, (rows, half, unit)).reshape(rows, half * unit)

    return piece


def down_pieces(w_down, fsdp_rank, ctx_size, fsdp_size):
    unit = FF // (ctx_size * fsdp_size)
    width = w_down.shape[1]
    view = w_down.reshape(2, fsdp_size * unit, width)

    def piece(bit, part):
        return lax.dynamic_slice(view, (part, (fsdp_rank ^ bit) * unit, 0), (1, unit, width))[0]

    return piece


def smooth_parts(values):
    share = 0.5 + 0.5 * lax.erf(values * (0.5**0.5))
    density = jnp.exp(-0.5 * values * values) * ((0.5 / jnp.pi) ** 0.5)
    return values * share, share + values * density


def one_table(pos, doc, rate, scaling):
    keeping = (pos[:, None] >= pos[None, :]) & (doc[:, None] == doc[None, :])
    spacing = jnp.where(keeping, (pos[:, None] - pos[None, :]).astype(jnp.float32), 0.0)
    return jnp.where(keeping, jnp.exp(rate * spacing) * scaling, 0.0)


def ctx_sum(x):
    return lax.psum_scatter(x, "ctx", scatter_dimension=0, tiled=True)


def body_heads(
    tokens,
    cotangent,
    w_query,
    w_key,
    w_value,
    w_gate,
    w_out,
    w_up,
    w_down,
    norm_gains,
    norm_biases,
    block_deal,
    doc_lengths,
):
    low = jnp.bfloat16
    ctx_size = lax.axis_size("ctx")
    fsdp_size = lax.axis_size("fsdp")
    tok_rows = tokens.shape[2]
    full_length = tok_rows * ctx_size
    width = tokens.shape[3]
    share = width // (ctx_size * fsdp_size)
    grad_scale = float(MICRO * fsdp_size * full_length) ** (-0.5)
    ctx_rank = lax.axis_index("ctx")
    fsdp_rank = lax.axis_index("fsdp")
    pos = stored_positions(block_deal, full_length, BLOCK)
    rate = jnp.log1p(-jnp.exp2(-5.0 - ctx_rank.astype(jnp.float32)))
    scaling = DK ** (-0.5)

    own_in = head_columns(w_query, w_key, w_value, w_gate, ctx_rank)
    tokens = after(tokens, own_in)
    rows_in = []
    norm_one = []
    x_own = []
    for m in range(MICRO):
        rows_in.append(after(tokens[m, 0], *x_own[-1:]).astype(jnp.float32))
        norm_one.append(jax.vjp(layer_norm, rows_in[m], norm_gains[0], norm_biases[0]))
        x_own.append(norm_one[m][0].astype(low))
    grad_rows = [cotangent[m, 0].astype(jnp.float32) for m in range(MICRO)]
    x_all = [lax.all_gather(x, "ctx", axis=0, tiled=True) for x in x_own]
    in_first = gather_first(own_in)
    in_blocks = gather_second(own_in, *in_first)
    w_in = jnp.concatenate(in_rank_order(in_blocks, fsdp_rank), axis=0)
    out_parts = out_quarter_parts(
        after(w_out, in_blocks[3]), ctx_rank, fsdp_rank, ctx_size, fsdp_size
    )

    def mix(m, x_now):
        doc = document_ids(pos, doc_lengths[m, 0])
        table = one_table(pos, doc, rate, scaling)
        joint = jnp.dot(x_now, w_in[:, : 2 * DK + DV], preferred_element_type=jnp.float32).astype(low)
        gate_pre = jnp.dot(x_now, w_in[:, 2 * DK + DV :], preferred_element_type=jnp.float32)
        query, key, value = joint[:, :DK], joint[:, DK : 2 * DK], joint[:, 2 * DK :]
        attend = (contract_rows(query, key) * table).astype(low)
        retained = add_single(attend, value)
        mixed, mix_pull = jax.vjp(gated_mix, gate_pre, retained)
        return table, query, key, value, attend, mix_pull, mixed.astype(low)

    kept = [mix(0, x_all[0])]
    out_parts = lax.optimization_barrier(tuple(out_parts) + (kept[0][6],))[:-1]
    quarter = choose_quarter(out_parts, ctx_rank, fsdp_rank)
    out_first = gather_first(quarter)
    out_blocks = gather_second(quarter, *out_first)
    w_head = jnp.concatenate(in_rank_order(out_blocks, fsdp_rank), axis=0)
    cot_in = [after(cotangent[m, 0], *out_first) for m in range(MICRO)]
    cot_first = [gather_first(cot_in[m]) for m in range(MICRO)]
    part = add_single(kept[0][6], w_head).astype(low)
    attn_out = [ctx_sum(after(part, *x_all[1:]))]
    for m in range(1, MICRO):
        firsts = [c for pair in cot_first for c in pair]
        kept.append(mix(m, after(x_all[m], part, *firsts)))
        part = add_single(kept[m][6], w_head).astype(low)
        attn_out.append(ctx_sum(part))
    cot_all = [
        jnp.concatenate(gather_second(cot_in[m], *cot_first[m]), axis=0) for m in range(MICRO)
    ]
    firsts = [c for pair in cot_first for c in pair]
    up_piece = up_pieces(after(w_up, *firsts), fsdp_rank, ctx_size, fsdp_size)
    up_mine = exchange(up_piece)
    down_piece = down_pieces(after(w_down, *firsts), fsdp_rank, ctx_size, fsdp_size)
    down_mine = exchange(down_piece)
    attn_out[0] = after(attn_out[0], part, *up_mine)
    up_own = exchanged(up_piece, up_mine, 1, fsdp_rank)
    down_own = exchanged(down_piece, down_mine, 0, fsdp_rank)

    outs = [None] * MICRO
    grad_attn = []
    grad_hidden = []
    ffn_kept = []
    norm_two_terms = []
    norm_part = None
    for m in range(MICRO):
        if m > 0:
            attn_out[m] = after(attn_out[m], norm_part)
        hidden = rows_in[m] + attn_out[m].astype(jnp.float32)
        normed_two, pull_two = jax.vjp(layer_norm, hidden, norm_gains[1], norm_biases[1])
        two_all = jnp.concatenate(plane_gather(normed_two.astype(low)), axis=0)
        active, slope = smooth_parts(add_single(two_all, up_own))
        active_low, slope = lax.optimization_barrier((active.astype(low), slope))
        grad_up = (back_rows(cot_all[m], down_own) * slope).astype(low)
        norm_part = back_rows(grad_up, up_own).astype(low)
        cut = [norm_part[j * tok_rows : (j + 1) * tok_rows] for j in range(fsdp_size)]
        grad_norm_two = after(plane_reduce(cut), *grad_attn[-1:])
        grad_ln, gain_two, bias_two = pull_two(grad_norm_two)
        norm_two_terms.append((gain_two, bias_two))
        total = grad_rows[m] + grad_ln
        grad_hidden.append(total)
        grad_attn.append(total.astype(low))
        ffn_kept.append((two_all, grad_up, active_low, hidden))

    grad_all = [lax.all_gather(grad_attn[m], "ctx", axis=0, tiled=True) for m in range(MICRO)]

    def unmix(m, grad_now):
        table, query, key, value, attend, mix_pull, mixed_low = kept[m]
        grad_mixed = back_rows(grad_now, w_head)
        grad_gate, grad_ret = mix_pull(grad_mixed)
        ret_low = grad_ret.astype(low)
        grad_scores = (contract_rows(ret_low, value) * table).astype(low)
        grad_query = add_single(grad_scores, key).astype(low)
        grad_key = contract_cols(grad_scores, query).astype(low)
        grad_value = contract_cols(attend, ret_low).astype(low)
        return jnp.concatenate([grad_query, grad_key, grad_value, grad_gate.astype(low)], axis=1)

    terms = []
    in_term = None
    out_term = None
    sums = []
    for m in range(MICRO):
        grad_now = after(grad_all[m], *(grad_attn[1:] if m == 0 else terms[-1:]))
        grad_in = unmix(m, grad_now)
        part = back_rows(grad_in, w_in).astype(low)
        terms.append(part)
        sums.append(ctx_sum(after(part, *grad_all[m + 1 :], *sums[-1:])))
        x_now, mixed_now, grad_in = lax.optimization_barrier(
            (x_all[m], kept[m][6], grad_in, part)
        )[:3]
        in_now = contract_cols(x_now, grad_in)
        out_now = contract_cols(mixed_now, grad_all[m])
        in_term = in_now if m == 0 else in_term + in_now
        out_term = out_now if m == 0 else out_term + out_now
        if m == 0:
            ready = [after(ffn_kept[n][2], part, grad_attn[n]) for n in range(MICRO)]
            for n in range(MICRO):
                ffn_part = add_single(ready[n], down_own).astype(low)
                cut = [ffn_part[j * tok_rows : (j + 1) * tok_rows] for j in range(fsdp_size)]
                outs[n] = (ffn_kept[n][3] + plane_reduce(cut)).astype(low)
            up_grad = sum(contract_cols(k[0], after(k[1], part)) for k in ffn_kept).astype(low)
            down_grad = sum(contract_cols(ready[n], cot_all[n]) for n in range(MICRO)).astype(low)
    in_term = in_term.astype(low)
    out_term = out_term.astype(low)
    up_sum = ctx_sum(after(up_grad, sums[-1]))
    down_sum = ctx_sum(after(down_grad, up_sum))

    grad_tokens = []
    norm_one_terms = []
    for m in range(MICRO):
        grad_ln, gain_one, bias_one = norm_one[m][1](sums[m].astype(jnp.float32))
        norm_one_terms.append((gain_one, bias_one))
        grad_tokens.append(grad_hidden[m] + grad_ln)

    in_view = in_term.reshape(ctx_size, fsdp_size, share, -1)
    in_sum = plane_reduce([pick(in_view, fsdp_rank ^ j, 1, 1)[:, 0] for j in range(fsdp_size)])
    in_mine = lax.all_to_all(in_sum.astype(low), "ctx", split_axis=0, concat_axis=0, tiled=True)
    rows = DV // fsdp_size
    g_out = plane_reduce([pick(out_term, fsdp_rank ^ j, rows, 0) for j in range(fsdp_size)])

    def by_head(first, size):
        part = in_mine[:, :, first : first + size].transpose(1, 0, 2)
        return part.reshape(share, -1).astype(jnp.float32) * grad_scale

    g_query = by_head(0, DK)
    g_key = by_head(DK, DK)
    g_value = by_head(2 * DK, DV)
    g_gate = by_head(2 * DK + DV, DV)

    up_view = up_sum.reshape(fsdp_size, share, -1)
    pieces = [lax.dynamic_index_in_dim(up_view, fsdp_rank, 0, keepdims=False)]
    for bit in range(1, fsdp_size):
        pieces.append(
            xy_swap(lax.dynamic_index_in_dim(up_view, fsdp_rank ^ bit, 0, keepdims=False), bit)
        )
    pieces = [p.reshape(share, ctx_size, -1) for p in in_rank_order(pieces, fsdp_rank)]
    g_up = jnp.stack(pieces, axis=2).reshape(share, FF).astype(jnp.float32) * grad_scale

    gain_rows = [sum(t[0] for t in norm_one_terms), sum(t[0] for t in norm_two_terms)]
    bias_rows = [sum(t[1] for t in norm_one_terms), sum(t[1] for t in norm_two_terms)]
    norm_sums = sum_everywhere(jnp.stack(gain_rows + bias_rows))
    norm_sums = pick(norm_sums, ctx_rank * fsdp_size + fsdp_rank, share, 1) * grad_scale
    return (
        jnp.stack(outs)[:, None],
        jnp.stack(grad_tokens)[:, None],
        g_query,
        g_key,
        g_value,
        g_gate,
        g_out * grad_scale,
        g_up,
        down_sum.astype(jnp.float32) * grad_scale,
        norm_sums[:2],
        norm_sums[2:],
    )


def solution(mesh):
    in_specs = (
        P(None, "fsdp", "ctx", None),
        P(None, "fsdp", "ctx", None),
        P("fsdp", None),
        P("fsdp", None),
        P("fsdp", None),
        P("fsdp", None),
        P("fsdp", None),
        P("fsdp", None),
        P("fsdp", None),
        P(),
        P(),
        P(),
        P(None, "fsdp", None),
    )
    out_specs = (
        P(None, "fsdp", "ctx", None),
        P(None, "fsdp", "ctx", None),
        P(("ctx", "fsdp"), None),
        P(("ctx", "fsdp"), None),
        P(("ctx", "fsdp"), None),
        P(("ctx", "fsdp"), None),
        P(("ctx", "fsdp"), None),
        P(("ctx", "fsdp"), None),
        P(("ctx", "fsdp"), None),
        P(None, ("ctx", "fsdp")),
        P(None, ("ctx", "fsdp")),
    )
    by_heads = mesh.shape["ctx"] == HEADS and mesh.shape["fsdp"] == 4
    chosen = body_heads if by_heads else body
    return jax.shard_map(chosen, mesh=mesh, in_specs=in_specs, out_specs=out_specs, check_vma=False)
```

```python
import jax
import jax.numpy as jnp
from jax import lax
from jax.experimental import pallas as pl
from jax.experimental.pallas import tpu as pltpu
from jax.sharding import PartitionSpec as P

HEADS = 8
DK = 256
DV = 512
FF = 4096
MICRO = 2
QW = 2048
VW = 4096
BLOCK = 64


epsilon = 1e-05
group_floor = 1.0


def layer_norm(values, gain_row, offset):
    center = jnp.mean(values, axis=-1, keepdims=True)
    centred = values - center
    spread = jnp.mean(centred * centred, axis=-1, keepdims=True)
    return centred * lax.rsqrt(spread + epsilon) * gain_row + offset


def gated_mix(gate_pre, retained):
    number = retained.shape[0]
    grouped = retained.reshape(number, -1, DV)
    center = jnp.mean(grouped, axis=-1, keepdims=True)
    centred = grouped - center
    spread = jnp.mean(centred * centred, axis=-1, keepdims=True)
    normed = (centred * lax.rsqrt(spread + group_floor)).reshape(number, -1)
    return jax.nn.silu(gate_pre) * normed


def smooth_act(values):
    return jax.nn.gelu(values, approximate=False)


def stored_positions(block_deal, full_length, block_size):
    stored = jnp.arange(full_length, dtype=jnp.int32)
    block_ids = stored // block_size
    slots_all = jnp.arange(block_deal.shape[0], dtype=jnp.int32)
    picked = jnp.sum(
        jnp.where(block_ids[:, None] == slots_all[None, :], block_deal[None, :], 0),
        axis=1,
        dtype=jnp.int32,
    )
    return picked * block_size + stored % block_size


def document_ids(positions, doc_sizes):
    starts = jnp.cumsum(doc_sizes, dtype=jnp.int32) - doc_sizes
    return (
        jnp.sum((positions[:, None] >= starts[None, :]).astype(jnp.int32), axis=1, dtype=jnp.int32)
        - 1
    )


def decay_table(query_pos, query_doc, key_pos, key_doc, decay_log, scaling):
    keeping = (query_pos[:, None] >= key_pos[None, :]) & (query_doc[:, None] == key_doc[None, :])
    spacing = jnp.where(keeping, (query_pos[:, None] - key_pos[None, :]).astype(jnp.float32), 0.0)
    factor = jnp.exp(decay_log[:, None, None] * spacing[None])
    return jnp.where(keeping[None], factor * scaling, 0.0)


def contract_rows(left, right):
    return lax.dot_general(
        left, right, (((1,), (1,)), ((), ())), preferred_element_type=jnp.float32
    )


def contract_cols(left, right):
    return lax.dot_general(
        left, right, (((0,), (0,)), ((), ())), preferred_element_type=jnp.float32
    )


def add_single(left, weight_piece):
    return jnp.dot(left, weight_piece, preferred_element_type=jnp.float32)


def back_rows(left, weight_piece):
    return contract_rows(left, weight_piece)


def weight_term(kept_acts, number):
    normed_one, grads_in, normed_two, grads_up, mixed_all, grads_attn, active_all, grads_ffn = (
        kept_acts
    )
    pieces = [
        contract_cols(normed_one, grads_in),
        contract_cols(normed_two, grads_up),
        contract_cols(mixed_all, grads_attn).reshape(number, -1),
        contract_cols(active_all, grads_ffn).reshape(number, -1),
    ]
    return jnp.concatenate(pieces, axis=1)


def body(
    tokens,
    cotangent,
    w_query,
    w_key,
    w_value,
    w_gate,
    w_out,
    w_up,
    w_down,
    norm_gains,
    norm_biases,
    block_deal,
    doc_lengths,
):
    ctx_size = lax.axis_size("ctx")
    tok_rows = tokens.shape[2]
    full_length = tok_rows * ctx_size
    model_width = tokens.shape[3]
    share_rows = model_width // lax.axis_size(("ctx", "fsdp"))
    grad_scale = float(MICRO * lax.axis_size("fsdp") * full_length) ** (-0.5)
    own_start = lax.axis_index("ctx") * tok_rows
    key_pos = stored_positions(block_deal, full_length, BLOCK)
    query_pos = lax.dynamic_slice_in_dim(key_pos, own_start, tok_rows)
    decay_log = jnp.log1p(-jnp.exp2(-5.0 - jnp.arange(HEADS).astype(jnp.float32)))
    scaling = DK ** (-0.5)
    out_list = []
    grad_list = []
    weight_sum = None
    gain_sum = jnp.zeros((2, model_width), jnp.float32)
    bias_sum = jnp.zeros((2, model_width), jnp.float32)
    for batch_index in range(MICRO):
        rows_in = tokens[batch_index, 0].astype(jnp.float32)
        grad_rows = cotangent[batch_index, 0].astype(jnp.float32)
        key_doc = document_ids(key_pos, doc_lengths[batch_index, 0])
        query_doc = lax.dynamic_slice_in_dim(key_doc, own_start, tok_rows)
        table = decay_table(query_pos, query_doc, key_pos, key_doc, decay_log, scaling)
        normed_one, norm_pull_one = jax.vjp(layer_norm, rows_in, norm_gains[0], norm_biases[0])
        low_one = normed_one.astype(jnp.bfloat16)
        pieces = (
            lax.all_gather(w_query, "fsdp", axis=0, tiled=True),
            lax.all_gather(w_key, "fsdp", axis=0, tiled=True),
            lax.all_gather(w_value, "fsdp", axis=0, tiled=True),
            lax.all_gather(w_gate, "fsdp", axis=0, tiled=True),
        )
        query_f, key_f, value_f, gate_pre = tuple(
            (
                jnp.dot(low_one, weight_piece, preferred_element_type=jnp.float32)
                for weight_piece in pieces
            )
        )
        query_low = query_f.astype(jnp.bfloat16)
        key_low = key_f.astype(jnp.bfloat16)
        value_low = value_f.astype(jnp.bfloat16)
        keys_all, values_all = (
            lax.all_gather(key_low, "ctx", axis=0, tiled=True),
            lax.all_gather(value_low, "ctx", axis=0, tiled=True),
        )
        query_heads = query_low.reshape(tok_rows, HEADS, DK)
        key_heads = keys_all.reshape(full_length, HEADS, DK)
        value_heads = values_all.reshape(full_length, HEADS, DV)
        scores = jnp.einsum(
            "thd,shd->hts", query_heads, key_heads, preferred_element_type=jnp.float32
        )
        attend = (scores * table).astype(jnp.bfloat16)
        retained = jnp.einsum(
            "hts,shd->thd", attend, value_heads, preferred_element_type=jnp.float32
        ).reshape(tok_rows, VW)
        mixed, mix_pull = jax.vjp(gated_mix, gate_pre, retained)
        mixed_low = mixed.astype(jnp.bfloat16)
        attn_out = add_single(mixed_low, lax.all_gather(w_out, "fsdp", axis=0, tiled=True))
        hidden = rows_in + attn_out
        normed_two, norm_pull_two = jax.vjp(layer_norm, hidden, norm_gains[1], norm_biases[1])
        low_two = normed_two.astype(jnp.bfloat16)
        up_pre = add_single(low_two, lax.all_gather(w_up, "fsdp", axis=0, tiled=True))
        active, act_pull = jax.vjp(smooth_act, up_pre)
        active_low = active.astype(jnp.bfloat16)
        ffn_out = add_single(active_low, lax.all_gather(w_down, "fsdp", axis=0, tiled=True))
        out_list.append((hidden + ffn_out).astype(jnp.bfloat16))
        grad_ffn = grad_rows.astype(jnp.bfloat16)
        grad_act = back_rows(grad_ffn, lax.all_gather(w_down, "fsdp", axis=0, tiled=True))
        grad_up = act_pull(grad_act)[0].astype(jnp.bfloat16)
        grad_norm_two = back_rows(grad_up, lax.all_gather(w_up, "fsdp", axis=0, tiled=True))
        grad_hidden_ln, grad_gain_two, grad_bias_two = norm_pull_two(grad_norm_two)
        grad_hidden = grad_rows + grad_hidden_ln
        grad_attn = grad_hidden.astype(jnp.bfloat16)
        grad_mixed = back_rows(grad_attn, lax.all_gather(w_out, "fsdp", axis=0, tiled=True))
        grad_gate_f, grad_ret_f = mix_pull(grad_mixed)
        grad_gate = grad_gate_f.astype(jnp.bfloat16)
        ret_low = grad_ret_f.astype(jnp.bfloat16)
        ret_heads = ret_low.reshape(tok_rows, HEADS, DV)
        grad_attend = jnp.einsum(
            "thd,shd->hts", ret_heads, value_heads, preferred_element_type=jnp.float32
        )
        grad_scores = (grad_attend * table).astype(jnp.bfloat16)
        grad_query = (
            jnp.einsum("hts,shd->thd", grad_scores, key_heads, preferred_element_type=jnp.float32)
            .reshape(tok_rows, QW)
            .astype(jnp.bfloat16)
        )
        key_part = jnp.einsum(
            "hts,thd->shd", grad_scores, query_heads, preferred_element_type=jnp.float32
        ).reshape(tok_rows * lax.axis_size("ctx"), QW)
        value_part = jnp.einsum(
            "hts,thd->shd", attend, ret_heads, preferred_element_type=jnp.float32
        ).reshape(tok_rows * lax.axis_size("ctx"), VW)
        key_value_sum = lax.psum_scatter(
            jnp.concatenate([key_part, value_part], axis=1).astype(jnp.bfloat16),
            "ctx",
            scatter_dimension=0,
            tiled=True,
        ).astype(jnp.float32)
        grad_key = key_value_sum[:, :QW].astype(jnp.bfloat16)
        grad_value = key_value_sum[:, QW:].astype(jnp.bfloat16)
        term_now = (
            contract_rows(grad_query, lax.all_gather(w_query, "fsdp", axis=0, tiled=True))
            + contract_rows(grad_key, lax.all_gather(w_key, "fsdp", axis=0, tiled=True))
            + contract_rows(grad_value, lax.all_gather(w_value, "fsdp", axis=0, tiled=True))
            + contract_rows(grad_gate, lax.all_gather(w_gate, "fsdp", axis=0, tiled=True))
        )
        grad_rows_ln, grad_gain_one, grad_bias_one = norm_pull_one(term_now)
        grad_list.append(grad_hidden + grad_rows_ln)
        gain_sum = gain_sum + jnp.stack([grad_gain_one, grad_gain_two])
        bias_sum = bias_sum + jnp.stack([grad_bias_one, grad_bias_two])
        kept_now = (
            low_one,
            jnp.concatenate([grad_query, grad_key, grad_value, grad_gate], axis=1),
            low_two,
            grad_up,
            mixed_low,
            grad_attn,
            active_low,
            grad_ffn,
        )
        term_sum = lax.psum_scatter(
            weight_term(kept_now, share_rows * lax.axis_size(("ctx", "fsdp"))),
            ("ctx", "fsdp"),
            scatter_dimension=0,
            tiled=True,
        )
        weight_sum = term_sum if weight_sum is None else weight_sum + term_sum
    weight_sum = weight_sum * grad_scale
    bounds = [QW, 2 * QW, 2 * QW + VW, 2 * QW + 2 * VW, 2 * QW + 2 * VW + FF, 2 * QW + 3 * VW + FF]
    g_query, g_key, g_value, g_gate, g_up, g_out_flat, g_down_flat = jnp.split(
        weight_sum, bounds, axis=1
    )
    g_out = g_out_flat.reshape(share_rows * (VW // model_width), model_width)
    g_down = g_down_flat.reshape(share_rows * (FF // model_width), model_width)
    gain_grads, bias_grads = (
        lax.psum_scatter(gain_sum, ("ctx", "fsdp"), scatter_dimension=1, tiled=True),
        lax.psum_scatter(bias_sum, ("ctx", "fsdp"), scatter_dimension=1, tiled=True),
    )
    gain_grads = gain_grads * grad_scale
    bias_grads = bias_grads * grad_scale
    output = jnp.stack(out_list)[:, None]
    grad_tokens = jnp.stack(grad_list)[:, None]
    return (
        output,
        grad_tokens,
        g_query,
        g_key,
        g_value,
        g_gate,
        g_out,
        g_up,
        g_down,
        gain_grads,
        bias_grads,
    )


def xy_swap(x, bit):
    return lax.ppermute(x, "fsdp", [(i, i ^ bit) for i in range(lax.axis_size("fsdp"))])


def core_swap(x):
    return lax.ppermute(x, "ctx", [(i, i ^ 1) for i in range(lax.axis_size("ctx"))])


def after(x, *earlier):
    return lax.optimization_barrier((x,) + tuple(earlier))[0]


def place(shape, items):
    arrays = []
    for item in items:
        if not any(item[0] is a for a in arrays):
            arrays.append(item[0])
    slots = [[item[0] is a for a in arrays].index(True) for item in items]
    kind = arrays[0].dtype

    def kernel(*refs):
        out, sems = refs[len(arrays)], refs[len(arrays) + 1]
        rank = lax.axis_index("fsdp")
        core = lax.axis_index("ctx") % 2
        copies = []
        for number, (array, start, rows, row, column) in enumerate(items):
            width = array.shape[1]
            row = pl.multiple_of(row(rank, core), rows) if callable(row) else row
            column = pl.multiple_of(column(rank, core), width) if callable(column) else column
            copies.append(
                pltpu.make_async_copy(
                    refs[slots[number]].at[pl.ds(start, rows), :],
                    out.at[pl.ds(row, rows), pl.ds(column, width)],
                    sems.at[number],
                )
            )
        for copy in copies:
            copy.start()
        for copy in copies:
            copy.wait()

    size = shape[0] * shape[1] * jnp.dtype(kind).itemsize
    return pl.pallas_call(
        kernel,
        out_shape=jax.ShapeDtypeStruct(shape, kind),
        in_specs=[pl.BlockSpec(memory_space=pl.ANY)] * len(arrays),
        out_specs=pl.BlockSpec(memory_space=pl.ANY),
        scratch_shapes=[pltpu.SemaphoreType.DMA((len(items),))],
        cost_estimate=pl.CostEstimate(flops=0, bytes_accessed=2 * size, transcendentals=0),
    )(*arrays)


def gather_first(x):
    return xy_swap(x, 1), xy_swap(x, 2)


def gather_second(first, second):
    half = first.shape[0] // 2
    return xy_swap(first[:half], 2), xy_swap(second[half:], 1)


def by_offset(x, first, second, low_part, high_part):
    rows, half = x.shape[0], x.shape[0] // 2
    return place(
        (4 * rows, x.shape[1]),
        [
            (x, 0, rows, 0, 0),
            (first, 0, rows, rows, 0),
            (low_part, 0, half, 2 * rows, 0),
            (high_part, 0, half, 2 * rows + half, 0),
            (second, 0, rows, 3 * rows, 0),
        ],
    )


def by_rank(x, first, second, low_part, high_part):
    rows, half = x.shape[0], x.shape[0] // 2
    return place(
        (4 * rows, x.shape[1]),
        [
            (x, 0, rows, lambda f, c: f * rows, 0),
            (first, 0, rows, lambda f, c: (f ^ 1) * rows, 0),
            (low_part, 0, half, lambda f, c: (f ^ 3) * rows, 0),
            (high_part, 0, half, lambda f, c: (f ^ 3) * rows + half, 0),
            (second, 0, rows, lambda f, c: (f ^ 2) * rows, 0),
        ],
    )


def plane_reduce_rows(part):
    rows, half = part.shape[0] // 4, part.shape[1] // 2
    wide = lambda v: v.astype(jnp.float32)
    left_in = xy_swap(part[rows : 3 * rows, :half], 1)
    right_in = xy_swap(part[2 * rows :, half:], 2)
    left_far = wide(part[3 * rows :, :half]) + wide(left_in[rows:])
    right_far = wide(part[rows : 2 * rows, half:]) + wide(right_in[:rows])
    left_last = xy_swap(left_far.astype(jnp.bfloat16), 2)
    right_last = xy_swap(right_far.astype(jnp.bfloat16), 1)
    left = wide(part[:rows, :half]) + wide(left_in[:rows]) + wide(left_last)
    right = wide(part[:rows, half:]) + wide(right_in[rows:]) + wide(right_last)
    return jnp.concatenate([left, right], axis=1)


def plane_reduce(blocks):
    half = blocks[0].shape[-1] // 2
    left = [b[..., :half] for b in blocks]
    right = [b[..., half:] for b in blocks]
    left_in = xy_swap(jnp.stack([left[1], left[3]]), 1).astype(jnp.float32)
    right_in = xy_swap(jnp.stack([right[2], right[3]]), 2).astype(jnp.float32)
    left_far = left[2].astype(jnp.float32) + left_in[1]
    right_far = right[1].astype(jnp.float32) + right_in[1]
    left_last = xy_swap(left_far.astype(jnp.bfloat16), 2).astype(jnp.float32)
    right_last = xy_swap(right_far.astype(jnp.bfloat16), 1).astype(jnp.float32)
    left_own = left[0].astype(jnp.float32) + left_in[0]
    right_own = right[0].astype(jnp.float32) + right_in[0]
    return jnp.concatenate([left_own + left_last, right_own + right_last], axis=-1)


def sum_everywhere(x):
    for axis in ("ctx", "fsdp"):
        size = lax.axis_size(axis)
        bit = 1
        while bit < size:
            x = x + lax.ppermute(x, axis, [(i, i ^ bit) for i in range(size)])
            bit *= 2
    return x


def in_rank_order(blocks, rank):
    odd = (rank % 2) == 1
    upper = (rank // 2) == 1
    one = [
        jnp.where(odd, blocks[1], blocks[0]),
        jnp.where(odd, blocks[0], blocks[1]),
        jnp.where(odd, blocks[3], blocks[2]),
        jnp.where(odd, blocks[2], blocks[3]),
    ]
    return [
        jnp.where(upper, one[2], one[0]),
        jnp.where(upper, one[3], one[1]),
        jnp.where(upper, one[0], one[2]),
        jnp.where(upper, one[1], one[3]),
    ]


def pick(x, index, size, axis):
    return lax.dynamic_slice_in_dim(x, index * size, size, axis)


def head_columns(w_query, w_key, w_value, w_gate, ctx_rank):
    return jnp.concatenate(
        [
            pick(w_query, ctx_rank, DK, 1),
            pick(w_key, ctx_rank, DK, 1),
            pick(w_value, ctx_rank, DV, 1),
            pick(w_gate, ctx_rank, DV, 1),
        ],
        axis=1,
    )


def out_pieces(w_out, ctx_rank, fsdp_rank, fsdp_size):
    rows = DV // fsdp_size
    start = (ctx_rank % 2) * DV
    return [
        lax.dynamic_slice_in_dim(w_out, start + (fsdp_rank ^ bit) * rows, rows, 0)
        for bit in range(fsdp_size)
    ]


def scatter_quarters(cuts, ctx_size, fsdp_size):
    parts = [cuts[0]]
    for bit in range(1, fsdp_size):
        pairs = [
            (c * fsdp_size + c // 2, c * fsdp_size + ((c // 2) ^ bit)) for c in range(ctx_size)
        ]
        parts.append(lax.ppermute(cuts[bit], ("ctx", "fsdp"), pairs))
    return parts


def choose_quarter(parts, ctx_rank, fsdp_rank):
    quarter = parts[0]
    for bit in range(1, len(parts)):
        quarter = jnp.where((fsdp_rank ^ (ctx_rank // 2)) == bit, parts[bit], quarter)
    return quarter


def up_pieces(w_up, fsdp_rank, ctx_size, fsdp_size):
    unit = FF // (ctx_size * fsdp_size)
    half = ctx_size // 2
    core = lax.axis_index("ctx") % 2

    def cut(bit, part):
        starts = [(part * half + i) * fsdp_size * unit for i in range(half)]
        place_in = (fsdp_rank ^ bit) * unit
        return jnp.concatenate(
            [lax.dynamic_slice_in_dim(w_up, s + place_in, unit, 1) for s in starts], axis=1
        )

    own = jnp.concatenate([cut(0, 0), cut(0, 1)], axis=1)
    return own, [cut(bit, core) for bit in range(1, fsdp_size)]


def down_pieces(w_down, fsdp_rank, ctx_size, fsdp_size):
    unit = FF // (ctx_size * fsdp_size)
    core = lax.axis_index("ctx") % 2

    def cut(bit, part):
        start = (part * fsdp_size + (fsdp_rank ^ bit)) * unit
        return lax.dynamic_slice_in_dim(w_down, start, unit, 0)

    own = jnp.concatenate([cut(0, 0), cut(0, 1)], axis=0)
    return own, [cut(bit, core) for bit in range(1, fsdp_size)]


def exchange(pieces):
    return [xy_swap(pieces[bit - 1], bit) for bit in (1, 2, 3)]


def both_cores(mine):
    rows = mine[0].shape[0]
    joint = place(
        (3 * rows, mine[0].shape[1]), [(mine[k], 0, rows, k * rows, 0) for k in range(3)]
    )
    return core_swap(joint)


def joined_up(own, mine, other):
    rows, half = mine[0].shape
    items = [(own, 0, rows, lambda f, c: f * rows, 0)]
    for k in range(3):
        at = lambda f, c, k=k: (f ^ (k + 1)) * rows
        items.append((mine[k], 0, rows, at, lambda f, c: c * half))
        items.append((other, k * rows, rows, at, lambda f, c: (1 - c) * half))
    return place((4 * rows, 2 * half), items)


def joined_down(own, mine, other):
    rows, width = mine[0].shape
    items = [(own, 0, 2 * rows, lambda f, c: f * 2 * rows, 0)]
    for k in range(3):
        items.append((mine[k], 0, rows, lambda f, c, k=k: ((f ^ (k + 1)) * 2 + c) * rows, 0))
        items.append(
            (other, k * rows, rows, lambda f, c, k=k: ((f ^ (k + 1)) * 2 + 1 - c) * rows, 0)
        )
    return place((8 * rows, width), items)


def smooth_parts(values):
    share = 0.5 + 0.5 * lax.erf(values * (0.5**0.5))
    density = jnp.exp(-0.5 * values * values) * ((0.5 / jnp.pi) ** 0.5)
    return values * share, share + values * density


def one_table(pos, doc, rate, scaling):
    keeping = (pos[:, None] >= pos[None, :]) & (doc[:, None] == doc[None, :])
    spacing = jnp.where(keeping, (pos[:, None] - pos[None, :]).astype(jnp.float32), 0.0)
    return jnp.where(keeping, jnp.exp(rate * spacing) * scaling, 0.0)


def ctx_sum(x):
    return lax.psum_scatter(x, "ctx", scatter_dimension=0, tiled=True)


def body_heads(
    tokens,
    cotangent,
    w_query,
    w_key,
    w_value,
    w_gate,
    w_out,
    w_up,
    w_down,
    norm_gains,
    norm_biases,
    block_deal,
    doc_lengths,
):
    low = jnp.bfloat16
    ctx_size = lax.axis_size("ctx")
    fsdp_size = lax.axis_size("fsdp")
    tok_rows = tokens.shape[2]
    full_length = tok_rows * ctx_size
    width = tokens.shape[3]
    share = width // (ctx_size * fsdp_size)
    grad_scale = float(MICRO * fsdp_size * full_length) ** (-0.5)
    ctx_rank = lax.axis_index("ctx")
    fsdp_rank = lax.axis_index("fsdp")
    pos = stored_positions(block_deal, full_length, BLOCK)
    rate = jnp.log1p(-jnp.exp2(-5.0 - ctx_rank.astype(jnp.float32)))
    scaling = DK ** (-0.5)

    own_in = head_columns(w_query, w_key, w_value, w_gate, ctx_rank)
    tokens = after(tokens, own_in)
    rows_in = []
    norm_one = []
    x_own = []
    for m in range(MICRO):
        rows_in.append(after(tokens[m, 0], *x_own[-1:]).astype(jnp.float32))
        norm_one.append(jax.vjp(layer_norm, rows_in[m], norm_gains[0], norm_biases[0]))
        x_own.append(norm_one[m][0].astype(low))
    grad_rows = [cotangent[m, 0].astype(jnp.float32) for m in range(MICRO)]
    x_all = [lax.all_gather(x, "ctx", axis=0, tiled=True) for x in x_own]
    in_first = gather_first(own_in)
    up_mine_own, up_cut = up_pieces(w_up, fsdp_rank, ctx_size, fsdp_size)
    down_mine_own, down_cut = down_pieces(w_down, fsdp_rank, ctx_size, fsdp_size)
    out_cut = out_pieces(w_out, ctx_rank, fsdp_rank, fsdp_size)
    cuts = [up_mine_own, down_mine_own] + up_cut + down_cut + out_cut
    in_first = lax.optimization_barrier(tuple(in_first) + tuple(cuts))[:2]
    in_second = gather_second(*in_first)
    w_in = by_rank(own_in, *in_first, *in_second)
    out_cut = lax.optimization_barrier(tuple(out_cut) + tuple(in_second))[: len(out_cut)]
    out_parts = scatter_quarters(out_cut, ctx_size, fsdp_size)

    def mix(m, x_now):
        doc = document_ids(pos, doc_lengths[m, 0])
        table = one_table(pos, doc, rate, scaling)
        joint = jnp.dot(x_now, w_in[:, : 2 * DK + DV], preferred_element_type=jnp.float32).astype(low)
        gate_pre = jnp.dot(x_now, w_in[:, 2 * DK + DV :], preferred_element_type=jnp.float32)
        query, key, value = joint[:, :DK], joint[:, DK : 2 * DK], joint[:, 2 * DK :]
        attend = (contract_rows(query, key) * table).astype(low)
        retained = add_single(attend, value)
        mixed, mix_pull = jax.vjp(gated_mix, gate_pre, retained)
        return table, query, key, value, attend, mix_pull, mixed.astype(low)

    kept = [mix(0, x_all[0])]
    out_parts = lax.optimization_barrier(tuple(out_parts) + (kept[0][6],))[:-1]
    quarter = choose_quarter(out_parts, ctx_rank, fsdp_rank)
    out_first = gather_first(quarter)
    out_second = gather_second(*out_first)
    w_head = by_rank(quarter, *out_first, *out_second)
    part = add_single(kept[0][6], w_head).astype(low)
    attn_out = [ctx_sum(after(part, *x_all[1:]))]
    for m in range(1, MICRO):
        kept.append(mix(m, after(x_all[m], *out_parts)))
        part = add_single(kept[m][6], w_head).astype(low)
        attn_out.append(ctx_sum(part))
    cot_in = [after(cotangent[m, 0], *out_second) for m in range(MICRO)]
    cot_first = [gather_first(cot_in[m]) for m in range(MICRO)]
    firsts = [c for pair in cot_first for c in pair]
    up_cut = lax.optimization_barrier(tuple(up_cut) + tuple(firsts))[: len(up_cut)]
    down_cut = lax.optimization_barrier(tuple(down_cut) + tuple(firsts))[: len(down_cut)]
    up_mine = exchange(up_cut)
    down_mine = exchange(down_cut)
    cot_second = [gather_second(*cot_first[m]) for m in range(MICRO)]
    attn_out[0] = after(attn_out[0], part, *up_mine)
    up_own = joined_up(up_mine_own, up_mine, both_cores(up_mine))
    down_own = joined_down(down_mine_own, down_mine, both_cores(down_mine))
    cot_all = [by_offset(cot_in[m], *cot_first[m], *cot_second[m]) for m in range(MICRO)]

    outs = [None] * MICRO
    grad_attn = []
    grad_hidden = []
    ffn_kept = []
    norm_two_terms = []
    norm_part = None
    for m in range(MICRO):
        if m > 0:
            attn_out[m] = after(attn_out[m], norm_part)
        hidden = rows_in[m] + attn_out[m].astype(jnp.float32)
        normed_two, pull_two = jax.vjp(layer_norm, hidden, norm_gains[1], norm_biases[1])
        two_own = normed_two.astype(low)
        two_first = gather_first(two_own)
        two_all = by_offset(two_own, *two_first, *gather_second(*two_first))
        active, slope = smooth_parts(add_single(two_all, up_own))
        active_low, slope = lax.optimization_barrier((active.astype(low), slope))
        grad_up = (back_rows(cot_all[m], down_own) * slope).astype(low)
        norm_part = back_rows(grad_up, up_own).astype(low)
        grad_norm_two = after(plane_reduce_rows(norm_part), *grad_attn[-1:])
        grad_ln, gain_two, bias_two = pull_two(grad_norm_two)
        norm_two_terms.append((gain_two, bias_two))
        total = grad_rows[m] + grad_ln
        grad_hidden.append(total)
        grad_attn.append(total.astype(low))
        ffn_kept.append((two_all, grad_up, active_low, hidden))

    grad_all = [lax.all_gather(grad_attn[m], "ctx", axis=0, tiled=True) for m in range(MICRO)]

    def unmix(m, grad_now):
        table, query, key, value, attend, mix_pull, mixed_low = kept[m]
        grad_mixed = back_rows(grad_now, w_head)
        grad_gate, grad_ret = mix_pull(grad_mixed)
        ret_low = grad_ret.astype(low)
        grad_scores = (contract_rows(ret_low, value) * table).astype(low)
        grad_query = add_single(grad_scores, key).astype(low)
        grad_key = contract_cols(grad_scores, query).astype(low)
        grad_value = contract_cols(attend, ret_low).astype(low)
        return jnp.concatenate([grad_query, grad_key, grad_value, grad_gate.astype(low)], axis=1)

    terms = []
    in_term = None
    out_term = None
    sums = []
    for m in range(MICRO):
        grad_now = after(grad_all[m], *(grad_attn[1:] if m == 0 else terms[-1:]))
        grad_in = unmix(m, grad_now)
        part = back_rows(grad_in, w_in).astype(low)
        terms.append(part)
        sums.append(ctx_sum(after(part, *grad_all[m + 1 :], *sums[-1:])))
        x_now, mixed_now, grad_in = lax.optimization_barrier(
            (x_all[m], kept[m][6], grad_in, part)
        )[:3]
        in_now = contract_cols(x_now, grad_in)
        out_now = contract_cols(mixed_now, grad_all[m])
        in_term = in_now if m == 0 else in_term + in_now
        out_term = out_now if m == 0 else out_term + out_now
        if m == 0:
            ready = [after(ffn_kept[n][2], part, grad_attn[n]) for n in range(MICRO)]
            for n in range(MICRO):
                ffn_part = add_single(ready[n], down_own).astype(low)
                outs[n] = (ffn_kept[n][3] + plane_reduce_rows(ffn_part)).astype(low)
            up_grad = sum(contract_cols(k[0], after(k[1], part)) for k in ffn_kept).astype(low)
            down_grad = sum(contract_cols(ready[n], cot_all[n]) for n in range(MICRO)).astype(low)
    in_term = in_term.astype(low)
    out_term = out_term.astype(low)
    up_sum = ctx_sum(after(up_grad, sums[-1]))
    down_sum = ctx_sum(after(down_grad, sums[-1]))

    grad_tokens = []
    norm_one_terms = []
    for m in range(MICRO):
        grad_ln, gain_one, bias_one = norm_one[m][1](sums[m].astype(jnp.float32))
        norm_one_terms.append((gain_one, bias_one))
        grad_tokens.append(grad_hidden[m] + grad_ln)

    gain_rows = [sum(t[0] for t in norm_one_terms), sum(t[0] for t in norm_two_terms)]
    bias_rows = [sum(t[1] for t in norm_one_terms), sum(t[1] for t in norm_two_terms)]
    norm_sums = sum_everywhere(jnp.stack(gain_rows + bias_rows))
    in_view = in_term.reshape(ctx_size, fsdp_size, share, -1)
    in_sum = plane_reduce([pick(in_view, fsdp_rank ^ j, 1, 1)[:, 0] for j in range(fsdp_size)])
    in_mine = lax.all_to_all(after(in_sum.astype(low), norm_sums), "ctx", split_axis=0, concat_axis=0, tiled=True)
    rows = DV // fsdp_size
    g_out = plane_reduce([pick(out_term, fsdp_rank ^ j, rows, 0) for j in range(fsdp_size)])

    def by_head(first, size):
        part = in_mine[:, :, first : first + size].transpose(1, 0, 2)
        return part.reshape(share, -1).astype(jnp.float32) * grad_scale

    g_query = by_head(0, DK)
    g_key = by_head(DK, DK)
    g_value = by_head(2 * DK, DV)
    g_gate = by_head(2 * DK + DV, DV)

    up_view = up_sum.reshape(fsdp_size, share, -1)
    pieces = [lax.dynamic_index_in_dim(up_view, fsdp_rank, 0, keepdims=False)]
    for bit in range(1, fsdp_size):
        pieces.append(
            xy_swap(lax.dynamic_index_in_dim(up_view, fsdp_rank ^ bit, 0, keepdims=False), bit)
        )
    pieces = [p.reshape(share, ctx_size, -1) for p in in_rank_order(pieces, fsdp_rank)]
    g_up = jnp.stack(pieces, axis=2).reshape(share, FF).astype(jnp.float32) * grad_scale

    norm_sums = pick(norm_sums, ctx_rank * fsdp_size + fsdp_rank, share, 1) * grad_scale
    return (
        jnp.stack(outs)[:, None],
        jnp.stack(grad_tokens)[:, None],
        g_query,
        g_key,
        g_value,
        g_gate,
        g_out * grad_scale,
        g_up,
        down_sum.astype(jnp.float32) * grad_scale,
        norm_sums[:2],
        norm_sums[2:],
    )


def solution(mesh):
    in_specs = (
        P(None, "fsdp", "ctx", None),
        P(None, "fsdp", "ctx", None),
        P("fsdp", None),
        P("fsdp", None),
        P("fsdp", None),
        P("fsdp", None),
        P("fsdp", None),
        P("fsdp", None),
        P("fsdp", None),
        P(),
        P(),
        P(),
        P(None, "fsdp", None),
    )
    out_specs = (
        P(None, "fsdp", "ctx", None),
        P(None, "fsdp", "ctx", None),
        P(("ctx", "fsdp"), None),
        P(("ctx", "fsdp"), None),
        P(("ctx", "fsdp"), None),
        P(("ctx", "fsdp"), None),
        P(("ctx", "fsdp"), None),
        P(("ctx", "fsdp"), None),
        P(("ctx", "fsdp"), None),
        P(None, ("ctx", "fsdp")),
        P(None, ("ctx", "fsdp")),
    )
    by_heads = mesh.shape["ctx"] == HEADS and mesh.shape["fsdp"] == 4
    chosen = body_heads if by_heads else body
    return jax.shard_map(chosen, mesh=mesh, in_specs=in_specs, out_specs=out_specs, check_vma=False)
```

```python
import jax
import jax.numpy as jnp
from jax import lax
from jax.experimental import pallas as pl
from jax.sharding import PartitionSpec as P

HEADS = 8
DK = 256
DV = 512
FF = 4096
MICRO = 2
QW = 2048
VW = 4096
BLOCK = 64


epsilon = 1e-05
group_floor = 1.0


def layer_norm(values, gain_row, offset):
    center = jnp.mean(values, axis=-1, keepdims=True)
    centred = values - center
    spread = jnp.mean(centred * centred, axis=-1, keepdims=True)
    return centred * lax.rsqrt(spread + epsilon) * gain_row + offset


def gated_mix(gate_pre, retained):
    number = retained.shape[0]
    grouped = retained.reshape(number, -1, DV)
    center = jnp.mean(grouped, axis=-1, keepdims=True)
    centred = grouped - center
    spread = jnp.mean(centred * centred, axis=-1, keepdims=True)
    normed = (centred * lax.rsqrt(spread + group_floor)).reshape(number, -1)
    return jax.nn.silu(gate_pre) * normed


def smooth_act(values):
    return jax.nn.gelu(values, approximate=False)


def stored_positions(block_deal, full_length, block_size):
    stored = jnp.arange(full_length, dtype=jnp.int32)
    block_ids = stored // block_size
    slots_all = jnp.arange(block_deal.shape[0], dtype=jnp.int32)
    picked = jnp.sum(
        jnp.where(block_ids[:, None] == slots_all[None, :], block_deal[None, :], 0),
        axis=1,
        dtype=jnp.int32,
    )
    return picked * block_size + stored % block_size


def document_ids(positions, doc_sizes):
    starts = jnp.cumsum(doc_sizes, dtype=jnp.int32) - doc_sizes
    return (
        jnp.sum((positions[:, None] >= starts[None, :]).astype(jnp.int32), axis=1, dtype=jnp.int32)
        - 1
    )


def decay_table(query_pos, query_doc, key_pos, key_doc, decay_log, scaling):
    keeping = (query_pos[:, None] >= key_pos[None, :]) & (query_doc[:, None] == key_doc[None, :])
    spacing = jnp.where(keeping, (query_pos[:, None] - key_pos[None, :]).astype(jnp.float32), 0.0)
    factor = jnp.exp(decay_log[:, None, None] * spacing[None])
    return jnp.where(keeping[None], factor * scaling, 0.0)


def contract_rows(left, right):
    return lax.dot_general(
        left, right, (((1,), (1,)), ((), ())), preferred_element_type=jnp.float32
    )


def contract_cols(left, right):
    return lax.dot_general(
        left, right, (((0,), (0,)), ((), ())), preferred_element_type=jnp.float32
    )


def add_single(left, weight_piece):
    return jnp.dot(left, weight_piece, preferred_element_type=jnp.float32)


def back_rows(left, weight_piece):
    return contract_rows(left, weight_piece)


def weight_term(kept_acts, number):
    normed_one, grads_in, normed_two, grads_up, mixed_all, grads_attn, active_all, grads_ffn = (
        kept_acts
    )
    pieces = [
        contract_cols(normed_one, grads_in),
        contract_cols(normed_two, grads_up),
        contract_cols(mixed_all, grads_attn).reshape(number, -1),
        contract_cols(active_all, grads_ffn).reshape(number, -1),
    ]
    return jnp.concatenate(pieces, axis=1)


def body(
    tokens,
    cotangent,
    w_query,
    w_key,
    w_value,
    w_gate,
    w_out,
    w_up,
    w_down,
    norm_gains,
    norm_biases,
    block_deal,
    doc_lengths,
):
    ctx_size = lax.axis_size("ctx")
    tok_rows = tokens.shape[2]
    full_length = tok_rows * ctx_size
    model_width = tokens.shape[3]
    share_rows = model_width // lax.axis_size(("ctx", "fsdp"))
    grad_scale = float(MICRO * lax.axis_size("fsdp") * full_length) ** (-0.5)
    own_start = lax.axis_index("ctx") * tok_rows
    key_pos = stored_positions(block_deal, full_length, BLOCK)
    query_pos = lax.dynamic_slice_in_dim(key_pos, own_start, tok_rows)
    decay_log = jnp.log1p(-jnp.exp2(-5.0 - jnp.arange(HEADS).astype(jnp.float32)))
    scaling = DK ** (-0.5)
    out_list = []
    grad_list = []
    weight_sum = None
    gain_sum = jnp.zeros((2, model_width), jnp.float32)
    bias_sum = jnp.zeros((2, model_width), jnp.float32)
    for batch_index in range(MICRO):
        rows_in = tokens[batch_index, 0].astype(jnp.float32)
        grad_rows = cotangent[batch_index, 0].astype(jnp.float32)
        key_doc = document_ids(key_pos, doc_lengths[batch_index, 0])
        query_doc = lax.dynamic_slice_in_dim(key_doc, own_start, tok_rows)
        table = decay_table(query_pos, query_doc, key_pos, key_doc, decay_log, scaling)
        normed_one, norm_pull_one = jax.vjp(layer_norm, rows_in, norm_gains[0], norm_biases[0])
        low_one = normed_one.astype(jnp.bfloat16)
        pieces = (
            lax.all_gather(w_query, "fsdp", axis=0, tiled=True),
            lax.all_gather(w_key, "fsdp", axis=0, tiled=True),
            lax.all_gather(w_value, "fsdp", axis=0, tiled=True),
            lax.all_gather(w_gate, "fsdp", axis=0, tiled=True),
        )
        query_f, key_f, value_f, gate_pre = tuple(
            (
                jnp.dot(low_one, weight_piece, preferred_element_type=jnp.float32)
                for weight_piece in pieces
            )
        )
        query_low = query_f.astype(jnp.bfloat16)
        key_low = key_f.astype(jnp.bfloat16)
        value_low = value_f.astype(jnp.bfloat16)
        keys_all, values_all = (
            lax.all_gather(key_low, "ctx", axis=0, tiled=True),
            lax.all_gather(value_low, "ctx", axis=0, tiled=True),
        )
        query_heads = query_low.reshape(tok_rows, HEADS, DK)
        key_heads = keys_all.reshape(full_length, HEADS, DK)
        value_heads = values_all.reshape(full_length, HEADS, DV)
        scores = jnp.einsum(
            "thd,shd->hts", query_heads, key_heads, preferred_element_type=jnp.float32
        )
        attend = (scores * table).astype(jnp.bfloat16)
        retained = jnp.einsum(
            "hts,shd->thd", attend, value_heads, preferred_element_type=jnp.float32
        ).reshape(tok_rows, VW)
        mixed, mix_pull = jax.vjp(gated_mix, gate_pre, retained)
        mixed_low = mixed.astype(jnp.bfloat16)
        attn_out = add_single(mixed_low, lax.all_gather(w_out, "fsdp", axis=0, tiled=True))
        hidden = rows_in + attn_out
        normed_two, norm_pull_two = jax.vjp(layer_norm, hidden, norm_gains[1], norm_biases[1])
        low_two = normed_two.astype(jnp.bfloat16)
        up_pre = add_single(low_two, lax.all_gather(w_up, "fsdp", axis=0, tiled=True))
        active, act_pull = jax.vjp(smooth_act, up_pre)
        active_low = active.astype(jnp.bfloat16)
        ffn_out = add_single(active_low, lax.all_gather(w_down, "fsdp", axis=0, tiled=True))
        out_list.append((hidden + ffn_out).astype(jnp.bfloat16))
        grad_ffn = grad_rows.astype(jnp.bfloat16)
        grad_act = back_rows(grad_ffn, lax.all_gather(w_down, "fsdp", axis=0, tiled=True))
        grad_up = act_pull(grad_act)[0].astype(jnp.bfloat16)
        grad_norm_two = back_rows(grad_up, lax.all_gather(w_up, "fsdp", axis=0, tiled=True))
        grad_hidden_ln, grad_gain_two, grad_bias_two = norm_pull_two(grad_norm_two)
        grad_hidden = grad_rows + grad_hidden_ln
        grad_attn = grad_hidden.astype(jnp.bfloat16)
        grad_mixed = back_rows(grad_attn, lax.all_gather(w_out, "fsdp", axis=0, tiled=True))
        grad_gate_f, grad_ret_f = mix_pull(grad_mixed)
        grad_gate = grad_gate_f.astype(jnp.bfloat16)
        ret_low = grad_ret_f.astype(jnp.bfloat16)
        ret_heads = ret_low.reshape(tok_rows, HEADS, DV)
        grad_attend = jnp.einsum(
            "thd,shd->hts", ret_heads, value_heads, preferred_element_type=jnp.float32
        )
        grad_scores = (grad_attend * table).astype(jnp.bfloat16)
        grad_query = (
            jnp.einsum("hts,shd->thd", grad_scores, key_heads, preferred_element_type=jnp.float32)
            .reshape(tok_rows, QW)
            .astype(jnp.bfloat16)
        )
        key_part = jnp.einsum(
            "hts,thd->shd", grad_scores, query_heads, preferred_element_type=jnp.float32
        ).reshape(tok_rows * lax.axis_size("ctx"), QW)
        value_part = jnp.einsum(
            "hts,thd->shd", attend, ret_heads, preferred_element_type=jnp.float32
        ).reshape(tok_rows * lax.axis_size("ctx"), VW)
        key_value_sum = lax.psum_scatter(
            jnp.concatenate([key_part, value_part], axis=1).astype(jnp.bfloat16),
            "ctx",
            scatter_dimension=0,
            tiled=True,
        ).astype(jnp.float32)
        grad_key = key_value_sum[:, :QW].astype(jnp.bfloat16)
        grad_value = key_value_sum[:, QW:].astype(jnp.bfloat16)
        term_now = (
            contract_rows(grad_query, lax.all_gather(w_query, "fsdp", axis=0, tiled=True))
            + contract_rows(grad_key, lax.all_gather(w_key, "fsdp", axis=0, tiled=True))
            + contract_rows(grad_value, lax.all_gather(w_value, "fsdp", axis=0, tiled=True))
            + contract_rows(grad_gate, lax.all_gather(w_gate, "fsdp", axis=0, tiled=True))
        )
        grad_rows_ln, grad_gain_one, grad_bias_one = norm_pull_one(term_now)
        grad_list.append(grad_hidden + grad_rows_ln)
        gain_sum = gain_sum + jnp.stack([grad_gain_one, grad_gain_two])
        bias_sum = bias_sum + jnp.stack([grad_bias_one, grad_bias_two])
        kept_now = (
            low_one,
            jnp.concatenate([grad_query, grad_key, grad_value, grad_gate], axis=1),
            low_two,
            grad_up,
            mixed_low,
            grad_attn,
            active_low,
            grad_ffn,
        )
        term_sum = lax.psum_scatter(
            weight_term(kept_now, share_rows * lax.axis_size(("ctx", "fsdp"))),
            ("ctx", "fsdp"),
            scatter_dimension=0,
            tiled=True,
        )
        weight_sum = term_sum if weight_sum is None else weight_sum + term_sum
    weight_sum = weight_sum * grad_scale
    bounds = [QW, 2 * QW, 2 * QW + VW, 2 * QW + 2 * VW, 2 * QW + 2 * VW + FF, 2 * QW + 3 * VW + FF]
    g_query, g_key, g_value, g_gate, g_up, g_out_flat, g_down_flat = jnp.split(
        weight_sum, bounds, axis=1
    )
    g_out = g_out_flat.reshape(share_rows * (VW // model_width), model_width)
    g_down = g_down_flat.reshape(share_rows * (FF // model_width), model_width)
    gain_grads, bias_grads = (
        lax.psum_scatter(gain_sum, ("ctx", "fsdp"), scatter_dimension=1, tiled=True),
        lax.psum_scatter(bias_sum, ("ctx", "fsdp"), scatter_dimension=1, tiled=True),
    )
    gain_grads = gain_grads * grad_scale
    bias_grads = bias_grads * grad_scale
    output = jnp.stack(out_list)[:, None]
    grad_tokens = jnp.stack(grad_list)[:, None]
    return (
        output,
        grad_tokens,
        g_query,
        g_key,
        g_value,
        g_gate,
        g_out,
        g_up,
        g_down,
        gain_grads,
        bias_grads,
    )


def xy_swap(x, bit):
    return lax.ppermute(x, "fsdp", [(i, i ^ bit) for i in range(lax.axis_size("fsdp"))])


def core_swap(x):
    return lax.ppermute(x, "ctx", [(i, i ^ 1) for i in range(lax.axis_size("ctx"))])


def after(x, *earlier):
    return lax.optimization_barrier((x,) + tuple(earlier))[0]


def place(shape, items):
    arrays = []
    for item in items:
        if not any(item[0] is a for a in arrays):
            arrays.append(item[0])
    slots = [[item[0] is a for a in arrays].index(True) for item in items]
    kind = arrays[0].dtype

    def kernel(*refs):
        out = refs[len(arrays)]
        rank = lax.axis_index("fsdp")
        core = lax.axis_index("ctx") % 2
        for number, (array, start, rows, row, column) in enumerate(items):
            width = array.shape[1]
            step = min(rows, 64)
            source = refs[slots[number]]
            base = row(rank, core) if callable(row) else row

            def copy(first, width=width, step=step, source=source, base=base, start=start, rows=rows):
                def one(turn, carry):
                    place_in = pl.multiple_of(start + turn * step, step)
                    place_out = pl.multiple_of(base + turn * step, step)
                    out[pl.ds(place_out, step), first : first + width] = source[
                        pl.ds(place_in, step), :
                    ]
                    return carry

                lax.fori_loop(0, rows // step, one, 0)

            if callable(column):
                for which in range(2):
                    pl.when(core == which)(lambda which=which: copy(column(rank, which)))
            else:
                copy(column)

    size = shape[0] * shape[1] * jnp.dtype(kind).itemsize
    return pl.pallas_call(
        kernel,
        out_shape=jax.ShapeDtypeStruct(shape, kind),
        cost_estimate=pl.CostEstimate(flops=0, bytes_accessed=2 * size, transcendentals=0),
    )(*arrays)


def gather_first(x):
    return xy_swap(x, 1), xy_swap(x, 2)


def gather_second(first, second):
    half = first.shape[0] // 2
    return xy_swap(first[:half], 2), xy_swap(second[half:], 1)


def by_offset(x, first, second, low_part, high_part):
    rows, half = x.shape[0], x.shape[0] // 2
    return place(
        (4 * rows, x.shape[1]),
        [
            (x, 0, rows, 0, 0),
            (first, 0, rows, rows, 0),
            (low_part, 0, half, 2 * rows, 0),
            (high_part, 0, half, 2 * rows + half, 0),
            (second, 0, rows, 3 * rows, 0),
        ],
    )


def by_rank(x, first, second, low_part, high_part):
    rows, half = x.shape[0], x.shape[0] // 2
    return place(
        (4 * rows, x.shape[1]),
        [
            (x, 0, rows, lambda f, c: f * rows, 0),
            (first, 0, rows, lambda f, c: (f ^ 1) * rows, 0),
            (low_part, 0, half, lambda f, c: (f ^ 3) * rows, 0),
            (high_part, 0, half, lambda f, c: (f ^ 3) * rows + half, 0),
            (second, 0, rows, lambda f, c: (f ^ 2) * rows, 0),
        ],
    )


def plane_reduce_rows(part):
    rows, half = part.shape[0] // 4, part.shape[1] // 2
    wide = lambda v: v.astype(jnp.float32)
    left_in = xy_swap(part[rows : 3 * rows, :half], 1)
    right_in = xy_swap(part[2 * rows :, half:], 2)
    left_far = wide(part[3 * rows :, :half]) + wide(left_in[rows:])
    right_far = wide(part[rows : 2 * rows, half:]) + wide(right_in[:rows])
    left_last = xy_swap(left_far.astype(jnp.bfloat16), 2)
    right_last = xy_swap(right_far.astype(jnp.bfloat16), 1)
    left = wide(part[:rows, :half]) + wide(left_in[:rows]) + wide(left_last)
    right = wide(part[:rows, half:]) + wide(right_in[rows:]) + wide(right_last)
    return jnp.concatenate([left, right], axis=1)


def plane_reduce(blocks):
    half = blocks[0].shape[-1] // 2
    left = [b[..., :half] for b in blocks]
    right = [b[..., half:] for b in blocks]
    left_in = xy_swap(jnp.stack([left[1], left[3]]), 1).astype(jnp.float32)
    right_in = xy_swap(jnp.stack([right[2], right[3]]), 2).astype(jnp.float32)
    left_far = left[2].astype(jnp.float32) + left_in[1]
    right_far = right[1].astype(jnp.float32) + right_in[1]
    left_last = xy_swap(left_far.astype(jnp.bfloat16), 2).astype(jnp.float32)
    right_last = xy_swap(right_far.astype(jnp.bfloat16), 1).astype(jnp.float32)
    left_own = left[0].astype(jnp.float32) + left_in[0]
    right_own = right[0].astype(jnp.float32) + right_in[0]
    return jnp.concatenate([left_own + left_last, right_own + right_last], axis=-1)


def sum_everywhere(x):
    for axis in ("ctx", "fsdp"):
        size = lax.axis_size(axis)
        bit = 1
        while bit < size:
            x = x + lax.ppermute(x, axis, [(i, i ^ bit) for i in range(size)])
            bit *= 2
    return x


def in_rank_order(blocks, rank):
    odd = (rank % 2) == 1
    upper = (rank // 2) == 1
    one = [
        jnp.where(odd, blocks[1], blocks[0]),
        jnp.where(odd, blocks[0], blocks[1]),
        jnp.where(odd, blocks[3], blocks[2]),
        jnp.where(odd, blocks[2], blocks[3]),
    ]
    return [
        jnp.where(upper, one[2], one[0]),
        jnp.where(upper, one[3], one[1]),
        jnp.where(upper, one[0], one[2]),
        jnp.where(upper, one[1], one[3]),
    ]


def pick(x, index, size, axis):
    return lax.dynamic_slice_in_dim(x, index * size, size, axis)


def head_columns(w_query, w_key, w_value, w_gate, ctx_rank):
    return jnp.concatenate(
        [
            pick(w_query, ctx_rank, DK, 1),
            pick(w_key, ctx_rank, DK, 1),
            pick(w_value, ctx_rank, DV, 1),
            pick(w_gate, ctx_rank, DV, 1),
        ],
        axis=1,
    )


def out_pieces(w_out, ctx_rank, fsdp_rank, fsdp_size):
    rows = DV // fsdp_size
    start = (ctx_rank % 2) * DV
    return [
        lax.dynamic_slice_in_dim(w_out, start + (fsdp_rank ^ bit) * rows, rows, 0)
        for bit in range(fsdp_size)
    ]


def scatter_quarters(cuts, ctx_size, fsdp_size):
    parts = [cuts[0]]
    for bit in range(1, fsdp_size):
        pairs = [
            (c * fsdp_size + c // 2, c * fsdp_size + ((c // 2) ^ bit)) for c in range(ctx_size)
        ]
        parts.append(lax.ppermute(cuts[bit], ("ctx", "fsdp"), pairs))
    return parts


def choose_quarter(parts, ctx_rank, fsdp_rank):
    quarter = parts[0]
    for bit in range(1, len(parts)):
        quarter = jnp.where((fsdp_rank ^ (ctx_rank // 2)) == bit, parts[bit], quarter)
    return quarter


def up_pieces(w_up, fsdp_rank, ctx_size, fsdp_size):
    unit = FF // (ctx_size * fsdp_size)
    half = ctx_size // 2
    core = lax.axis_index("ctx") % 2

    def cut(bit, part):
        starts = [(part * half + i) * fsdp_size * unit for i in range(half)]
        place_in = (fsdp_rank ^ bit) * unit
        return jnp.concatenate(
            [lax.dynamic_slice_in_dim(w_up, s + place_in, unit, 1) for s in starts], axis=1
        )

    own = jnp.concatenate([cut(0, 0), cut(0, 1)], axis=1)
    return own, [cut(bit, core) for bit in range(1, fsdp_size)]


def down_pieces(w_down, fsdp_rank, ctx_size, fsdp_size):
    unit = FF // (ctx_size * fsdp_size)
    core = lax.axis_index("ctx") % 2

    def cut(bit, part):
        start = (part * fsdp_size + (fsdp_rank ^ bit)) * unit
        return lax.dynamic_slice_in_dim(w_down, start, unit, 0)

    own = jnp.concatenate([cut(0, 0), cut(0, 1)], axis=0)
    return own, [cut(bit, core) for bit in range(1, fsdp_size)]


def exchange(pieces):
    return [xy_swap(pieces[bit - 1], bit) for bit in (1, 2, 3)]


def both_cores(mine):
    rows = mine[0].shape[0]
    joint = place(
        (3 * rows, mine[0].shape[1]), [(mine[k], 0, rows, k * rows, 0) for k in range(3)]
    )
    return core_swap(joint)


def joined_up(own, mine, other):
    rows, half = mine[0].shape
    items = [(own, 0, rows, lambda f, c: f * rows, 0)]
    for k in range(3):
        at = lambda f, c, k=k: (f ^ (k + 1)) * rows
        items.append((mine[k], 0, rows, at, lambda f, c: c * half))
        items.append((other, k * rows, rows, at, lambda f, c: (1 - c) * half))
    return place((4 * rows, 2 * half), items)


def joined_down(own, mine, other):
    rows, width = mine[0].shape
    items = [(own, 0, 2 * rows, lambda f, c: f * 2 * rows, 0)]
    for k in range(3):
        items.append((mine[k], 0, rows, lambda f, c, k=k: ((f ^ (k + 1)) * 2 + c) * rows, 0))
        items.append(
            (other, k * rows, rows, lambda f, c, k=k: ((f ^ (k + 1)) * 2 + 1 - c) * rows, 0)
        )
    return place((8 * rows, width), items)


def smooth_parts(values):
    share = 0.5 + 0.5 * lax.erf(values * (0.5**0.5))
    density = jnp.exp(-0.5 * values * values) * ((0.5 / jnp.pi) ** 0.5)
    return values * share, share + values * density


def one_table(pos, doc, rate, scaling):
    keeping = (pos[:, None] >= pos[None, :]) & (doc[:, None] == doc[None, :])
    spacing = jnp.where(keeping, (pos[:, None] - pos[None, :]).astype(jnp.float32), 0.0)
    return jnp.where(keeping, jnp.exp(rate * spacing) * scaling, 0.0)


def ctx_sum(x):
    return lax.psum_scatter(x, "ctx", scatter_dimension=0, tiled=True)


def body_heads(
    tokens,
    cotangent,
    w_query,
    w_key,
    w_value,
    w_gate,
    w_out,
    w_up,
    w_down,
    norm_gains,
    norm_biases,
    block_deal,
    doc_lengths,
):
    low = jnp.bfloat16
    ctx_size = lax.axis_size("ctx")
    fsdp_size = lax.axis_size("fsdp")
    tok_rows = tokens.shape[2]
    full_length = tok_rows * ctx_size
    width = tokens.shape[3]
    share = width // (ctx_size * fsdp_size)
    grad_scale = float(MICRO * fsdp_size * full_length) ** (-0.5)
    ctx_rank = lax.axis_index("ctx")
    fsdp_rank = lax.axis_index("fsdp")
    pos = stored_positions(block_deal, full_length, BLOCK)
    rate = jnp.log1p(-jnp.exp2(-5.0 - ctx_rank.astype(jnp.float32)))
    scaling = DK ** (-0.5)

    own_in = head_columns(w_query, w_key, w_value, w_gate, ctx_rank)
    tokens = after(tokens, own_in)
    rows_in = []
    norm_one = []
    x_own = []
    for m in range(MICRO):
        rows_in.append(after(tokens[m, 0], *x_own[-1:]).astype(jnp.float32))
        norm_one.append(jax.vjp(layer_norm, rows_in[m], norm_gains[0], norm_biases[0]))
        x_own.append(norm_one[m][0].astype(low))
    grad_rows = [cotangent[m, 0].astype(jnp.float32) for m in range(MICRO)]
    x_all = [lax.all_gather(x, "ctx", axis=0, tiled=True) for x in x_own]
    in_first = gather_first(own_in)
    up_mine_own, up_cut = up_pieces(w_up, fsdp_rank, ctx_size, fsdp_size)
    down_mine_own, down_cut = down_pieces(w_down, fsdp_rank, ctx_size, fsdp_size)
    out_cut = out_pieces(w_out, ctx_rank, fsdp_rank, fsdp_size)
    cuts = [up_mine_own, down_mine_own] + up_cut + down_cut + out_cut
    in_first = lax.optimization_barrier(tuple(in_first) + tuple(cuts))[:2]
    in_second = gather_second(*in_first)
    w_in = by_rank(own_in, *in_first, *in_second)
    out_cut = lax.optimization_barrier(tuple(out_cut) + tuple(in_second))[: len(out_cut)]
    out_parts = scatter_quarters(out_cut, ctx_size, fsdp_size)

    def mix(m, x_now):
        doc = document_ids(pos, doc_lengths[m, 0])
        table = one_table(pos, doc, rate, scaling)
        joint = jnp.dot(x_now, w_in[:, : 2 * DK + DV], preferred_element_type=jnp.float32).astype(low)
        gate_pre = jnp.dot(x_now, w_in[:, 2 * DK + DV :], preferred_element_type=jnp.float32)
        query, key, value = joint[:, :DK], joint[:, DK : 2 * DK], joint[:, 2 * DK :]
        attend = (contract_rows(query, key) * table).astype(low)
        retained = add_single(attend, value)
        mixed, mix_pull = jax.vjp(gated_mix, gate_pre, retained)
        return table, query, key, value, attend, mix_pull, mixed.astype(low)

    kept = [mix(0, x_all[0])]
    out_parts = lax.optimization_barrier(tuple(out_parts) + (kept[0][6],))[:-1]
    quarter = choose_quarter(out_parts, ctx_rank, fsdp_rank)
    out_first = gather_first(quarter)
    out_second = gather_second(*out_first)
    w_head = by_rank(quarter, *out_first, *out_second)
    part = add_single(kept[0][6], w_head).astype(low)
    attn_out = [ctx_sum(after(part, *x_all[1:]))]
    for m in range(1, MICRO):
        kept.append(mix(m, after(x_all[m], *out_parts)))
        part = add_single(kept[m][6], w_head).astype(low)
        attn_out.append(ctx_sum(part))
    cot_in = [after(cotangent[m, 0], *out_second) for m in range(MICRO)]
    cot_first = [gather_first(cot_in[m]) for m in range(MICRO)]
    firsts = [c for pair in cot_first for c in pair]
    up_cut = lax.optimization_barrier(tuple(up_cut) + tuple(firsts))[: len(up_cut)]
    down_cut = lax.optimization_barrier(tuple(down_cut) + tuple(firsts))[: len(down_cut)]
    up_mine = exchange(up_cut)
    down_mine = exchange(down_cut)
    cot_second = [gather_second(*cot_first[m]) for m in range(MICRO)]
    attn_out[0] = after(attn_out[0], part, *up_mine)
    up_own = joined_up(up_mine_own, up_mine, both_cores(up_mine))
    down_own = joined_down(down_mine_own, down_mine, both_cores(down_mine))
    cot_all = [by_offset(cot_in[m], *cot_first[m], *cot_second[m]) for m in range(MICRO)]

    outs = [None] * MICRO
    grad_attn = []
    grad_hidden = []
    ffn_kept = []
    norm_two_terms = []
    norm_part = None
    for m in range(MICRO):
        if m > 0:
            attn_out[m] = after(attn_out[m], norm_part)
        hidden = rows_in[m] + attn_out[m].astype(jnp.float32)
        normed_two, pull_two = jax.vjp(layer_norm, hidden, norm_gains[1], norm_biases[1])
        two_own = normed_two.astype(low)
        two_first = gather_first(two_own)
        two_all = by_offset(two_own, *two_first, *gather_second(*two_first))
        active, slope = smooth_parts(add_single(two_all, up_own))
        active_low, slope = lax.optimization_barrier((active.astype(low), slope))
        grad_up = (back_rows(cot_all[m], down_own) * slope).astype(low)
        norm_part = back_rows(grad_up, up_own).astype(low)
        grad_norm_two = after(plane_reduce_rows(norm_part), *grad_attn[-1:])
        grad_ln, gain_two, bias_two = pull_two(grad_norm_two)
        norm_two_terms.append((gain_two, bias_two))
        total = grad_rows[m] + grad_ln
        grad_hidden.append(total)
        grad_attn.append(total.astype(low))
        ffn_kept.append((two_all, grad_up, active_low, hidden))

    grad_all = [lax.all_gather(grad_attn[m], "ctx", axis=0, tiled=True) for m in range(MICRO)]

    def unmix(m, grad_now):
        table, query, key, value, attend, mix_pull, mixed_low = kept[m]
        grad_mixed = back_rows(grad_now, w_head)
        grad_gate, grad_ret = mix_pull(grad_mixed)
        ret_low = grad_ret.astype(low)
        grad_scores = (contract_rows(ret_low, value) * table).astype(low)
        grad_query = add_single(grad_scores, key).astype(low)
        grad_key = contract_cols(grad_scores, query).astype(low)
        grad_value = contract_cols(attend, ret_low).astype(low)
        return jnp.concatenate([grad_query, grad_key, grad_value, grad_gate.astype(low)], axis=1)

    terms = []
    in_term = None
    out_term = None
    sums = []
    for m in range(MICRO):
        grad_now = after(grad_all[m], *(grad_attn[1:] if m == 0 else terms[-1:]))
        grad_in = unmix(m, grad_now)
        part = back_rows(grad_in, w_in).astype(low)
        terms.append(part)
        sums.append(ctx_sum(after(part, *grad_all[m + 1 :], *sums[-1:])))
        x_now, mixed_now, grad_in = lax.optimization_barrier(
            (x_all[m], kept[m][6], grad_in, part)
        )[:3]
        in_now = contract_cols(x_now, grad_in)
        out_now = contract_cols(mixed_now, grad_all[m])
        in_term = in_now if m == 0 else (in_term + in_now).astype(low)
        out_term = out_now if m == 0 else (out_term + out_now).astype(low)
        sums[m] = after(sums[m], in_term, out_term)
        if m == 0:
            ready = [after(ffn_kept[n][2], part, grad_attn[n]) for n in range(MICRO)]
            for n in range(MICRO):
                ffn_part = add_single(ready[n], down_own).astype(low)
                outs[n] = (ffn_kept[n][3] + plane_reduce_rows(ffn_part)).astype(low)
            up_grad = sum(contract_cols(k[0], after(k[1], part)) for k in ffn_kept).astype(low)
            down_grad = sum(contract_cols(ready[n], cot_all[n]) for n in range(MICRO)).astype(low)
    up_sum = ctx_sum(after(up_grad, sums[-1]))
    down_sum = ctx_sum(after(down_grad, sums[-1]))

    grad_tokens = []
    norm_one_terms = []
    for m in range(MICRO):
        grad_ln, gain_one, bias_one = norm_one[m][1](sums[m].astype(jnp.float32))
        norm_one_terms.append((gain_one, bias_one))
        grad_tokens.append(grad_hidden[m] + grad_ln)

    gain_rows = [sum(t[0] for t in norm_one_terms), sum(t[0] for t in norm_two_terms)]
    bias_rows = [sum(t[1] for t in norm_one_terms), sum(t[1] for t in norm_two_terms)]
    norm_sums = sum_everywhere(jnp.stack(gain_rows + bias_rows))
    in_view = in_term.reshape(ctx_size, fsdp_size, share, -1)
    in_sum = plane_reduce([pick(in_view, fsdp_rank ^ j, 1, 1)[:, 0] for j in range(fsdp_size)])
    in_mine = lax.all_to_all(after(in_sum.astype(low), norm_sums), "ctx", split_axis=0, concat_axis=0, tiled=True)
    rows = DV // fsdp_size
    g_out = plane_reduce([pick(out_term, fsdp_rank ^ j, rows, 0) for j in range(fsdp_size)])

    def by_head(first, size):
        part = in_mine[:, :, first : first + size].transpose(1, 0, 2)
        return part.reshape(share, -1).astype(jnp.float32) * grad_scale

    g_query = by_head(0, DK)
    g_key = by_head(DK, DK)
    g_value = by_head(2 * DK, DV)
    g_gate = by_head(2 * DK + DV, DV)

    up_view = up_sum.reshape(fsdp_size, share, -1)
    pieces = [lax.dynamic_index_in_dim(up_view, fsdp_rank, 0, keepdims=False)]
    for bit in range(1, fsdp_size):
        pieces.append(
            xy_swap(lax.dynamic_index_in_dim(up_view, fsdp_rank ^ bit, 0, keepdims=False), bit)
        )
    pieces = [p.reshape(share, ctx_size, -1) for p in in_rank_order(pieces, fsdp_rank)]
    g_up = jnp.stack(pieces, axis=2).reshape(share, FF).astype(jnp.float32) * grad_scale

    norm_sums = pick(norm_sums, ctx_rank * fsdp_size + fsdp_rank, share, 1) * grad_scale
    return (
        jnp.stack(outs)[:, None],
        jnp.stack(grad_tokens)[:, None],
        g_query,
        g_key,
        g_value,
        g_gate,
        g_out * grad_scale,
        g_up,
        down_sum.astype(jnp.float32) * grad_scale,
        norm_sums[:2],
        norm_sums[2:],
    )


def solution(mesh):
    in_specs = (
        P(None, "fsdp", "ctx", None),
        P(None, "fsdp", "ctx", None),
        P("fsdp", None),
        P("fsdp", None),
        P("fsdp", None),
        P("fsdp", None),
        P("fsdp", None),
        P("fsdp", None),
        P("fsdp", None),
        P(),
        P(),
        P(),
        P(None, "fsdp", None),
    )
    out_specs = (
        P(None, "fsdp", "ctx", None),
        P(None, "fsdp", "ctx", None),
        P(("ctx", "fsdp"), None),
        P(("ctx", "fsdp"), None),
        P(("ctx", "fsdp"), None),
        P(("ctx", "fsdp"), None),
        P(("ctx", "fsdp"), None),
        P(("ctx", "fsdp"), None),
        P(("ctx", "fsdp"), None),
        P(None, ("ctx", "fsdp")),
        P(None, ("ctx", "fsdp")),
    )
    by_heads = mesh.shape["ctx"] == HEADS and mesh.shape["fsdp"] == 4
    chosen = body_heads if by_heads else body
    return jax.shard_map(chosen, mesh=mesh, in_specs=in_specs, out_specs=out_specs, check_vma=False)
```

```python
import jax
import jax.numpy as jnp
from jax import lax
from jax.experimental import pallas as pl
from jax.sharding import PartitionSpec as P

HEADS = 8
DK = 256
DV = 512
FF = 4096
MICRO = 2
QW = 2048
VW = 4096
BLOCK = 64


epsilon = 1e-05
group_floor = 1.0


def layer_norm(values, gain_row, offset):
    center = jnp.mean(values, axis=-1, keepdims=True)
    centred = values - center
    spread = jnp.mean(centred * centred, axis=-1, keepdims=True)
    return centred * lax.rsqrt(spread + epsilon) * gain_row + offset


def gated_mix(gate_pre, retained):
    number = retained.shape[0]
    grouped = retained.reshape(number, -1, DV)
    center = jnp.mean(grouped, axis=-1, keepdims=True)
    centred = grouped - center
    spread = jnp.mean(centred * centred, axis=-1, keepdims=True)
    normed = (centred * lax.rsqrt(spread + group_floor)).reshape(number, -1)
    return jax.nn.silu(gate_pre) * normed


def smooth_act(values):
    return jax.nn.gelu(values, approximate=False)


def stored_positions(block_deal, full_length, block_size):
    stored = jnp.arange(full_length, dtype=jnp.int32)
    block_ids = stored // block_size
    slots_all = jnp.arange(block_deal.shape[0], dtype=jnp.int32)
    picked = jnp.sum(
        jnp.where(block_ids[:, None] == slots_all[None, :], block_deal[None, :], 0),
        axis=1,
        dtype=jnp.int32,
    )
    return picked * block_size + stored % block_size


def document_ids(positions, doc_sizes):
    starts = jnp.cumsum(doc_sizes, dtype=jnp.int32) - doc_sizes
    return (
        jnp.sum((positions[:, None] >= starts[None, :]).astype(jnp.int32), axis=1, dtype=jnp.int32)
        - 1
    )


def decay_table(query_pos, query_doc, key_pos, key_doc, decay_log, scaling):
    keeping = (query_pos[:, None] >= key_pos[None, :]) & (query_doc[:, None] == key_doc[None, :])
    spacing = jnp.where(keeping, (query_pos[:, None] - key_pos[None, :]).astype(jnp.float32), 0.0)
    factor = jnp.exp(decay_log[:, None, None] * spacing[None])
    return jnp.where(keeping[None], factor * scaling, 0.0)


def contract_rows(left, right):
    return lax.dot_general(
        left, right, (((1,), (1,)), ((), ())), preferred_element_type=jnp.float32
    )


def contract_cols(left, right):
    return lax.dot_general(
        left, right, (((0,), (0,)), ((), ())), preferred_element_type=jnp.float32
    )


def add_single(left, weight_piece):
    return jnp.dot(left, weight_piece, preferred_element_type=jnp.float32)


def back_rows(left, weight_piece):
    return contract_rows(left, weight_piece)


def weight_term(kept_acts, number):
    normed_one, grads_in, normed_two, grads_up, mixed_all, grads_attn, active_all, grads_ffn = (
        kept_acts
    )
    pieces = [
        contract_cols(normed_one, grads_in),
        contract_cols(normed_two, grads_up),
        contract_cols(mixed_all, grads_attn).reshape(number, -1),
        contract_cols(active_all, grads_ffn).reshape(number, -1),
    ]
    return jnp.concatenate(pieces, axis=1)


def body(
    tokens,
    cotangent,
    w_query,
    w_key,
    w_value,
    w_gate,
    w_out,
    w_up,
    w_down,
    norm_gains,
    norm_biases,
    block_deal,
    doc_lengths,
):
    ctx_size = lax.axis_size("ctx")
    tok_rows = tokens.shape[2]
    full_length = tok_rows * ctx_size
    model_width = tokens.shape[3]
    share_rows = model_width // lax.axis_size(("ctx", "fsdp"))
    grad_scale = float(MICRO * lax.axis_size("fsdp") * full_length) ** (-0.5)
    own_start = lax.axis_index("ctx") * tok_rows
    key_pos = stored_positions(block_deal, full_length, BLOCK)
    query_pos = lax.dynamic_slice_in_dim(key_pos, own_start, tok_rows)
    decay_log = jnp.log1p(-jnp.exp2(-5.0 - jnp.arange(HEADS).astype(jnp.float32)))
    scaling = DK ** (-0.5)
    out_list = []
    grad_list = []
    weight_sum = None
    gain_sum = jnp.zeros((2, model_width), jnp.float32)
    bias_sum = jnp.zeros((2, model_width), jnp.float32)
    for batch_index in range(MICRO):
        rows_in = tokens[batch_index, 0].astype(jnp.float32)
        grad_rows = cotangent[batch_index, 0].astype(jnp.float32)
        key_doc = document_ids(key_pos, doc_lengths[batch_index, 0])
        query_doc = lax.dynamic_slice_in_dim(key_doc, own_start, tok_rows)
        table = decay_table(query_pos, query_doc, key_pos, key_doc, decay_log, scaling)
        normed_one, norm_pull_one = jax.vjp(layer_norm, rows_in, norm_gains[0], norm_biases[0])
        low_one = normed_one.astype(jnp.bfloat16)
        pieces = (
            lax.all_gather(w_query, "fsdp", axis=0, tiled=True),
            lax.all_gather(w_key, "fsdp", axis=0, tiled=True),
            lax.all_gather(w_value, "fsdp", axis=0, tiled=True),
            lax.all_gather(w_gate, "fsdp", axis=0, tiled=True),
        )
        query_f, key_f, value_f, gate_pre = tuple(
            (
                jnp.dot(low_one, weight_piece, preferred_element_type=jnp.float32)
                for weight_piece in pieces
            )
        )
        query_low = query_f.astype(jnp.bfloat16)
        key_low = key_f.astype(jnp.bfloat16)
        value_low = value_f.astype(jnp.bfloat16)
        keys_all, values_all = (
            lax.all_gather(key_low, "ctx", axis=0, tiled=True),
            lax.all_gather(value_low, "ctx", axis=0, tiled=True),
        )
        query_heads = query_low.reshape(tok_rows, HEADS, DK)
        key_heads = keys_all.reshape(full_length, HEADS, DK)
        value_heads = values_all.reshape(full_length, HEADS, DV)
        scores = jnp.einsum(
            "thd,shd->hts", query_heads, key_heads, preferred_element_type=jnp.float32
        )
        attend = (scores * table).astype(jnp.bfloat16)
        retained = jnp.einsum(
            "hts,shd->thd", attend, value_heads, preferred_element_type=jnp.float32
        ).reshape(tok_rows, VW)
        mixed, mix_pull = jax.vjp(gated_mix, gate_pre, retained)
        mixed_low = mixed.astype(jnp.bfloat16)
        attn_out = add_single(mixed_low, lax.all_gather(w_out, "fsdp", axis=0, tiled=True))
        hidden = rows_in + attn_out
        normed_two, norm_pull_two = jax.vjp(layer_norm, hidden, norm_gains[1], norm_biases[1])
        low_two = normed_two.astype(jnp.bfloat16)
        up_pre = add_single(low_two, lax.all_gather(w_up, "fsdp", axis=0, tiled=True))
        active, act_pull = jax.vjp(smooth_act, up_pre)
        active_low = active.astype(jnp.bfloat16)
        ffn_out = add_single(active_low, lax.all_gather(w_down, "fsdp", axis=0, tiled=True))
        out_list.append((hidden + ffn_out).astype(jnp.bfloat16))
        grad_ffn = grad_rows.astype(jnp.bfloat16)
        grad_act = back_rows(grad_ffn, lax.all_gather(w_down, "fsdp", axis=0, tiled=True))
        grad_up = act_pull(grad_act)[0].astype(jnp.bfloat16)
        grad_norm_two = back_rows(grad_up, lax.all_gather(w_up, "fsdp", axis=0, tiled=True))
        grad_hidden_ln, grad_gain_two, grad_bias_two = norm_pull_two(grad_norm_two)
        grad_hidden = grad_rows + grad_hidden_ln
        grad_attn = grad_hidden.astype(jnp.bfloat16)
        grad_mixed = back_rows(grad_attn, lax.all_gather(w_out, "fsdp", axis=0, tiled=True))
        grad_gate_f, grad_ret_f = mix_pull(grad_mixed)
        grad_gate = grad_gate_f.astype(jnp.bfloat16)
        ret_low = grad_ret_f.astype(jnp.bfloat16)
        ret_heads = ret_low.reshape(tok_rows, HEADS, DV)
        grad_attend = jnp.einsum(
            "thd,shd->hts", ret_heads, value_heads, preferred_element_type=jnp.float32
        )
        grad_scores = (grad_attend * table).astype(jnp.bfloat16)
        grad_query = (
            jnp.einsum("hts,shd->thd", grad_scores, key_heads, preferred_element_type=jnp.float32)
            .reshape(tok_rows, QW)
            .astype(jnp.bfloat16)
        )
        key_part = jnp.einsum(
            "hts,thd->shd", grad_scores, query_heads, preferred_element_type=jnp.float32
        ).reshape(tok_rows * lax.axis_size("ctx"), QW)
        value_part = jnp.einsum(
            "hts,thd->shd", attend, ret_heads, preferred_element_type=jnp.float32
        ).reshape(tok_rows * lax.axis_size("ctx"), VW)
        key_value_sum = lax.psum_scatter(
            jnp.concatenate([key_part, value_part], axis=1).astype(jnp.bfloat16),
            "ctx",
            scatter_dimension=0,
            tiled=True,
        ).astype(jnp.float32)
        grad_key = key_value_sum[:, :QW].astype(jnp.bfloat16)
        grad_value = key_value_sum[:, QW:].astype(jnp.bfloat16)
        term_now = (
            contract_rows(grad_query, lax.all_gather(w_query, "fsdp", axis=0, tiled=True))
            + contract_rows(grad_key, lax.all_gather(w_key, "fsdp", axis=0, tiled=True))
            + contract_rows(grad_value, lax.all_gather(w_value, "fsdp", axis=0, tiled=True))
            + contract_rows(grad_gate, lax.all_gather(w_gate, "fsdp", axis=0, tiled=True))
        )
        grad_rows_ln, grad_gain_one, grad_bias_one = norm_pull_one(term_now)
        grad_list.append(grad_hidden + grad_rows_ln)
        gain_sum = gain_sum + jnp.stack([grad_gain_one, grad_gain_two])
        bias_sum = bias_sum + jnp.stack([grad_bias_one, grad_bias_two])
        kept_now = (
            low_one,
            jnp.concatenate([grad_query, grad_key, grad_value, grad_gate], axis=1),
            low_two,
            grad_up,
            mixed_low,
            grad_attn,
            active_low,
            grad_ffn,
        )
        term_sum = lax.psum_scatter(
            weight_term(kept_now, share_rows * lax.axis_size(("ctx", "fsdp"))),
            ("ctx", "fsdp"),
            scatter_dimension=0,
            tiled=True,
        )
        weight_sum = term_sum if weight_sum is None else weight_sum + term_sum
    weight_sum = weight_sum * grad_scale
    bounds = [QW, 2 * QW, 2 * QW + VW, 2 * QW + 2 * VW, 2 * QW + 2 * VW + FF, 2 * QW + 3 * VW + FF]
    g_query, g_key, g_value, g_gate, g_up, g_out_flat, g_down_flat = jnp.split(
        weight_sum, bounds, axis=1
    )
    g_out = g_out_flat.reshape(share_rows * (VW // model_width), model_width)
    g_down = g_down_flat.reshape(share_rows * (FF // model_width), model_width)
    gain_grads, bias_grads = (
        lax.psum_scatter(gain_sum, ("ctx", "fsdp"), scatter_dimension=1, tiled=True),
        lax.psum_scatter(bias_sum, ("ctx", "fsdp"), scatter_dimension=1, tiled=True),
    )
    gain_grads = gain_grads * grad_scale
    bias_grads = bias_grads * grad_scale
    output = jnp.stack(out_list)[:, None]
    grad_tokens = jnp.stack(grad_list)[:, None]
    return (
        output,
        grad_tokens,
        g_query,
        g_key,
        g_value,
        g_gate,
        g_out,
        g_up,
        g_down,
        gain_grads,
        bias_grads,
    )


def xy_swap(x, bit):
    return lax.ppermute(x, "fsdp", [(i, i ^ bit) for i in range(lax.axis_size("fsdp"))])


def core_swap(x):
    return lax.ppermute(x, "ctx", [(i, i ^ 1) for i in range(lax.axis_size("ctx"))])


def after(x, *earlier):
    return lax.optimization_barrier((x,) + tuple(earlier))[0]


def place(shape, items):
    arrays = []
    for item in items:
        if not any(item[0] is a for a in arrays):
            arrays.append(item[0])
    slots = [[item[0] is a for a in arrays].index(True) for item in items]
    kind = arrays[0].dtype

    def kernel(*refs):
        out = refs[len(arrays)]
        rank = lax.axis_index("fsdp")
        core = lax.axis_index("ctx") % 2
        for number, (array, start, rows, row, column) in enumerate(items):
            width = array.shape[1]
            step = min(rows, 64)
            source = refs[slots[number]]
            base = row(rank, core) if callable(row) else row

            def copy(first, width=width, step=step, source=source, base=base, start=start, rows=rows):
                def one(turn, carry):
                    place_in = pl.multiple_of(start + turn * step, step)
                    place_out = pl.multiple_of(base + turn * step, step)
                    out[pl.ds(place_out, step), first : first + width] = source[
                        pl.ds(place_in, step), :
                    ]
                    return carry

                lax.fori_loop(0, rows // step, one, 0)

            if callable(column):
                for which in range(2):
                    pl.when(core == which)(lambda which=which: copy(column(rank, which)))
            else:
                copy(column)

    size = shape[0] * shape[1] * jnp.dtype(kind).itemsize
    return pl.pallas_call(
        kernel,
        out_shape=jax.ShapeDtypeStruct(shape, kind),
        cost_estimate=pl.CostEstimate(flops=0, bytes_accessed=2 * size, transcendentals=0),
    )(*arrays)


def gather_first(x):
    return xy_swap(x, 1), xy_swap(x, 2)


def gather_second(first, second):
    half = first.shape[0] // 2
    return xy_swap(first[:half], 2), xy_swap(second[half:], 1)


def by_offset(x, first, second, low_part, high_part):
    rows, half = x.shape[0], x.shape[0] // 2
    return place(
        (4 * rows, x.shape[1]),
        [
            (x, 0, rows, 0, 0),
            (first, 0, rows, rows, 0),
            (low_part, 0, half, 2 * rows, 0),
            (high_part, 0, half, 2 * rows + half, 0),
            (second, 0, rows, 3 * rows, 0),
        ],
    )


def by_rank(x, first, second, low_part, high_part):
    rows, half = x.shape[0], x.shape[0] // 2
    return place(
        (4 * rows, x.shape[1]),
        [
            (x, 0, rows, lambda f, c: f * rows, 0),
            (first, 0, rows, lambda f, c: (f ^ 1) * rows, 0),
            (low_part, 0, half, lambda f, c: (f ^ 3) * rows, 0),
            (high_part, 0, half, lambda f, c: (f ^ 3) * rows + half, 0),
            (second, 0, rows, lambda f, c: (f ^ 2) * rows, 0),
        ],
    )


def plane_reduce_rows(part):
    rows, half = part.shape[0] // 4, part.shape[1] // 2
    wide = lambda v: v.astype(jnp.float32)
    left_in = xy_swap(part[rows : 3 * rows, :half], 1)
    right_in = xy_swap(part[2 * rows :, half:], 2)
    left_far = wide(part[3 * rows :, :half]) + wide(left_in[rows:])
    right_far = wide(part[rows : 2 * rows, half:]) + wide(right_in[:rows])
    left_last = xy_swap(left_far.astype(jnp.bfloat16), 2)
    right_last = xy_swap(right_far.astype(jnp.bfloat16), 1)
    left = wide(part[:rows, :half]) + wide(left_in[:rows]) + wide(left_last)
    right = wide(part[:rows, half:]) + wide(right_in[rows:]) + wide(right_last)
    return jnp.concatenate([left, right], axis=1)


def plane_reduce(blocks):
    half = blocks[0].shape[-1] // 2
    left = [b[..., :half] for b in blocks]
    right = [b[..., half:] for b in blocks]
    left_in = xy_swap(jnp.stack([left[1], left[3]]), 1).astype(jnp.float32)
    right_in = xy_swap(jnp.stack([right[2], right[3]]), 2).astype(jnp.float32)
    left_far = left[2].astype(jnp.float32) + left_in[1]
    right_far = right[1].astype(jnp.float32) + right_in[1]
    left_last = xy_swap(left_far.astype(jnp.bfloat16), 2).astype(jnp.float32)
    right_last = xy_swap(right_far.astype(jnp.bfloat16), 1).astype(jnp.float32)
    left_own = left[0].astype(jnp.float32) + left_in[0]
    right_own = right[0].astype(jnp.float32) + right_in[0]
    return jnp.concatenate([left_own + left_last, right_own + right_last], axis=-1)


def sum_everywhere(x):
    for axis in ("ctx", "fsdp"):
        size = lax.axis_size(axis)
        bit = 1
        while bit < size:
            x = x + lax.ppermute(x, axis, [(i, i ^ bit) for i in range(size)])
            bit *= 2
    return x


def in_rank_order(blocks, rank):
    odd = (rank % 2) == 1
    upper = (rank // 2) == 1
    one = [
        jnp.where(odd, blocks[1], blocks[0]),
        jnp.where(odd, blocks[0], blocks[1]),
        jnp.where(odd, blocks[3], blocks[2]),
        jnp.where(odd, blocks[2], blocks[3]),
    ]
    return [
        jnp.where(upper, one[2], one[0]),
        jnp.where(upper, one[3], one[1]),
        jnp.where(upper, one[0], one[2]),
        jnp.where(upper, one[1], one[3]),
    ]


def pick(x, index, size, axis):
    return lax.dynamic_slice_in_dim(x, index * size, size, axis)


def head_columns(w_query, w_key, w_value, w_gate, ctx_rank):
    return jnp.concatenate(
        [
            pick(w_query, ctx_rank, DK, 1),
            pick(w_key, ctx_rank, DK, 1),
            pick(w_value, ctx_rank, DV, 1),
            pick(w_gate, ctx_rank, DV, 1),
        ],
        axis=1,
    )


def out_pieces(w_out, ctx_rank, fsdp_rank, fsdp_size):
    rows = DV // fsdp_size
    start = (ctx_rank % 2) * DV
    return [
        lax.dynamic_slice_in_dim(w_out, start + (fsdp_rank ^ bit) * rows, rows, 0)
        for bit in range(fsdp_size)
    ]


def scatter_quarters(cuts, ctx_size, fsdp_size):
    parts = [cuts[0]]
    for bit in range(1, fsdp_size):
        pairs = [
            (c * fsdp_size + c // 2, c * fsdp_size + ((c // 2) ^ bit)) for c in range(ctx_size)
        ]
        parts.append(lax.ppermute(cuts[bit], ("ctx", "fsdp"), pairs))
    return parts


def choose_quarter(parts, ctx_rank, fsdp_rank):
    quarter = parts[0]
    for bit in range(1, len(parts)):
        quarter = jnp.where((fsdp_rank ^ (ctx_rank // 2)) == bit, parts[bit], quarter)
    return quarter


def copy_block(target, row, column, source, row_in, column_in, rows, width):
    step = min(rows, 64)

    def one(turn, carry):
        place_in = pl.multiple_of(row_in + turn * step, step)
        place_out = pl.multiple_of(row + turn * step, step)
        taken = source[pl.ds(place_in, step), pl.ds(column_in, width)]
        target[pl.ds(place_out, step), pl.ds(column, width)] = taken
        return carry

    lax.fori_loop(0, rows // step, one, 0)


def cut_ffn(w_up, w_down):
    ctx_size, fsdp_size = lax.axis_size("ctx"), lax.axis_size("fsdp")
    rows, width = w_up.shape[0], w_down.shape[1]
    unit, half = FF // (ctx_size * fsdp_size), ctx_size // 2
    wide = half * unit
    fourth = width // 4

    def kernel(up, down, *outs):
        rank = lax.axis_index("fsdp")
        core = lax.axis_index("ctx") % 2
        for number in range(fsdp_size - 1):
            other = rank ^ (number + 1)
            for i in range(half):
                column = pl.multiple_of(((core * half + i) * fsdp_size + other) * unit, unit)
                copy_block(outs[number], 0, i * unit, up, 0, column, rows, unit)
            for i in range(2):
                for q in range(2):
                    column = pl.multiple_of(core * 2 * fourth + q * fourth, fourth)
                    row = (i * fsdp_size + other) * unit
                    copy_block(
                        outs[number], (2 * i + q) * unit, wide, down, row, column, unit, fourth
                    )

    kind = jax.ShapeDtypeStruct((rows, wide + fourth), w_up.dtype)
    return list(pl.pallas_call(kernel, out_shape=[kind] * (fsdp_size - 1))(w_up, w_down))


def join_ffn(w_up, w_down, mine, other):
    ctx_size, fsdp_size = lax.axis_size("ctx"), lax.axis_size("fsdp")
    rows, width = w_up.shape[0], w_down.shape[1]
    unit, half = FF // (ctx_size * fsdp_size), ctx_size // 2
    wide = half * unit
    fourth = width // 4

    def kernel(up, down, *refs):
        up_out, down_out = refs[2 * len(mine) :]
        rank = lax.axis_index("fsdp")
        core = lax.axis_index("ctx") % 2
        for i in range(ctx_size):
            column = pl.multiple_of((i * fsdp_size + rank) * unit, unit)
            copy_block(up_out, rank * rows, i * unit, up, 0, column, rows, unit)
        for i in range(2):
            copy_block(
                down_out, (2 * rank + i) * unit, 0, down, (i * fsdp_size + rank) * unit, 0, unit, width
            )
        for number in range(2 * len(mine)):
            source = rank ^ (number % len(mine) + 1)
            part = core if number < len(mine) else 1 - core
            column = pl.multiple_of(part * wide, wide)
            copy_block(up_out, source * rows, column, refs[number], 0, 0, rows, wide)
            for i in range(2):
                for q in range(2):
                    column = pl.multiple_of(part * 2 * fourth + q * fourth, fourth)
                    row = (2 * source + i) * unit
                    copy_block(
                        down_out, row, column, refs[number], (2 * i + q) * unit, wide, unit, fourth
                    )

    shapes = [
        jax.ShapeDtypeStruct((fsdp_size * rows, FF // fsdp_size), w_up.dtype),
        jax.ShapeDtypeStruct((FF // fsdp_size, width), w_up.dtype),
    ]
    return pl.pallas_call(kernel, out_shape=shapes)(w_up, w_down, *mine, *other)


def smooth_parts(values):
    share = 0.5 + 0.5 * lax.erf(values * (0.5**0.5))
    density = jnp.exp(-0.5 * values * values) * ((0.5 / jnp.pi) ** 0.5)
    return values * share, share + values * density


def one_table(pos, doc, rate, scaling):
    keeping = (pos[:, None] >= pos[None, :]) & (doc[:, None] == doc[None, :])
    spacing = jnp.where(keeping, (pos[:, None] - pos[None, :]).astype(jnp.float32), 0.0)
    return jnp.where(keeping, jnp.exp(rate * spacing) * scaling, 0.0)


def ctx_sum(x):
    return lax.psum_scatter(x, "ctx", scatter_dimension=0, tiled=True)


def body_heads(
    tokens,
    cotangent,
    w_query,
    w_key,
    w_value,
    w_gate,
    w_out,
    w_up,
    w_down,
    norm_gains,
    norm_biases,
    block_deal,
    doc_lengths,
):
    low = jnp.bfloat16
    ctx_size = lax.axis_size("ctx")
    fsdp_size = lax.axis_size("fsdp")
    tok_rows = tokens.shape[2]
    full_length = tok_rows * ctx_size
    width = tokens.shape[3]
    share = width // (ctx_size * fsdp_size)
    grad_scale = float(MICRO * fsdp_size * full_length) ** (-0.5)
    ctx_rank = lax.axis_index("ctx")
    fsdp_rank = lax.axis_index("fsdp")
    pos = stored_positions(block_deal, full_length, BLOCK)
    rate = jnp.log1p(-jnp.exp2(-5.0 - ctx_rank.astype(jnp.float32)))
    scaling = DK ** (-0.5)

    own_in = head_columns(w_query, w_key, w_value, w_gate, ctx_rank)
    tokens = after(tokens, own_in)
    rows_in = []
    norm_one = []
    x_own = []
    for m in range(MICRO):
        rows_in.append(after(tokens[m, 0], *x_own[-1:]).astype(jnp.float32))
        norm_one.append(jax.vjp(layer_norm, rows_in[m], norm_gains[0], norm_biases[0]))
        x_own.append(norm_one[m][0].astype(low))
    grad_rows = [cotangent[m, 0].astype(jnp.float32) for m in range(MICRO)]
    x_all = [lax.all_gather(x, "ctx", axis=0, tiled=True) for x in x_own]
    in_first = gather_first(own_in)
    ffn_cut = cut_ffn(w_up, w_down)
    out_cut = out_pieces(w_out, ctx_rank, fsdp_rank, fsdp_size)
    in_first = lax.optimization_barrier(tuple(in_first) + tuple(ffn_cut) + tuple(out_cut))[:2]
    in_second = gather_second(*in_first)
    w_in = by_rank(own_in, *in_first, *in_second)
    out_cut = lax.optimization_barrier(tuple(out_cut) + tuple(in_first))[: len(out_cut)]
    out_parts = scatter_quarters(out_cut, ctx_size, fsdp_size)

    def mix(m, x_now, *earlier):
        doc = document_ids(pos, doc_lengths[m, 0])
        table = one_table(pos, doc, rate, scaling)
        joint = jnp.dot(x_now, w_in[:, : 2 * DK + DV], preferred_element_type=jnp.float32).astype(low)
        joint = after(joint, *earlier)
        gate_pre = jnp.dot(x_now, w_in[:, 2 * DK + DV :], preferred_element_type=jnp.float32)
        query, key, value = joint[:, :DK], joint[:, DK : 2 * DK], joint[:, 2 * DK :]
        attend = (contract_rows(query, key) * table).astype(low)
        retained = add_single(attend, value)
        mixed, mix_pull = jax.vjp(gated_mix, gate_pre, retained)
        return table, query, key, value, attend, mix_pull, mixed.astype(low)

    kept = [mix(0, x_all[0])]
    out_parts = lax.optimization_barrier(tuple(out_parts) + (kept[0][6],))[:-1]
    quarter = choose_quarter(out_parts, ctx_rank, fsdp_rank)
    out_first = gather_first(quarter)
    out_second = gather_second(*out_first)
    w_head = by_rank(quarter, *out_first, *out_second)
    cot_own = after(cotangent.reshape(MICRO * tok_rows, width), *out_first)
    cot_first = gather_first(cot_own)
    ffn_cut = lax.optimization_barrier(tuple(ffn_cut) + tuple(out_second))[: len(ffn_cut)]
    ffn_mine = [xy_swap(ffn_cut[bit - 1], bit) for bit in range(1, fsdp_size)]
    part = add_single(kept[0][6], w_head).astype(low)
    attn_out = [ctx_sum(after(part, *x_all[1:]))]
    for m in range(1, MICRO):
        kept.append(mix(m, after(x_all[m], *out_parts), *cot_first))
        part = add_single(kept[m][6], w_head).astype(low)
        attn_out.append(ctx_sum(after(part, *ffn_mine)))
    cot_second = gather_second(*cot_first)
    up_own, down_own = join_ffn(w_up, w_down, ffn_mine, [core_swap(x) for x in ffn_mine])
    cot_all = [
        place(
            (fsdp_size * tok_rows, width),
            [
                (cot_own, m * tok_rows, tok_rows, 0, 0),
                (cot_first[0], m * tok_rows, tok_rows, tok_rows, 0),
                (cot_second[m], 0, tok_rows, 2 * tok_rows, 0),
                (cot_first[1], m * tok_rows, tok_rows, 3 * tok_rows, 0),
            ],
        )
        for m in range(MICRO)
    ]

    outs = [None] * MICRO
    grad_attn = []
    grad_hidden = []
    ffn_kept = []
    norm_two_terms = []
    norm_part = None
    for m in range(MICRO):
        if m > 0:
            attn_out[m] = after(attn_out[m], norm_part)
        hidden = rows_in[m] + attn_out[m].astype(jnp.float32)
        normed_two, pull_two = jax.vjp(layer_norm, hidden, norm_gains[1], norm_biases[1])
        two_own = normed_two.astype(low)
        two_first = gather_first(two_own)
        two_second = gather_second(*two_first)
        two_own = after(two_own, up_own, down_own, cot_all[m])
        two_all = by_offset(two_own, *two_first, *two_second)
        active, slope = smooth_parts(add_single(two_all, up_own))
        active_low, slope = lax.optimization_barrier((active.astype(low), slope))
        grad_up = (back_rows(cot_all[m], down_own) * slope).astype(low)
        norm_part = back_rows(grad_up, up_own).astype(low)
        grad_norm_two = after(plane_reduce_rows(norm_part), *grad_attn[-1:])
        grad_ln, gain_two, bias_two = pull_two(grad_norm_two)
        norm_two_terms.append((gain_two, bias_two))
        total = grad_rows[m] + grad_ln
        grad_hidden.append(total)
        grad_attn.append(total.astype(low))
        ffn_kept.append((two_all, grad_up, active_low, hidden))

    grad_all = [lax.all_gather(grad_attn[m], "ctx", axis=0, tiled=True) for m in range(MICRO)]

    def unmix(m, grad_now):
        table, query, key, value, attend, mix_pull, mixed_low = kept[m]
        grad_mixed = back_rows(grad_now, w_head)
        grad_gate, grad_ret = mix_pull(grad_mixed)
        ret_low = grad_ret.astype(low)
        grad_scores = (contract_rows(ret_low, value) * table).astype(low)
        grad_query = add_single(grad_scores, key).astype(low)
        grad_key = contract_cols(grad_scores, query).astype(low)
        grad_value = contract_cols(attend, ret_low).astype(low)
        return jnp.concatenate([grad_query, grad_key, grad_value, grad_gate.astype(low)], axis=1)

    terms = []
    in_term = None
    out_term = None
    sums = []
    fill = ()
    for m in range(MICRO):
        grad_now = after(grad_all[m], *(grad_attn[1:] if m == 0 else terms[-1:]), *fill)
        grad_in = unmix(m, grad_now)
        part = back_rows(grad_in, w_in).astype(low)
        terms.append(part)
        sums.append(ctx_sum(after(part, *grad_all[m + 1 :], *sums[-1:])))
        x_now, mixed_now, grad_in = lax.optimization_barrier(
            (x_all[m], kept[m][6], grad_in, part) + tuple(v for v in outs if v is not None)
        )[:3]
        in_now = contract_cols(x_now, grad_in)
        out_now = contract_cols(mixed_now, grad_all[m])
        in_term = in_now if m == 0 else (in_term + in_now).astype(low)
        out_term = out_now if m == 0 else (out_term + out_now).astype(low)
        if m == 0:
            ready = [after(ffn_kept[n][2], part, grad_attn[n]) for n in range(MICRO)]
            fill = tuple(add_single(ready[n], down_own).astype(low) for n in range(MICRO))
            for n in range(MICRO):
                outs[n] = (ffn_kept[n][3] + plane_reduce_rows(fill[n])).astype(low)
            up_grad = sum(contract_cols(k[0], after(k[1], part)) for k in ffn_kept).astype(low)
            down_grad = sum(contract_cols(ready[n], cot_all[n]) for n in range(MICRO)).astype(low)
            sums[m] = after(sums[m], in_term, out_term)
        else:
            sums[m] = after(sums[m], in_term, out_term, up_grad, down_grad)
    up_sum = ctx_sum(after(up_grad, sums[-1]))
    down_sum = ctx_sum(after(down_grad, sums[-1]))

    grad_tokens = []
    norm_one_terms = []
    for m in range(MICRO):
        grad_ln, gain_one, bias_one = norm_one[m][1](sums[m].astype(jnp.float32))
        norm_one_terms.append((gain_one, bias_one))
        grad_tokens.append(grad_hidden[m] + grad_ln)

    gain_rows = [sum(t[0] for t in norm_one_terms), sum(t[0] for t in norm_two_terms)]
    bias_rows = [sum(t[1] for t in norm_one_terms), sum(t[1] for t in norm_two_terms)]
    norm_sums = sum_everywhere(jnp.stack(gain_rows + bias_rows))
    in_view = in_term.reshape(ctx_size, fsdp_size, share, -1)
    in_sum = plane_reduce([pick(in_view, fsdp_rank ^ j, 1, 1)[:, 0] for j in range(fsdp_size)])
    in_mine = lax.all_to_all(after(in_sum.astype(low), norm_sums), "ctx", split_axis=0, concat_axis=0, tiled=True)
    out_term = after(out_term, in_sum)
    rows = DV // fsdp_size
    g_out = plane_reduce([pick(out_term, fsdp_rank ^ j, rows, 0) for j in range(fsdp_size)])

    def by_head(first, size):
        part = in_mine[:, :, first : first + size].transpose(1, 0, 2)
        return part.reshape(share, -1).astype(jnp.float32) * grad_scale

    g_query = by_head(0, DK)
    g_key = by_head(DK, DK)
    g_value = by_head(2 * DK, DV)
    g_gate = by_head(2 * DK + DV, DV)

    up_view = up_sum.reshape(fsdp_size, share, -1)
    pieces = [lax.dynamic_index_in_dim(up_view, fsdp_rank, 0, keepdims=False)]
    for bit in range(1, fsdp_size):
        pieces.append(
            xy_swap(lax.dynamic_index_in_dim(up_view, fsdp_rank ^ bit, 0, keepdims=False), bit)
        )
    pieces = [p.reshape(share, ctx_size, -1) for p in in_rank_order(pieces, fsdp_rank)]
    g_up = jnp.stack(pieces, axis=2).reshape(share, FF).astype(jnp.float32) * grad_scale

    norm_sums = pick(norm_sums, ctx_rank * fsdp_size + fsdp_rank, share, 1) * grad_scale
    return (
        jnp.stack(outs)[:, None],
        jnp.stack(grad_tokens)[:, None],
        g_query,
        g_key,
        g_value,
        g_gate,
        g_out * grad_scale,
        g_up,
        down_sum.astype(jnp.float32) * grad_scale,
        norm_sums[:2],
        norm_sums[2:],
    )


def solution(mesh):
    in_specs = (
        P(None, "fsdp", "ctx", None),
        P(None, "fsdp", "ctx", None),
        P("fsdp", None),
        P("fsdp", None),
        P("fsdp", None),
        P("fsdp", None),
        P("fsdp", None),
        P("fsdp", None),
        P("fsdp", None),
        P(),
        P(),
        P(),
        P(None, "fsdp", None),
    )
    out_specs = (
        P(None, "fsdp", "ctx", None),
        P(None, "fsdp", "ctx", None),
        P(("ctx", "fsdp"), None),
        P(("ctx", "fsdp"), None),
        P(("ctx", "fsdp"), None),
        P(("ctx", "fsdp"), None),
        P(("ctx", "fsdp"), None),
        P(("ctx", "fsdp"), None),
        P(("ctx", "fsdp"), None),
        P(None, ("ctx", "fsdp")),
        P(None, ("ctx", "fsdp")),
    )
    by_heads = mesh.shape["ctx"] == HEADS and mesh.shape["fsdp"] == 4
    chosen = body_heads if by_heads else body
    return jax.shard_map(chosen, mesh=mesh, in_specs=in_specs, out_specs=out_specs, check_vma=False)
```

```python
import jax
import jax.numpy as jnp
from jax import lax
from jax.experimental import pallas as pl
from jax.sharding import PartitionSpec as P

HEADS = 8
DK = 256
DV = 512
FF = 4096
MICRO = 2
QW = 2048
VW = 4096
BLOCK = 64


epsilon = 1e-05
group_floor = 1.0


def layer_norm(values, gain_row, offset):
    center = jnp.mean(values, axis=-1, keepdims=True)
    centred = values - center
    spread = jnp.mean(centred * centred, axis=-1, keepdims=True)
    return centred * lax.rsqrt(spread + epsilon) * gain_row + offset


def gated_mix(gate_pre, retained):
    number = retained.shape[0]
    grouped = retained.reshape(number, -1, DV)
    center = jnp.mean(grouped, axis=-1, keepdims=True)
    centred = grouped - center
    spread = jnp.mean(centred * centred, axis=-1, keepdims=True)
    normed = (centred * lax.rsqrt(spread + group_floor)).reshape(number, -1)
    return jax.nn.silu(gate_pre) * normed


def smooth_act(values):
    return jax.nn.gelu(values, approximate=False)


def stored_positions(block_deal, full_length, block_size):
    stored = jnp.arange(full_length, dtype=jnp.int32)
    block_ids = stored // block_size
    slots_all = jnp.arange(block_deal.shape[0], dtype=jnp.int32)
    picked = jnp.sum(
        jnp.where(block_ids[:, None] == slots_all[None, :], block_deal[None, :], 0),
        axis=1,
        dtype=jnp.int32,
    )
    return picked * block_size + stored % block_size


def document_ids(positions, doc_sizes):
    starts = jnp.cumsum(doc_sizes, dtype=jnp.int32) - doc_sizes
    return (
        jnp.sum((positions[:, None] >= starts[None, :]).astype(jnp.int32), axis=1, dtype=jnp.int32)
        - 1
    )


def decay_table(query_pos, query_doc, key_pos, key_doc, decay_log, scaling):
    keeping = (query_pos[:, None] >= key_pos[None, :]) & (query_doc[:, None] == key_doc[None, :])
    spacing = jnp.where(keeping, (query_pos[:, None] - key_pos[None, :]).astype(jnp.float32), 0.0)
    factor = jnp.exp(decay_log[:, None, None] * spacing[None])
    return jnp.where(keeping[None], factor * scaling, 0.0)


def contract_rows(left, right):
    return lax.dot_general(
        left, right, (((1,), (1,)), ((), ())), preferred_element_type=jnp.float32
    )


def contract_cols(left, right):
    return lax.dot_general(
        left, right, (((0,), (0,)), ((), ())), preferred_element_type=jnp.float32
    )


def add_single(left, weight_piece):
    return jnp.dot(left, weight_piece, preferred_element_type=jnp.float32)


def back_rows(left, weight_piece):
    return contract_rows(left, weight_piece)


def weight_term(kept_acts, number):
    normed_one, grads_in, normed_two, grads_up, mixed_all, grads_attn, active_all, grads_ffn = (
        kept_acts
    )
    pieces = [
        contract_cols(normed_one, grads_in),
        contract_cols(normed_two, grads_up),
        contract_cols(mixed_all, grads_attn).reshape(number, -1),
        contract_cols(active_all, grads_ffn).reshape(number, -1),
    ]
    return jnp.concatenate(pieces, axis=1)


def body(
    tokens,
    cotangent,
    w_query,
    w_key,
    w_value,
    w_gate,
    w_out,
    w_up,
    w_down,
    norm_gains,
    norm_biases,
    block_deal,
    doc_lengths,
):
    ctx_size = lax.axis_size("ctx")
    tok_rows = tokens.shape[2]
    full_length = tok_rows * ctx_size
    model_width = tokens.shape[3]
    share_rows = model_width // lax.axis_size(("ctx", "fsdp"))
    grad_scale = float(MICRO * lax.axis_size("fsdp") * full_length) ** (-0.5)
    own_start = lax.axis_index("ctx") * tok_rows
    key_pos = stored_positions(block_deal, full_length, BLOCK)
    query_pos = lax.dynamic_slice_in_dim(key_pos, own_start, tok_rows)
    decay_log = jnp.log1p(-jnp.exp2(-5.0 - jnp.arange(HEADS).astype(jnp.float32)))
    scaling = DK ** (-0.5)
    out_list = []
    grad_list = []
    weight_sum = None
    gain_sum = jnp.zeros((2, model_width), jnp.float32)
    bias_sum = jnp.zeros((2, model_width), jnp.float32)
    for batch_index in range(MICRO):
        rows_in = tokens[batch_index, 0].astype(jnp.float32)
        grad_rows = cotangent[batch_index, 0].astype(jnp.float32)
        key_doc = document_ids(key_pos, doc_lengths[batch_index, 0])
        query_doc = lax.dynamic_slice_in_dim(key_doc, own_start, tok_rows)
        table = decay_table(query_pos, query_doc, key_pos, key_doc, decay_log, scaling)
        normed_one, norm_pull_one = jax.vjp(layer_norm, rows_in, norm_gains[0], norm_biases[0])
        low_one = normed_one.astype(jnp.bfloat16)
        pieces = (
            lax.all_gather(w_query, "fsdp", axis=0, tiled=True),
            lax.all_gather(w_key, "fsdp", axis=0, tiled=True),
            lax.all_gather(w_value, "fsdp", axis=0, tiled=True),
            lax.all_gather(w_gate, "fsdp", axis=0, tiled=True),
        )
        query_f, key_f, value_f, gate_pre = tuple(
            (
                jnp.dot(low_one, weight_piece, preferred_element_type=jnp.float32)
                for weight_piece in pieces
            )
        )
        query_low = query_f.astype(jnp.bfloat16)
        key_low = key_f.astype(jnp.bfloat16)
        value_low = value_f.astype(jnp.bfloat16)
        keys_all, values_all = (
            lax.all_gather(key_low, "ctx", axis=0, tiled=True),
            lax.all_gather(value_low, "ctx", axis=0, tiled=True),
        )
        query_heads = query_low.reshape(tok_rows, HEADS, DK)
        key_heads = keys_all.reshape(full_length, HEADS, DK)
        value_heads = values_all.reshape(full_length, HEADS, DV)
        scores = jnp.einsum(
            "thd,shd->hts", query_heads, key_heads, preferred_element_type=jnp.float32
        )
        attend = (scores * table).astype(jnp.bfloat16)
        retained = jnp.einsum(
            "hts,shd->thd", attend, value_heads, preferred_element_type=jnp.float32
        ).reshape(tok_rows, VW)
        mixed, mix_pull = jax.vjp(gated_mix, gate_pre, retained)
        mixed_low = mixed.astype(jnp.bfloat16)
        attn_out = add_single(mixed_low, lax.all_gather(w_out, "fsdp", axis=0, tiled=True))
        hidden = rows_in + attn_out
        normed_two, norm_pull_two = jax.vjp(layer_norm, hidden, norm_gains[1], norm_biases[1])
        low_two = normed_two.astype(jnp.bfloat16)
        up_pre = add_single(low_two, lax.all_gather(w_up, "fsdp", axis=0, tiled=True))
        active, act_pull = jax.vjp(smooth_act, up_pre)
        active_low = active.astype(jnp.bfloat16)
        ffn_out = add_single(active_low, lax.all_gather(w_down, "fsdp", axis=0, tiled=True))
        out_list.append((hidden + ffn_out).astype(jnp.bfloat16))
        grad_ffn = grad_rows.astype(jnp.bfloat16)
        grad_act = back_rows(grad_ffn, lax.all_gather(w_down, "fsdp", axis=0, tiled=True))
        grad_up = act_pull(grad_act)[0].astype(jnp.bfloat16)
        grad_norm_two = back_rows(grad_up, lax.all_gather(w_up, "fsdp", axis=0, tiled=True))
        grad_hidden_ln, grad_gain_two, grad_bias_two = norm_pull_two(grad_norm_two)
        grad_hidden = grad_rows + grad_hidden_ln
        grad_attn = grad_hidden.astype(jnp.bfloat16)
        grad_mixed = back_rows(grad_attn, lax.all_gather(w_out, "fsdp", axis=0, tiled=True))
        grad_gate_f, grad_ret_f = mix_pull(grad_mixed)
        grad_gate = grad_gate_f.astype(jnp.bfloat16)
        ret_low = grad_ret_f.astype(jnp.bfloat16)
        ret_heads = ret_low.reshape(tok_rows, HEADS, DV)
        grad_attend = jnp.einsum(
            "thd,shd->hts", ret_heads, value_heads, preferred_element_type=jnp.float32
        )
        grad_scores = (grad_attend * table).astype(jnp.bfloat16)
        grad_query = (
            jnp.einsum("hts,shd->thd", grad_scores, key_heads, preferred_element_type=jnp.float32)
            .reshape(tok_rows, QW)
            .astype(jnp.bfloat16)
        )
        key_part = jnp.einsum(
            "hts,thd->shd", grad_scores, query_heads, preferred_element_type=jnp.float32
        ).reshape(tok_rows * lax.axis_size("ctx"), QW)
        value_part = jnp.einsum(
            "hts,thd->shd", attend, ret_heads, preferred_element_type=jnp.float32
        ).reshape(tok_rows * lax.axis_size("ctx"), VW)
        key_value_sum = lax.psum_scatter(
            jnp.concatenate([key_part, value_part], axis=1).astype(jnp.bfloat16),
            "ctx",
            scatter_dimension=0,
            tiled=True,
        ).astype(jnp.float32)
        grad_key = key_value_sum[:, :QW].astype(jnp.bfloat16)
        grad_value = key_value_sum[:, QW:].astype(jnp.bfloat16)
        term_now = (
            contract_rows(grad_query, lax.all_gather(w_query, "fsdp", axis=0, tiled=True))
            + contract_rows(grad_key, lax.all_gather(w_key, "fsdp", axis=0, tiled=True))
            + contract_rows(grad_value, lax.all_gather(w_value, "fsdp", axis=0, tiled=True))
            + contract_rows(grad_gate, lax.all_gather(w_gate, "fsdp", axis=0, tiled=True))
        )
        grad_rows_ln, grad_gain_one, grad_bias_one = norm_pull_one(term_now)
        grad_list.append(grad_hidden + grad_rows_ln)
        gain_sum = gain_sum + jnp.stack([grad_gain_one, grad_gain_two])
        bias_sum = bias_sum + jnp.stack([grad_bias_one, grad_bias_two])
        kept_now = (
            low_one,
            jnp.concatenate([grad_query, grad_key, grad_value, grad_gate], axis=1),
            low_two,
            grad_up,
            mixed_low,
            grad_attn,
            active_low,
            grad_ffn,
        )
        term_sum = lax.psum_scatter(
            weight_term(kept_now, share_rows * lax.axis_size(("ctx", "fsdp"))),
            ("ctx", "fsdp"),
            scatter_dimension=0,
            tiled=True,
        )
        weight_sum = term_sum if weight_sum is None else weight_sum + term_sum
    weight_sum = weight_sum * grad_scale
    bounds = [QW, 2 * QW, 2 * QW + VW, 2 * QW + 2 * VW, 2 * QW + 2 * VW + FF, 2 * QW + 3 * VW + FF]
    g_query, g_key, g_value, g_gate, g_up, g_out_flat, g_down_flat = jnp.split(
        weight_sum, bounds, axis=1
    )
    g_out = g_out_flat.reshape(share_rows * (VW // model_width), model_width)
    g_down = g_down_flat.reshape(share_rows * (FF // model_width), model_width)
    gain_grads, bias_grads = (
        lax.psum_scatter(gain_sum, ("ctx", "fsdp"), scatter_dimension=1, tiled=True),
        lax.psum_scatter(bias_sum, ("ctx", "fsdp"), scatter_dimension=1, tiled=True),
    )
    gain_grads = gain_grads * grad_scale
    bias_grads = bias_grads * grad_scale
    output = jnp.stack(out_list)[:, None]
    grad_tokens = jnp.stack(grad_list)[:, None]
    return (
        output,
        grad_tokens,
        g_query,
        g_key,
        g_value,
        g_gate,
        g_out,
        g_up,
        g_down,
        gain_grads,
        bias_grads,
    )


def xy_swap(x, bit):
    return lax.ppermute(x, "fsdp", [(i, i ^ bit) for i in range(lax.axis_size("fsdp"))])


def core_swap(x):
    return lax.ppermute(x, "ctx", [(i, i ^ 1) for i in range(lax.axis_size("ctx"))])


def after(x, *earlier):
    return lax.optimization_barrier((x,) + tuple(earlier))[0]


def place(shape, items):
    arrays = []
    for item in items:
        if not any(item[0] is a for a in arrays):
            arrays.append(item[0])
    slots = [[item[0] is a for a in arrays].index(True) for item in items]
    kind = arrays[0].dtype

    def kernel(*refs):
        out = refs[len(arrays)]
        rank = lax.axis_index("fsdp")
        core = lax.axis_index("ctx") % 2
        for number, (array, start, rows, row, column) in enumerate(items):
            width = array.shape[1]
            step = min(rows, 64)
            source = refs[slots[number]]
            base = row(rank, core) if callable(row) else row

            def copy(first, width=width, step=step, source=source, base=base, start=start, rows=rows):
                def one(turn, carry):
                    place_in = pl.multiple_of(start + turn * step, step)
                    place_out = pl.multiple_of(base + turn * step, step)
                    out[pl.ds(place_out, step), first : first + width] = source[
                        pl.ds(place_in, step), :
                    ]
                    return carry

                lax.fori_loop(0, rows // step, one, 0)

            if callable(column):
                for which in range(2):
                    pl.when(core == which)(lambda which=which: copy(column(rank, which)))
            else:
                copy(column)

    size = shape[0] * shape[1] * jnp.dtype(kind).itemsize
    return pl.pallas_call(
        kernel,
        out_shape=jax.ShapeDtypeStruct(shape, kind),
        cost_estimate=pl.CostEstimate(flops=0, bytes_accessed=2 * size, transcendentals=0),
    )(*arrays)


def gather_first(x):
    return xy_swap(x, 1), xy_swap(x, 2)


def gather_second(first, second):
    half = first.shape[0] // 2
    return xy_swap(first[:half], 2), xy_swap(second[half:], 1)


def by_offset(x, first, second, low_part, high_part):
    rows, half = x.shape[0], x.shape[0] // 2
    return place(
        (4 * rows, x.shape[1]),
        [
            (x, 0, rows, 0, 0),
            (first, 0, rows, rows, 0),
            (low_part, 0, half, 2 * rows, 0),
            (high_part, 0, half, 2 * rows + half, 0),
            (second, 0, rows, 3 * rows, 0),
        ],
    )


def by_rank(x, first, second, low_part, high_part):
    rows, half = x.shape[0], x.shape[0] // 2
    return place(
        (4 * rows, x.shape[1]),
        [
            (x, 0, rows, lambda f, c: f * rows, 0),
            (first, 0, rows, lambda f, c: (f ^ 1) * rows, 0),
            (low_part, 0, half, lambda f, c: (f ^ 3) * rows, 0),
            (high_part, 0, half, lambda f, c: (f ^ 3) * rows + half, 0),
            (second, 0, rows, lambda f, c: (f ^ 2) * rows, 0),
        ],
    )


def plane_reduce_rows(part):
    rows, half = part.shape[0] // 4, part.shape[1] // 2
    wide = lambda v: v.astype(jnp.float32)
    left_in = xy_swap(part[rows : 3 * rows, :half], 1)
    right_in = xy_swap(part[2 * rows :, half:], 2)
    left_far = wide(part[3 * rows :, :half]) + wide(left_in[rows:])
    right_far = wide(part[rows : 2 * rows, half:]) + wide(right_in[:rows])
    left_last = xy_swap(left_far.astype(jnp.bfloat16), 2)
    right_last = xy_swap(right_far.astype(jnp.bfloat16), 1)
    left = wide(part[:rows, :half]) + wide(left_in[:rows]) + wide(left_last)
    right = wide(part[:rows, half:]) + wide(right_in[rows:]) + wide(right_last)
    return jnp.concatenate([left, right], axis=1)


def reduce_first(blocks):
    half = blocks[0].shape[-1] // 2
    left_in = xy_swap(jnp.stack([blocks[1][..., :half], blocks[3][..., :half]]), 1)
    right_in = xy_swap(jnp.stack([blocks[2][..., half:], blocks[3][..., half:]]), 2)
    return left_in, right_in


def reduce_second(blocks, left_in, right_in):
    half = blocks[0].shape[-1] // 2
    wide = lambda v: v.astype(jnp.float32)
    left_far = wide(blocks[2][..., :half]) + wide(left_in[1])
    right_far = wide(blocks[1][..., half:]) + wide(right_in[1])
    left_last = xy_swap(left_far.astype(jnp.bfloat16), 2)
    right_last = xy_swap(right_far.astype(jnp.bfloat16), 1)
    left = wide(blocks[0][..., :half]) + wide(left_in[0]) + wide(left_last)
    right = wide(blocks[0][..., half:]) + wide(right_in[0]) + wide(right_last)
    return jnp.concatenate([left, right], axis=-1)


def sum_everywhere(x):
    for axis in ("ctx", "fsdp"):
        size = lax.axis_size(axis)
        bit = 1
        while bit < size:
            x = x + lax.ppermute(x, axis, [(i, i ^ bit) for i in range(size)])
            bit *= 2
    return x


def in_rank_order(blocks, rank):
    odd = (rank % 2) == 1
    upper = (rank // 2) == 1
    one = [
        jnp.where(odd, blocks[1], blocks[0]),
        jnp.where(odd, blocks[0], blocks[1]),
        jnp.where(odd, blocks[3], blocks[2]),
        jnp.where(odd, blocks[2], blocks[3]),
    ]
    return [
        jnp.where(upper, one[2], one[0]),
        jnp.where(upper, one[3], one[1]),
        jnp.where(upper, one[0], one[2]),
        jnp.where(upper, one[1], one[3]),
    ]


def pick(x, index, size, axis):
    return lax.dynamic_slice_in_dim(x, index * size, size, axis)


def head_columns(w_query, w_key, w_value, w_gate, ctx_rank):
    return jnp.concatenate(
        [
            pick(w_query, ctx_rank, DK, 1),
            pick(w_key, ctx_rank, DK, 1),
            pick(w_value, ctx_rank, DV, 1),
            pick(w_gate, ctx_rank, DV, 1),
        ],
        axis=1,
    )


def out_pieces(w_out, ctx_rank, fsdp_rank, fsdp_size):
    rows = DV // fsdp_size
    start = (ctx_rank % 2) * DV
    return [
        lax.dynamic_slice_in_dim(w_out, start + (fsdp_rank ^ bit) * rows, rows, 0)
        for bit in range(fsdp_size)
    ]


def scatter_quarters(cuts, ctx_size, fsdp_size):
    parts = [cuts[0]]
    for bit in range(1, fsdp_size):
        pairs = [
            (c * fsdp_size + c // 2, c * fsdp_size + ((c // 2) ^ bit)) for c in range(ctx_size)
        ]
        parts.append(lax.ppermute(cuts[bit], ("ctx", "fsdp"), pairs))
    return parts


def choose_quarter(parts, ctx_rank, fsdp_rank):
    quarter = parts[0]
    for bit in range(1, len(parts)):
        quarter = jnp.where((fsdp_rank ^ (ctx_rank // 2)) == bit, parts[bit], quarter)
    return quarter


def copy_block(target, row, column, source, row_in, column_in, rows, width):
    step = min(rows, 64)

    def one(turn, carry):
        place_in = pl.multiple_of(row_in + turn * step, step)
        place_out = pl.multiple_of(row + turn * step, step)
        taken = source[pl.ds(place_in, step), pl.ds(column_in, width)]
        target[pl.ds(place_out, step), pl.ds(column, width)] = taken
        return carry

    lax.fori_loop(0, rows // step, one, 0)


def cut_ffn(w_up, w_down):
    ctx_size, fsdp_size = lax.axis_size("ctx"), lax.axis_size("fsdp")
    rows, width = w_up.shape[0], w_down.shape[1]
    unit, half = FF // (ctx_size * fsdp_size), ctx_size // 2
    wide = half * unit
    fourth = width // 4

    def kernel(up, down, *outs):
        rank = lax.axis_index("fsdp")
        core = lax.axis_index("ctx") % 2
        for number in range(fsdp_size - 1):
            other = rank ^ (number + 1)
            for i in range(half):
                column = pl.multiple_of(((core * half + i) * fsdp_size + other) * unit, unit)
                copy_block(outs[number], 0, i * unit, up, 0, column, rows, unit)
            for i in range(2):
                for q in range(2):
                    column = pl.multiple_of(core * 2 * fourth + q * fourth, fourth)
                    row = (i * fsdp_size + other) * unit
                    copy_block(
                        outs[number], (2 * i + q) * unit, wide, down, row, column, unit, fourth
                    )

    kind = jax.ShapeDtypeStruct((rows, wide + fourth), w_up.dtype)
    return list(pl.pallas_call(kernel, out_shape=[kind] * (fsdp_size - 1))(w_up, w_down))


def join_ffn(w_up, w_down, mine, other):
    ctx_size, fsdp_size = lax.axis_size("ctx"), lax.axis_size("fsdp")
    rows, width = w_up.shape[0], w_down.shape[1]
    unit, half = FF // (ctx_size * fsdp_size), ctx_size // 2
    wide = half * unit
    fourth = width // 4

    def kernel(up, down, *refs):
        up_out, down_out = refs[2 * len(mine) :]
        rank = lax.axis_index("fsdp")
        core = lax.axis_index("ctx") % 2
        for i in range(ctx_size):
            column = pl.multiple_of((i * fsdp_size + rank) * unit, unit)
            copy_block(up_out, rank * rows, i * unit, up, 0, column, rows, unit)
        for i in range(2):
            copy_block(
                down_out, (2 * rank + i) * unit, 0, down, (i * fsdp_size + rank) * unit, 0, unit, width
            )
        for number in range(2 * len(mine)):
            source = rank ^ (number % len(mine) + 1)
            part = core if number < len(mine) else 1 - core
            column = pl.multiple_of(part * wide, wide)
            copy_block(up_out, source * rows, column, refs[number], 0, 0, rows, wide)
            for i in range(2):
                for q in range(2):
                    column = pl.multiple_of(part * 2 * fourth + q * fourth, fourth)
                    row = (2 * source + i) * unit
                    copy_block(
                        down_out, row, column, refs[number], (2 * i + q) * unit, wide, unit, fourth
                    )

    shapes = [
        jax.ShapeDtypeStruct((fsdp_size * rows, FF // fsdp_size), w_up.dtype),
        jax.ShapeDtypeStruct((FF // fsdp_size, width), w_up.dtype),
    ]
    return pl.pallas_call(kernel, out_shape=shapes)(w_up, w_down, *mine, *other)


def smooth_parts(values):
    share = 0.5 + 0.5 * lax.erf(values * (0.5**0.5))
    density = jnp.exp(-0.5 * values * values) * ((0.5 / jnp.pi) ** 0.5)
    return values * share, share + values * density


def one_table(pos, doc, rate, scaling):
    keeping = (pos[:, None] >= pos[None, :]) & (doc[:, None] == doc[None, :])
    spacing = jnp.where(keeping, (pos[:, None] - pos[None, :]).astype(jnp.float32), 0.0)
    return jnp.where(keeping, jnp.exp(rate * spacing) * scaling, 0.0)


def ctx_sum(x):
    return lax.psum_scatter(x, "ctx", scatter_dimension=0, tiled=True)


def body_heads(
    tokens,
    cotangent,
    w_query,
    w_key,
    w_value,
    w_gate,
    w_out,
    w_up,
    w_down,
    norm_gains,
    norm_biases,
    block_deal,
    doc_lengths,
):
    low = jnp.bfloat16
    ctx_size = lax.axis_size("ctx")
    fsdp_size = lax.axis_size("fsdp")
    tok_rows = tokens.shape[2]
    full_length = tok_rows * ctx_size
    width = tokens.shape[3]
    share = width // (ctx_size * fsdp_size)
    grad_scale = float(MICRO * fsdp_size * full_length) ** (-0.5)
    ctx_rank = lax.axis_index("ctx")
    fsdp_rank = lax.axis_index("fsdp")
    pos = stored_positions(block_deal, full_length, BLOCK)
    rate = jnp.log1p(-jnp.exp2(-5.0 - ctx_rank.astype(jnp.float32)))
    scaling = DK ** (-0.5)

    own_in = head_columns(w_query, w_key, w_value, w_gate, ctx_rank)
    tokens = after(tokens, own_in)
    rows_in = []
    norm_one = []
    x_own = []
    for m in range(MICRO):
        rows_in.append(after(tokens[m, 0], *x_own[-1:]).astype(jnp.float32))
        norm_one.append(jax.vjp(layer_norm, rows_in[m], norm_gains[0], norm_biases[0]))
        x_own.append(norm_one[m][0].astype(low))
    grad_rows = [cotangent[m, 0].astype(jnp.float32) for m in range(MICRO)]
    x_all = [lax.all_gather(x, "ctx", axis=0, tiled=True) for x in x_own]
    in_first = gather_first(own_in)
    ffn_cut = cut_ffn(w_up, w_down)
    out_cut = out_pieces(w_out, ctx_rank, fsdp_rank, fsdp_size)
    in_first = lax.optimization_barrier(tuple(in_first) + tuple(ffn_cut) + tuple(out_cut))[:2]
    in_second = gather_second(*in_first)
    w_in = by_rank(own_in, *in_first, *in_second)
    out_cut = lax.optimization_barrier(tuple(out_cut) + tuple(in_first))[: len(out_cut)]
    out_parts = scatter_quarters(out_cut, ctx_size, fsdp_size)

    def mix(m, x_now, *earlier):
        doc = document_ids(pos, doc_lengths[m, 0])
        table = one_table(pos, doc, rate, scaling)
        joint = jnp.dot(x_now, w_in[:, : 2 * DK + DV], preferred_element_type=jnp.float32).astype(low)
        joint = after(joint, *earlier)
        gate_pre = jnp.dot(x_now, w_in[:, 2 * DK + DV :], preferred_element_type=jnp.float32)
        query, key, value = joint[:, :DK], joint[:, DK : 2 * DK], joint[:, 2 * DK :]
        attend = (contract_rows(query, key) * table).astype(low)
        retained = add_single(attend, value)
        mixed, mix_pull = jax.vjp(gated_mix, gate_pre, retained)
        return table, query, key, value, attend, mix_pull, mixed.astype(low)

    kept = [mix(0, x_all[0])]
    out_parts = lax.optimization_barrier(tuple(out_parts) + (kept[0][4],))[:-1]
    quarter = choose_quarter(out_parts, ctx_rank, fsdp_rank)
    out_first = gather_first(quarter)
    out_second = gather_second(*out_first)
    w_head = by_rank(quarter, *out_first, *out_second)
    cot_own = after(cotangent.reshape(MICRO * tok_rows, width), *out_first)
    cot_first = gather_first(cot_own)
    ffn_cut = lax.optimization_barrier(tuple(ffn_cut) + tuple(out_second))[: len(ffn_cut)]
    ffn_mine = [xy_swap(ffn_cut[bit - 1], bit) for bit in range(1, fsdp_size)]
    part = add_single(kept[0][6], w_head).astype(low)
    attn_out = [ctx_sum(after(part, *x_all[1:]))]
    for m in range(1, MICRO):
        kept.append(mix(m, after(x_all[m], *out_parts), *cot_first))
        part = add_single(kept[m][6], w_head).astype(low)
        attn_out.append(ctx_sum(after(part, *ffn_mine[:2])))
    cot_second = gather_second(*cot_first)
    up_own, down_own = join_ffn(w_up, w_down, ffn_mine, [core_swap(x) for x in ffn_mine])
    cot_all = [
        place(
            (fsdp_size * tok_rows, width),
            [
                (cot_own, m * tok_rows, tok_rows, 0, 0),
                (cot_first[0], m * tok_rows, tok_rows, tok_rows, 0),
                (cot_second[m], 0, tok_rows, 2 * tok_rows, 0),
                (cot_first[1], m * tok_rows, tok_rows, 3 * tok_rows, 0),
            ],
        )
        for m in range(MICRO)
    ]

    outs = [None] * MICRO
    grad_attn = []
    grad_hidden = []
    ffn_kept = []
    norm_two_terms = []

    def enter(m):
        hidden = rows_in[m] + attn_out[m].astype(jnp.float32)
        normed_two, pull_two = jax.vjp(layer_norm, hidden, norm_gains[1], norm_biases[1])
        two_own = normed_two.astype(low)
        return hidden, pull_two, two_own, gather_first(two_own)

    entered = [enter(0)]
    for m in range(MICRO):
        hidden, pull_two, two_own, two_first = entered[m]
        two_first = lax.optimization_barrier(tuple(two_first) + (up_own, down_own))[:2]
        two_second = gather_second(*two_first)
        two_second = lax.optimization_barrier(tuple(two_second) + (cot_all[m],))[:2]
        two_all = by_offset(two_own, *two_first, *two_second)
        active, slope = smooth_parts(add_single(two_all, up_own))
        active_low, slope = lax.optimization_barrier((active.astype(low), slope))
        grad_up = (back_rows(cot_all[m], down_own) * slope).astype(low)
        norm_part = back_rows(grad_up, up_own).astype(low)
        later = ()
        if m + 1 < MICRO:
            attn_out[m + 1] = after(attn_out[m + 1], norm_part)
            entered.append(enter(m + 1))
            later = entered[m + 1][3]
        grad_norm_two = after(plane_reduce_rows(norm_part), *grad_attn[-1:], *later)
        grad_ln, gain_two, bias_two = pull_two(grad_norm_two)
        norm_two_terms.append((gain_two, bias_two))
        total = grad_rows[m] + grad_ln
        grad_hidden.append(total)
        grad_attn.append(total.astype(low))
        ffn_kept.append((two_all, grad_up, active_low, hidden))

    grad_all = [lax.all_gather(grad_attn[m], "ctx", axis=0, tiled=True) for m in range(MICRO)]

    def unmix(m, grad_now):
        table, query, key, value, attend, mix_pull, mixed_low = kept[m]
        grad_mixed = back_rows(grad_now, w_head)
        grad_gate, grad_ret = mix_pull(grad_mixed)
        ret_low = grad_ret.astype(low)
        grad_scores = (contract_rows(ret_low, value) * table).astype(low)
        grad_query = add_single(grad_scores, key).astype(low)
        grad_key = contract_cols(grad_scores, query).astype(low)
        grad_value = contract_cols(attend, ret_low).astype(low)
        return jnp.concatenate([grad_query, grad_key, grad_value, grad_gate.astype(low)], axis=1)

    terms = []
    sums = []
    fill = ()
    for m in range(MICRO):
        grad_now = after(grad_all[m], *(grad_attn[1:] if m == 0 else terms[-1:]), *fill)
        grad_in = unmix(m, grad_now)
        part = back_rows(grad_in, w_in).astype(low)
        terms.append(part)
        sums.append(ctx_sum(after(part, *grad_all[m + 1 :], *sums[-1:])))
        x_now, grad_in = lax.optimization_barrier((x_all[m], grad_in, part))[:2]
        in_now = contract_cols(x_now, grad_in)
        if m == 0:
            in_term = in_now
            sums[m] = after(sums[m], in_term)
            ready = [after(ffn_kept[n][2], part, grad_attn[n]) for n in range(MICRO)]
            fill = tuple(add_single(ready[n], down_own).astype(low) for n in range(MICRO))
        else:
            in_term = (in_term + in_now).astype(low)
    in_view = in_term.reshape(ctx_size, fsdp_size, share, -1)
    in_blocks_out = [pick(in_view, fsdp_rank ^ j, 1, 1)[:, 0] for j in range(fsdp_size)]
    in_sent = reduce_first(in_blocks_out)
    up_grad = sum(contract_cols(k[0], after(k[1], in_term)) for k in ffn_kept).astype(low)
    down_grad = sum(
        contract_cols(after(ready[n], up_grad), cot_all[n]) for n in range(MICRO)
    ).astype(low)
    sums[-1] = after(sums[-1], up_grad, *in_sent)
    up_sum = ctx_sum(after(up_grad, sums[-1]))
    down_sum = ctx_sum(after(down_grad, sums[-1]))
    in_sum = reduce_second(in_blocks_out, *in_sent).astype(low)
    in_mine = lax.all_to_all(in_sum, "ctx", split_axis=0, concat_axis=0, tiled=True)
    for n in range(MICRO):
        outs[n] = (ffn_kept[n][3] + plane_reduce_rows(after(fill[n], *in_sent))).astype(low)
    out_term = sum(
        contract_cols(after(kept[m][6], down_grad), grad_all[m]) for m in range(MICRO)
    ).astype(low)

    grad_tokens = []
    norm_one_terms = []
    for m in range(MICRO):
        grad_ln, gain_one, bias_one = norm_one[m][1](sums[m].astype(jnp.float32))
        norm_one_terms.append((gain_one, bias_one))
        grad_tokens.append(grad_hidden[m] + grad_ln)

    gain_rows = [sum(t[0] for t in norm_one_terms), sum(t[0] for t in norm_two_terms)]
    bias_rows = [sum(t[1] for t in norm_one_terms), sum(t[1] for t in norm_two_terms)]
    norm_sums = sum_everywhere(jnp.stack(gain_rows + bias_rows))
    out_term = after(out_term, in_sum)
    rows = DV // fsdp_size
    out_blocks = [pick(out_term, fsdp_rank ^ j, rows, 0) for j in range(fsdp_size)]
    g_out = reduce_second(out_blocks, *reduce_first(out_blocks))

    def by_head(first, size):
        part = in_mine[:, :, first : first + size].transpose(1, 0, 2)
        return part.reshape(share, -1).astype(jnp.float32) * grad_scale

    g_query = by_head(0, DK)
    g_key = by_head(DK, DK)
    g_value = by_head(2 * DK, DV)
    g_gate = by_head(2 * DK + DV, DV)

    up_view = up_sum.reshape(fsdp_size, share, -1)
    pieces = [lax.dynamic_index_in_dim(up_view, fsdp_rank, 0, keepdims=False)]
    for bit in range(1, fsdp_size):
        pieces.append(
            xy_swap(lax.dynamic_index_in_dim(up_view, fsdp_rank ^ bit, 0, keepdims=False), bit)
        )
    pieces = [p.reshape(share, ctx_size, -1) for p in in_rank_order(pieces, fsdp_rank)]
    g_up = jnp.stack(pieces, axis=2).reshape(share, FF).astype(jnp.float32) * grad_scale

    norm_sums = pick(norm_sums, ctx_rank * fsdp_size + fsdp_rank, share, 1) * grad_scale
    return (
        jnp.stack(outs)[:, None],
        jnp.stack(grad_tokens)[:, None],
        g_query,
        g_key,
        g_value,
        g_gate,
        g_out * grad_scale,
        g_up,
        down_sum.astype(jnp.float32) * grad_scale,
        norm_sums[:2],
        norm_sums[2:],
    )


def solution(mesh):
    in_specs = (
        P(None, "fsdp", "ctx", None),
        P(None, "fsdp", "ctx", None),
        P("fsdp", None),
        P("fsdp", None),
        P("fsdp", None),
        P("fsdp", None),
        P("fsdp", None),
        P("fsdp", None),
        P("fsdp", None),
        P(),
        P(),
        P(),
        P(None, "fsdp", None),
    )
    out_specs = (
        P(None, "fsdp", "ctx", None),
        P(None, "fsdp", "ctx", None),
        P(("ctx", "fsdp"), None),
        P(("ctx", "fsdp"), None),
        P(("ctx", "fsdp"), None),
        P(("ctx", "fsdp"), None),
        P(("ctx", "fsdp"), None),
        P(("ctx", "fsdp"), None),
        P(("ctx", "fsdp"), None),
        P(None, ("ctx", "fsdp")),
        P(None, ("ctx", "fsdp")),
    )
    by_heads = mesh.shape["ctx"] == HEADS and mesh.shape["fsdp"] == 4
    chosen = body_heads if by_heads else body
    return jax.shard_map(chosen, mesh=mesh, in_specs=in_specs, out_specs=out_specs, check_vma=False)
```

```python
import jax
import jax.numpy as jnp
from jax import lax
from jax.experimental import pallas as pl
from jax.sharding import PartitionSpec as P

HEADS = 8
DK = 256
DV = 512
FF = 4096
MICRO = 2
QW = 2048
VW = 4096
BLOCK = 64


epsilon = 1e-05
group_floor = 1.0


def layer_norm(values, gain_row, offset):
    center = jnp.mean(values, axis=-1, keepdims=True)
    centred = values - center
    spread = jnp.mean(centred * centred, axis=-1, keepdims=True)
    return centred * lax.rsqrt(spread + epsilon) * gain_row + offset


def gated_mix(gate_pre, retained):
    number = retained.shape[0]
    grouped = retained.reshape(number, -1, DV)
    center = jnp.mean(grouped, axis=-1, keepdims=True)
    centred = grouped - center
    spread = jnp.mean(centred * centred, axis=-1, keepdims=True)
    normed = (centred * lax.rsqrt(spread + group_floor)).reshape(number, -1)
    return jax.nn.silu(gate_pre) * normed


def smooth_act(values):
    return jax.nn.gelu(values, approximate=False)


def stored_positions(block_deal, full_length, block_size):
    stored = jnp.arange(full_length, dtype=jnp.int32)
    block_ids = stored // block_size
    slots_all = jnp.arange(block_deal.shape[0], dtype=jnp.int32)
    picked = jnp.sum(
        jnp.where(block_ids[:, None] == slots_all[None, :], block_deal[None, :], 0),
        axis=1,
        dtype=jnp.int32,
    )
    return picked * block_size + stored % block_size


def document_ids(positions, doc_sizes):
    starts = jnp.cumsum(doc_sizes, dtype=jnp.int32) - doc_sizes
    return (
        jnp.sum((positions[:, None] >= starts[None, :]).astype(jnp.int32), axis=1, dtype=jnp.int32)
        - 1
    )


def decay_table(query_pos, query_doc, key_pos, key_doc, decay_log, scaling):
    keeping = (query_pos[:, None] >= key_pos[None, :]) & (query_doc[:, None] == key_doc[None, :])
    spacing = jnp.where(keeping, (query_pos[:, None] - key_pos[None, :]).astype(jnp.float32), 0.0)
    factor = jnp.exp(decay_log[:, None, None] * spacing[None])
    return jnp.where(keeping[None], factor * scaling, 0.0)


def contract_rows(left, right):
    return lax.dot_general(
        left, right, (((1,), (1,)), ((), ())), preferred_element_type=jnp.float32
    )


def contract_cols(left, right):
    return lax.dot_general(
        left, right, (((0,), (0,)), ((), ())), preferred_element_type=jnp.float32
    )


def add_single(left, weight_piece):
    return jnp.dot(left, weight_piece, preferred_element_type=jnp.float32)


def back_rows(left, weight_piece):
    return contract_rows(left, weight_piece)


def weight_term(kept_acts, number):
    normed_one, grads_in, normed_two, grads_up, mixed_all, grads_attn, active_all, grads_ffn = (
        kept_acts
    )
    pieces = [
        contract_cols(normed_one, grads_in),
        contract_cols(normed_two, grads_up),
        contract_cols(mixed_all, grads_attn).reshape(number, -1),
        contract_cols(active_all, grads_ffn).reshape(number, -1),
    ]
    return jnp.concatenate(pieces, axis=1)


def body(
    tokens,
    cotangent,
    w_query,
    w_key,
    w_value,
    w_gate,
    w_out,
    w_up,
    w_down,
    norm_gains,
    norm_biases,
    block_deal,
    doc_lengths,
):
    ctx_size = lax.axis_size("ctx")
    tok_rows = tokens.shape[2]
    full_length = tok_rows * ctx_size
    model_width = tokens.shape[3]
    share_rows = model_width // lax.axis_size(("ctx", "fsdp"))
    grad_scale = float(MICRO * lax.axis_size("fsdp") * full_length) ** (-0.5)
    own_start = lax.axis_index("ctx") * tok_rows
    key_pos = stored_positions(block_deal, full_length, BLOCK)
    query_pos = lax.dynamic_slice_in_dim(key_pos, own_start, tok_rows)
    decay_log = jnp.log1p(-jnp.exp2(-5.0 - jnp.arange(HEADS).astype(jnp.float32)))
    scaling = DK ** (-0.5)
    out_list = []
    grad_list = []
    weight_sum = None
    gain_sum = jnp.zeros((2, model_width), jnp.float32)
    bias_sum = jnp.zeros((2, model_width), jnp.float32)
    for batch_index in range(MICRO):
        rows_in = tokens[batch_index, 0].astype(jnp.float32)
        grad_rows = cotangent[batch_index, 0].astype(jnp.float32)
        key_doc = document_ids(key_pos, doc_lengths[batch_index, 0])
        query_doc = lax.dynamic_slice_in_dim(key_doc, own_start, tok_rows)
        table = decay_table(query_pos, query_doc, key_pos, key_doc, decay_log, scaling)
        normed_one, norm_pull_one = jax.vjp(layer_norm, rows_in, norm_gains[0], norm_biases[0])
        low_one = normed_one.astype(jnp.bfloat16)
        pieces = (
            lax.all_gather(w_query, "fsdp", axis=0, tiled=True),
            lax.all_gather(w_key, "fsdp", axis=0, tiled=True),
            lax.all_gather(w_value, "fsdp", axis=0, tiled=True),
            lax.all_gather(w_gate, "fsdp", axis=0, tiled=True),
        )
        query_f, key_f, value_f, gate_pre = tuple(
            (
                jnp.dot(low_one, weight_piece, preferred_element_type=jnp.float32)
                for weight_piece in pieces
            )
        )
        query_low = query_f.astype(jnp.bfloat16)
        key_low = key_f.astype(jnp.bfloat16)
        value_low = value_f.astype(jnp.bfloat16)
        keys_all, values_all = (
            lax.all_gather(key_low, "ctx", axis=0, tiled=True),
            lax.all_gather(value_low, "ctx", axis=0, tiled=True),
        )
        query_heads = query_low.reshape(tok_rows, HEADS, DK)
        key_heads = keys_all.reshape(full_length, HEADS, DK)
        value_heads = values_all.reshape(full_length, HEADS, DV)
        scores = jnp.einsum(
            "thd,shd->hts", query_heads, key_heads, preferred_element_type=jnp.float32
        )
        attend = (scores * table).astype(jnp.bfloat16)
        retained = jnp.einsum(
            "hts,shd->thd", attend, value_heads, preferred_element_type=jnp.float32
        ).reshape(tok_rows, VW)
        mixed, mix_pull = jax.vjp(gated_mix, gate_pre, retained)
        mixed_low = mixed.astype(jnp.bfloat16)
        attn_out = add_single(mixed_low, lax.all_gather(w_out, "fsdp", axis=0, tiled=True))
        hidden = rows_in + attn_out
        normed_two, norm_pull_two = jax.vjp(layer_norm, hidden, norm_gains[1], norm_biases[1])
        low_two = normed_two.astype(jnp.bfloat16)
        up_pre = add_single(low_two, lax.all_gather(w_up, "fsdp", axis=0, tiled=True))
        active, act_pull = jax.vjp(smooth_act, up_pre)
        active_low = active.astype(jnp.bfloat16)
        ffn_out = add_single(active_low, lax.all_gather(w_down, "fsdp", axis=0, tiled=True))
        out_list.append((hidden + ffn_out).astype(jnp.bfloat16))
        grad_ffn = grad_rows.astype(jnp.bfloat16)
        grad_act = back_rows(grad_ffn, lax.all_gather(w_down, "fsdp", axis=0, tiled=True))
        grad_up = act_pull(grad_act)[0].astype(jnp.bfloat16)
        grad_norm_two = back_rows(grad_up, lax.all_gather(w_up, "fsdp", axis=0, tiled=True))
        grad_hidden_ln, grad_gain_two, grad_bias_two = norm_pull_two(grad_norm_two)
        grad_hidden = grad_rows + grad_hidden_ln
        grad_attn = grad_hidden.astype(jnp.bfloat16)
        grad_mixed = back_rows(grad_attn, lax.all_gather(w_out, "fsdp", axis=0, tiled=True))
        grad_gate_f, grad_ret_f = mix_pull(grad_mixed)
        grad_gate = grad_gate_f.astype(jnp.bfloat16)
        ret_low = grad_ret_f.astype(jnp.bfloat16)
        ret_heads = ret_low.reshape(tok_rows, HEADS, DV)
        grad_attend = jnp.einsum(
            "thd,shd->hts", ret_heads, value_heads, preferred_element_type=jnp.float32
        )
        grad_scores = (grad_attend * table).astype(jnp.bfloat16)
        grad_query = (
            jnp.einsum("hts,shd->thd", grad_scores, key_heads, preferred_element_type=jnp.float32)
            .reshape(tok_rows, QW)
            .astype(jnp.bfloat16)
        )
        key_part = jnp.einsum(
            "hts,thd->shd", grad_scores, query_heads, preferred_element_type=jnp.float32
        ).reshape(tok_rows * lax.axis_size("ctx"), QW)
        value_part = jnp.einsum(
            "hts,thd->shd", attend, ret_heads, preferred_element_type=jnp.float32
        ).reshape(tok_rows * lax.axis_size("ctx"), VW)
        key_value_sum = lax.psum_scatter(
            jnp.concatenate([key_part, value_part], axis=1).astype(jnp.bfloat16),
            "ctx",
            scatter_dimension=0,
            tiled=True,
        ).astype(jnp.float32)
        grad_key = key_value_sum[:, :QW].astype(jnp.bfloat16)
        grad_value = key_value_sum[:, QW:].astype(jnp.bfloat16)
        term_now = (
            contract_rows(grad_query, lax.all_gather(w_query, "fsdp", axis=0, tiled=True))
            + contract_rows(grad_key, lax.all_gather(w_key, "fsdp", axis=0, tiled=True))
            + contract_rows(grad_value, lax.all_gather(w_value, "fsdp", axis=0, tiled=True))
            + contract_rows(grad_gate, lax.all_gather(w_gate, "fsdp", axis=0, tiled=True))
        )
        grad_rows_ln, grad_gain_one, grad_bias_one = norm_pull_one(term_now)
        grad_list.append(grad_hidden + grad_rows_ln)
        gain_sum = gain_sum + jnp.stack([grad_gain_one, grad_gain_two])
        bias_sum = bias_sum + jnp.stack([grad_bias_one, grad_bias_two])
        kept_now = (
            low_one,
            jnp.concatenate([grad_query, grad_key, grad_value, grad_gate], axis=1),
            low_two,
            grad_up,
            mixed_low,
            grad_attn,
            active_low,
            grad_ffn,
        )
        term_sum = lax.psum_scatter(
            weight_term(kept_now, share_rows * lax.axis_size(("ctx", "fsdp"))),
            ("ctx", "fsdp"),
            scatter_dimension=0,
            tiled=True,
        )
        weight_sum = term_sum if weight_sum is None else weight_sum + term_sum
    weight_sum = weight_sum * grad_scale
    bounds = [QW, 2 * QW, 2 * QW + VW, 2 * QW + 2 * VW, 2 * QW + 2 * VW + FF, 2 * QW + 3 * VW + FF]
    g_query, g_key, g_value, g_gate, g_up, g_out_flat, g_down_flat = jnp.split(
        weight_sum, bounds, axis=1
    )
    g_out = g_out_flat.reshape(share_rows * (VW // model_width), model_width)
    g_down = g_down_flat.reshape(share_rows * (FF // model_width), model_width)
    gain_grads, bias_grads = (
        lax.psum_scatter(gain_sum, ("ctx", "fsdp"), scatter_dimension=1, tiled=True),
        lax.psum_scatter(bias_sum, ("ctx", "fsdp"), scatter_dimension=1, tiled=True),
    )
    gain_grads = gain_grads * grad_scale
    bias_grads = bias_grads * grad_scale
    output = jnp.stack(out_list)[:, None]
    grad_tokens = jnp.stack(grad_list)[:, None]
    return (
        output,
        grad_tokens,
        g_query,
        g_key,
        g_value,
        g_gate,
        g_out,
        g_up,
        g_down,
        gain_grads,
        bias_grads,
    )


def xy_swap(x, bit):
    return lax.ppermute(x, "fsdp", [(i, i ^ bit) for i in range(lax.axis_size("fsdp"))])


def core_swap(x):
    return lax.ppermute(x, "ctx", [(i, i ^ 1) for i in range(lax.axis_size("ctx"))])


def after(x, *earlier):
    return lax.optimization_barrier((x,) + tuple(earlier))[0]


def place(shape, items):
    arrays = []
    for item in items:
        if not any(item[0] is a for a in arrays):
            arrays.append(item[0])
    slots = [[item[0] is a for a in arrays].index(True) for item in items]
    kind = arrays[0].dtype

    def kernel(*refs):
        out = refs[len(arrays)]
        rank = lax.axis_index("fsdp")
        core = lax.axis_index("ctx") % 2
        for number, (array, start, rows, row, column) in enumerate(items):
            width = array.shape[1]
            step = min(rows, 64)
            source = refs[slots[number]]
            base = row(rank, core) if callable(row) else row

            def copy(first, width=width, step=step, source=source, base=base, start=start, rows=rows):
                def one(turn, carry):
                    place_in = pl.multiple_of(start + turn * step, step)
                    place_out = pl.multiple_of(base + turn * step, step)
                    out[pl.ds(place_out, step), first : first + width] = source[
                        pl.ds(place_in, step), :
                    ]
                    return carry

                lax.fori_loop(0, rows // step, one, 0)

            if callable(column):
                for which in range(2):
                    pl.when(core == which)(lambda which=which: copy(column(rank, which)))
            else:
                copy(column)

    size = shape[0] * shape[1] * jnp.dtype(kind).itemsize
    return pl.pallas_call(
        kernel,
        out_shape=jax.ShapeDtypeStruct(shape, kind),
        cost_estimate=pl.CostEstimate(flops=0, bytes_accessed=2 * size, transcendentals=0),
    )(*arrays)


def gather_first(x):
    return xy_swap(x, 1), xy_swap(x, 2)


def gather_second(first, second):
    half = first.shape[0] // 2
    return xy_swap(first[:half], 2), xy_swap(second[half:], 1)


def by_offset(x, first, second, low_part, high_part):
    rows, half = x.shape[0], x.shape[0] // 2
    return place(
        (4 * rows, x.shape[1]),
        [
            (x, 0, rows, 0, 0),
            (first, 0, rows, rows, 0),
            (low_part, 0, half, 2 * rows, 0),
            (high_part, 0, half, 2 * rows + half, 0),
            (second, 0, rows, 3 * rows, 0),
        ],
    )


def by_rank(x, first, second, low_part, high_part):
    rows, half = x.shape[0], x.shape[0] // 2
    return place(
        (4 * rows, x.shape[1]),
        [
            (x, 0, rows, lambda f, c: f * rows, 0),
            (first, 0, rows, lambda f, c: (f ^ 1) * rows, 0),
            (low_part, 0, half, lambda f, c: (f ^ 3) * rows, 0),
            (high_part, 0, half, lambda f, c: (f ^ 3) * rows + half, 0),
            (second, 0, rows, lambda f, c: (f ^ 2) * rows, 0),
        ],
    )


def rows_first(part):
    rows, half = part.shape[0] // 4, part.shape[1] // 2
    return xy_swap(part[rows : 3 * rows, :half], 1), xy_swap(part[2 * rows :, half:], 2)


def rows_second(part, left_in, right_in):
    rows, half = part.shape[0] // 4, part.shape[1] // 2
    wide = lambda v: v.astype(jnp.float32)
    left_far = wide(part[3 * rows :, :half]) + wide(left_in[rows:])
    right_far = wide(part[rows : 2 * rows, half:]) + wide(right_in[:rows])
    left_last = xy_swap(left_far.astype(jnp.bfloat16), 2)
    right_last = xy_swap(right_far.astype(jnp.bfloat16), 1)
    left = wide(part[:rows, :half]) + wide(left_in[:rows]) + wide(left_last)
    right = wide(part[:rows, half:]) + wide(right_in[rows:]) + wide(right_last)
    return jnp.concatenate([left, right], axis=1)


def reduce_first(blocks):
    half = blocks[0].shape[-1] // 2
    left_in = xy_swap(jnp.stack([blocks[1][..., :half], blocks[3][..., :half]]), 1)
    right_in = xy_swap(jnp.stack([blocks[2][..., half:], blocks[3][..., half:]]), 2)
    return left_in, right_in


def reduce_second(blocks, left_in, right_in):
    half = blocks[0].shape[-1] // 2
    wide = lambda v: v.astype(jnp.float32)
    left_far = wide(blocks[2][..., :half]) + wide(left_in[1])
    right_far = wide(blocks[1][..., half:]) + wide(right_in[1])
    left_last = xy_swap(left_far.astype(jnp.bfloat16), 2)
    right_last = xy_swap(right_far.astype(jnp.bfloat16), 1)
    left = wide(blocks[0][..., :half]) + wide(left_in[0]) + wide(left_last)
    right = wide(blocks[0][..., half:]) + wide(right_in[0]) + wide(right_last)
    return jnp.concatenate([left, right], axis=-1)


def sum_everywhere(x):
    for axis in ("ctx", "fsdp"):
        size = lax.axis_size(axis)
        bit = 1
        while bit < size:
            x = x + lax.ppermute(x, axis, [(i, i ^ bit) for i in range(size)])
            bit *= 2
    return x


def in_rank_order(blocks, rank):
    odd = (rank % 2) == 1
    upper = (rank // 2) == 1
    one = [
        jnp.where(odd, blocks[1], blocks[0]),
        jnp.where(odd, blocks[0], blocks[1]),
        jnp.where(odd, blocks[3], blocks[2]),
        jnp.where(odd, blocks[2], blocks[3]),
    ]
    return [
        jnp.where(upper, one[2], one[0]),
        jnp.where(upper, one[3], one[1]),
        jnp.where(upper, one[0], one[2]),
        jnp.where(upper, one[1], one[3]),
    ]


def pick(x, index, size, axis):
    return lax.dynamic_slice_in_dim(x, index * size, size, axis)


def head_columns(w_query, w_key, w_value, w_gate, ctx_rank):
    return jnp.concatenate(
        [
            pick(w_query, ctx_rank, DK, 1),
            pick(w_key, ctx_rank, DK, 1),
            pick(w_value, ctx_rank, DV, 1),
            pick(w_gate, ctx_rank, DV, 1),
        ],
        axis=1,
    )


def out_pieces(w_out, ctx_rank, fsdp_rank, fsdp_size):
    rows = DV // fsdp_size
    start = (ctx_rank % 2) * DV
    return [
        lax.dynamic_slice_in_dim(w_out, start + (fsdp_rank ^ bit) * rows, rows, 0)
        for bit in range(fsdp_size)
    ]


def scatter_quarters(cuts, ctx_size, fsdp_size):
    parts = [cuts[0]]
    for bit in range(1, fsdp_size):
        pairs = [
            (c * fsdp_size + c // 2, c * fsdp_size + ((c // 2) ^ bit)) for c in range(ctx_size)
        ]
        parts.append(lax.ppermute(cuts[bit], ("ctx", "fsdp"), pairs))
    return parts


def choose_quarter(parts, ctx_rank, fsdp_rank):
    quarter = parts[0]
    for bit in range(1, len(parts)):
        quarter = jnp.where((fsdp_rank ^ (ctx_rank // 2)) == bit, parts[bit], quarter)
    return quarter


def copy_block(target, row, column, source, row_in, column_in, rows, width):
    step = min(rows, 64)

    def one(turn, carry):
        place_in = pl.multiple_of(row_in + turn * step, step)
        place_out = pl.multiple_of(row + turn * step, step)
        taken = source[pl.ds(place_in, step), pl.ds(column_in, width)]
        target[pl.ds(place_out, step), pl.ds(column, width)] = taken
        return carry

    lax.fori_loop(0, rows // step, one, 0)


def cut_ffn(w_up, w_down):
    ctx_size, fsdp_size = lax.axis_size("ctx"), lax.axis_size("fsdp")
    rows, width = w_up.shape[0], w_down.shape[1]
    unit, half = FF // (ctx_size * fsdp_size), ctx_size // 2
    wide = half * unit
    fourth = width // 4

    def kernel(up, down, *outs):
        rank = lax.axis_index("fsdp")
        core = lax.axis_index("ctx") % 2
        for number in range(fsdp_size - 1):
            other = rank ^ (number + 1)
            for i in range(half):
                column = pl.multiple_of(((core * half + i) * fsdp_size + other) * unit, unit)
                copy_block(outs[number], 0, i * unit, up, 0, column, rows, unit)
            for i in range(2):
                for q in range(2):
                    column = pl.multiple_of(core * 2 * fourth + q * fourth, fourth)
                    row = (i * fsdp_size + other) * unit
                    copy_block(
                        outs[number], (2 * i + q) * unit, wide, down, row, column, unit, fourth
                    )

    kind = jax.ShapeDtypeStruct((rows, wide + fourth), w_up.dtype)
    return list(pl.pallas_call(kernel, out_shape=[kind] * (fsdp_size - 1))(w_up, w_down))


def join_ffn(w_up, w_down, mine, other):
    ctx_size, fsdp_size = lax.axis_size("ctx"), lax.axis_size("fsdp")
    rows, width = w_up.shape[0], w_down.shape[1]
    unit, half = FF // (ctx_size * fsdp_size), ctx_size // 2
    wide = half * unit
    fourth = width // 4

    def kernel(up, down, *refs):
        up_out, down_out = refs[2 * len(mine) :]
        rank = lax.axis_index("fsdp")
        core = lax.axis_index("ctx") % 2
        for i in range(ctx_size):
            column = pl.multiple_of((i * fsdp_size + rank) * unit, unit)
            copy_block(up_out, rank * rows, i * unit, up, 0, column, rows, unit)
        for i in range(2):
            copy_block(
                down_out, (2 * rank + i) * unit, 0, down, (i * fsdp_size + rank) * unit, 0, unit, width
            )
        for number in range(2 * len(mine)):
            source = rank ^ (number % len(mine) + 1)
            part = core if number < len(mine) else 1 - core
            column = pl.multiple_of(part * wide, wide)
            copy_block(up_out, source * rows, column, refs[number], 0, 0, rows, wide)
            for i in range(2):
                for q in range(2):
                    column = pl.multiple_of(part * 2 * fourth + q * fourth, fourth)
                    row = (2 * source + i) * unit
                    copy_block(
                        down_out, row, column, refs[number], (2 * i + q) * unit, wide, unit, fourth
                    )

    shapes = [
        jax.ShapeDtypeStruct((fsdp_size * rows, FF // fsdp_size), w_up.dtype),
        jax.ShapeDtypeStruct((FF // fsdp_size, width), w_up.dtype),
    ]
    return pl.pallas_call(kernel, out_shape=shapes)(w_up, w_down, *mine, *other)


def smooth_parts(values):
    share = 0.5 + 0.5 * lax.erf(values * (0.5**0.5))
    density = jnp.exp(-0.5 * values * values) * ((0.5 / jnp.pi) ** 0.5)
    return values * share, share + values * density


def one_table(pos, doc, rate, scaling):
    keeping = (pos[:, None] >= pos[None, :]) & (doc[:, None] == doc[None, :])
    spacing = jnp.where(keeping, (pos[:, None] - pos[None, :]).astype(jnp.float32), 0.0)
    return jnp.where(keeping, jnp.exp(rate * spacing) * scaling, 0.0)


def chip_sum(x):
    size = lax.axis_size("ctx")
    view = x.reshape(size // 2, 2, x.shape[0] // size, x.shape[1])
    core = lax.axis_index("ctx") % 2
    own = lax.dynamic_index_in_dim(view, core, 1, keepdims=False)
    other = core_swap(lax.dynamic_index_in_dim(view, 1 - core, 1, keepdims=False))
    half = (own.astype(jnp.float32) + other.astype(jnp.float32)).astype(x.dtype)
    groups = [[2 * i + h for i in range(size // 2)] for h in range(2)]
    half = half.reshape(x.shape[0] // 2, x.shape[1])
    return half, groups


def ctx_sum(x):
    return lax.psum_scatter(x, "ctx", scatter_dimension=0, tiled=True)


def body_heads(
    tokens,
    cotangent,
    w_query,
    w_key,
    w_value,
    w_gate,
    w_out,
    w_up,
    w_down,
    norm_gains,
    norm_biases,
    block_deal,
    doc_lengths,
):
    low = jnp.bfloat16
    ctx_size = lax.axis_size("ctx")
    fsdp_size = lax.axis_size("fsdp")
    tok_rows = tokens.shape[2]
    full_length = tok_rows * ctx_size
    width = tokens.shape[3]
    share = width // (ctx_size * fsdp_size)
    grad_scale = float(MICRO * fsdp_size * full_length) ** (-0.5)
    ctx_rank = lax.axis_index("ctx")
    fsdp_rank = lax.axis_index("fsdp")
    pos = stored_positions(block_deal, full_length, BLOCK)
    rate = jnp.log1p(-jnp.exp2(-5.0 - ctx_rank.astype(jnp.float32)))
    scaling = DK ** (-0.5)

    own_in = head_columns(w_query, w_key, w_value, w_gate, ctx_rank)
    tokens = after(tokens, own_in)
    rows_in = []
    norm_one = []
    x_own = []
    for m in range(MICRO):
        rows_in.append(after(tokens[m, 0], *x_own[-1:]).astype(jnp.float32))
        norm_one.append(jax.vjp(layer_norm, rows_in[m], norm_gains[0], norm_biases[0]))
        x_own.append(norm_one[m][0].astype(low))
    grad_rows = [cotangent[m, 0].astype(jnp.float32) for m in range(MICRO)]
    x_all = [lax.all_gather(x, "ctx", axis=0, tiled=True) for x in x_own]
    in_first = gather_first(own_in)
    ffn_cut = cut_ffn(w_up, w_down)
    out_cut = out_pieces(w_out, ctx_rank, fsdp_rank, fsdp_size)
    in_first = lax.optimization_barrier(tuple(in_first) + tuple(ffn_cut) + tuple(out_cut))[:2]
    in_second = gather_second(*in_first)
    w_in = by_rank(own_in, *in_first, *in_second)
    out_cut = lax.optimization_barrier(tuple(out_cut) + tuple(in_first))[: len(out_cut)]
    out_parts = scatter_quarters(out_cut, ctx_size, fsdp_size)

    def mix(m, x_now, *earlier):
        doc = document_ids(pos, doc_lengths[m, 0])
        table = one_table(pos, doc, rate, scaling)
        joint = jnp.dot(x_now, w_in[:, : 2 * DK + DV], preferred_element_type=jnp.float32).astype(low)
        joint = after(joint, *earlier)
        gate_pre = jnp.dot(x_now, w_in[:, 2 * DK + DV :], preferred_element_type=jnp.float32)
        query, key, value = joint[:, :DK], joint[:, DK : 2 * DK], joint[:, 2 * DK :]
        attend = (contract_rows(query, key) * table).astype(low)
        retained = add_single(attend, value)
        mixed, mix_pull = jax.vjp(gated_mix, gate_pre, retained)
        return table, query, key, value, attend, mix_pull, mixed.astype(low)

    kept = [mix(0, x_all[0])]
    out_parts = lax.optimization_barrier(tuple(out_parts) + (kept[0][4],))[:-1]
    quarter = choose_quarter(out_parts, ctx_rank, fsdp_rank)
    out_first = gather_first(quarter)
    out_second = gather_second(*out_first)
    w_head = by_rank(quarter, *out_first, *out_second)
    cot_own = after(cotangent.reshape(MICRO * tok_rows, width), *out_first)
    cot_first = gather_first(cot_own)
    ffn_cut = lax.optimization_barrier(tuple(ffn_cut) + tuple(out_second))[: len(ffn_cut)]
    ffn_mine = [xy_swap(ffn_cut[bit - 1], bit) for bit in range(1, fsdp_size)]
    part = add_single(kept[0][6], w_head).astype(low)
    attn_out = [ctx_sum(after(part, *x_all[1:], *cot_first))]
    for m in range(1, MICRO):
        kept.append(mix(m, after(x_all[m], *cot_first), *ffn_mine[:1]))
        part = add_single(kept[m][6], w_head).astype(low)
        attn_out.append(ctx_sum(after(part, *ffn_mine)))
    cot_second = gather_second(*cot_first)
    def enter(m):
        hidden = rows_in[m] + attn_out[m].astype(jnp.float32)
        normed_two, pull_two = jax.vjp(layer_norm, hidden, norm_gains[1], norm_biases[1])
        two_own = normed_two.astype(low)
        return hidden, pull_two, two_own, gather_first(two_own)

    entered = [enter(0)]
    ffn_mine = lax.optimization_barrier(tuple(ffn_mine) + (entered[0][2],))[:-1]
    up_own, down_own = join_ffn(w_up, w_down, ffn_mine, [core_swap(x) for x in ffn_mine])
    cot_all = [
        place(
            (fsdp_size * tok_rows, width),
            [
                (cot_own, m * tok_rows, tok_rows, 0, 0),
                (cot_first[0], m * tok_rows, tok_rows, tok_rows, 0),
                (cot_second[m], 0, tok_rows, 2 * tok_rows, 0),
                (cot_first[1], m * tok_rows, tok_rows, 3 * tok_rows, 0),
            ],
        )
        for m in range(MICRO)
    ]

    outs = [None] * MICRO
    grad_attn = []
    grad_hidden = []
    ffn_kept = []
    norm_two_terms = []

    for m in range(MICRO):
        hidden, pull_two, two_own, two_first = entered[m]
        if m == 0:
            two_first = lax.optimization_barrier(tuple(two_first) + (up_own, down_own))[:2]
            two_second = gather_second(*two_first)
        two_second = lax.optimization_barrier(tuple(two_second) + tuple(cot_all))[:2]
        two_all = by_offset(two_own, *two_first, *two_second)
        active, slope = smooth_parts(add_single(two_all, up_own))
        active_low, slope = lax.optimization_barrier((active.astype(low), slope))
        grad_up = (back_rows(cot_all[m], down_own) * slope).astype(low)
        norm_part = back_rows(grad_up, up_own).astype(low)
        sent = rows_first(norm_part)
        later = ()
        if m + 1 < MICRO:
            attn_out[m + 1] = after(attn_out[m + 1], norm_part)
            entered.append(enter(m + 1))
            sent = lax.optimization_barrier(tuple(sent) + (entered[m + 1][2],))[:2]
            two_second = gather_second(*entered[m + 1][3])
            later = two_second
        grad_norm_two = after(rows_second(norm_part, *sent), *grad_attn[-1:], *later)
        grad_ln, gain_two, bias_two = pull_two(grad_norm_two)
        norm_two_terms.append((gain_two, bias_two))
        total = grad_rows[m] + grad_ln
        grad_hidden.append(total)
        grad_attn.append(total.astype(low))
        ffn_kept.append((two_all, grad_up, active_low, hidden))

    grad_all = [lax.all_gather(grad_attn[m], "ctx", axis=0, tiled=True) for m in range(MICRO)]

    def unmix(m, grad_now):
        table, query, key, value, attend, mix_pull, mixed_low = kept[m]
        grad_mixed = back_rows(grad_now, w_head)
        grad_gate, grad_ret = mix_pull(grad_mixed)
        ret_low = grad_ret.astype(low)
        grad_scores = (contract_rows(ret_low, value) * table).astype(low)
        grad_query = add_single(grad_scores, key).astype(low)
        grad_key = contract_cols(grad_scores, query).astype(low)
        grad_value = contract_cols(attend, ret_low).astype(low)
        return jnp.concatenate([grad_query, grad_key, grad_value, grad_gate.astype(low)], axis=1)

    terms = []
    sums = []
    fill = ()
    for m in range(MICRO):
        grad_now = after(grad_all[m], *(grad_attn[1:] if m == 0 else terms[-1:]), *fill)
        grad_in = unmix(m, grad_now)
        part = back_rows(grad_in, w_in).astype(low)
        terms.append(part)
        sums.append(ctx_sum(after(part, *grad_all[m + 1 :], *sums[-1:])))
        x_now, grad_in = lax.optimization_barrier((x_all[m], grad_in, part))[:2]
        in_now = contract_cols(x_now, grad_in)
        if m == 0:
            in_term = in_now
            sums[m] = after(sums[m], in_term)
            ready = [after(ffn_kept[n][2], part, grad_attn[n]) for n in range(MICRO)]
            fill = tuple(add_single(ready[n], down_own).astype(low) for n in range(MICRO))
        else:
            in_term = (in_term + in_now).astype(low)
    in_view = in_term.reshape(ctx_size, fsdp_size, share, -1)
    in_blocks_out = [pick(in_view, fsdp_rank ^ j, 1, 1)[:, 0] for j in range(fsdp_size)]
    in_sent = reduce_first(in_blocks_out)
    up_grad = sum(contract_cols(k[0], after(k[1], in_term)) for k in ffn_kept).astype(low)
    down_grad = sum(
        contract_cols(after(ready[n], up_grad), cot_all[n]) for n in range(MICRO)
    ).astype(low)
    up_half, groups = chip_sum(up_grad)
    down_half, groups = chip_sum(down_grad)
    sums[-1] = after(sums[-1], up_half, *in_sent)
    over_z = dict(scatter_dimension=0, tiled=True, axis_index_groups=groups)
    up_sum = lax.psum_scatter(after(up_half, sums[-1]), "ctx", **over_z)
    down_sum = lax.psum_scatter(after(down_half, sums[-1]), "ctx", **over_z)
    in_sum = reduce_second(in_blocks_out, *in_sent).astype(low)
    in_mine = lax.all_to_all(in_sum, "ctx", split_axis=0, concat_axis=0, tiled=True)
    for n in range(MICRO):
        ffn_part = after(fill[n], *in_sent)
        outs[n] = (ffn_kept[n][3] + rows_second(ffn_part, *rows_first(ffn_part))).astype(low)
    out_term = sum(
        contract_cols(after(kept[m][6], down_grad), grad_all[m]) for m in range(MICRO)
    ).astype(low)

    grad_tokens = []
    norm_one_terms = []
    for m in range(MICRO):
        grad_ln, gain_one, bias_one = norm_one[m][1](sums[m].astype(jnp.float32))
        norm_one_terms.append((gain_one, bias_one))
        grad_tokens.append(grad_hidden[m] + grad_ln)

    gain_rows = [sum(t[0] for t in norm_one_terms), sum(t[0] for t in norm_two_terms)]
    bias_rows = [sum(t[1] for t in norm_one_terms), sum(t[1] for t in norm_two_terms)]
    norm_sums = sum_everywhere(jnp.stack(gain_rows + bias_rows))
    out_term = after(out_term, in_sum)
    rows = DV // fsdp_size
    out_blocks = [pick(out_term, fsdp_rank ^ j, rows, 0) for j in range(fsdp_size)]
    g_out = reduce_second(out_blocks, *reduce_first(out_blocks))

    up_view = up_sum.reshape(fsdp_size, share, -1)
    pieces = [lax.dynamic_index_in_dim(up_view, fsdp_rank, 0, keepdims=False)]
    for bit in range(1, fsdp_size):
        pieces.append(
            xy_swap(lax.dynamic_index_in_dim(up_view, fsdp_rank ^ bit, 0, keepdims=False), bit)
        )
    in_mine = lax.optimization_barrier((in_mine, norm_sums) + tuple(pieces))[0]
    down_sum = after(down_sum, in_mine)
    def by_head(first, size):
        part = in_mine[:, :, first : first + size].transpose(1, 0, 2)
        return part.reshape(share, -1).astype(jnp.float32) * grad_scale

    g_query = by_head(0, DK)
    g_key = by_head(DK, DK)
    g_value = by_head(2 * DK, DV)
    g_gate = by_head(2 * DK + DV, DV)

    pieces = [p.reshape(share, ctx_size, -1) for p in in_rank_order(pieces, fsdp_rank)]
    g_up = jnp.stack(pieces, axis=2).reshape(share, FF).astype(jnp.float32) * grad_scale

    norm_sums = pick(norm_sums, ctx_rank * fsdp_size + fsdp_rank, share, 1) * grad_scale
    return (
        jnp.stack(outs)[:, None],
        jnp.stack(grad_tokens)[:, None],
        g_query,
        g_key,
        g_value,
        g_gate,
        g_out * grad_scale,
        g_up,
        down_sum.astype(jnp.float32) * grad_scale,
        norm_sums[:2],
        norm_sums[2:],
    )


def solution(mesh):
    in_specs = (
        P(None, "fsdp", "ctx", None),
        P(None, "fsdp", "ctx", None),
        P("fsdp", None),
        P("fsdp", None),
        P("fsdp", None),
        P("fsdp", None),
        P("fsdp", None),
        P("fsdp", None),
        P("fsdp", None),
        P(),
        P(),
        P(),
        P(None, "fsdp", None),
    )
    out_specs = (
        P(None, "fsdp", "ctx", None),
        P(None, "fsdp", "ctx", None),
        P(("ctx", "fsdp"), None),
        P(("ctx", "fsdp"), None),
        P(("ctx", "fsdp"), None),
        P(("ctx", "fsdp"), None),
        P(("ctx", "fsdp"), None),
        P(("ctx", "fsdp"), None),
        P(("ctx", "fsdp"), None),
        P(None, ("ctx", "fsdp")),
        P(None, ("ctx", "fsdp")),
    )
    by_heads = mesh.shape["ctx"] == HEADS and mesh.shape["fsdp"] == 4
    chosen = body_heads if by_heads else body
    return jax.shard_map(chosen, mesh=mesh, in_specs=in_specs, out_specs=out_specs, check_vma=False)
```

```python
import jax
import jax.numpy as jnp
from jax import lax
from jax.experimental import pallas as pl
from jax.sharding import PartitionSpec as P

HEADS = 8
DK = 256
DV = 512
FF = 4096
MICRO = 2
QW = 2048
VW = 4096
BLOCK = 64


epsilon = 1e-05
group_floor = 1.0


def layer_norm(values, gain_row, offset):
    center = jnp.mean(values, axis=-1, keepdims=True)
    centred = values - center
    spread = jnp.mean(centred * centred, axis=-1, keepdims=True)
    return centred * lax.rsqrt(spread + epsilon) * gain_row + offset


def gated_mix(gate_pre, retained):
    number = retained.shape[0]
    grouped = retained.reshape(number, -1, DV)
    center = jnp.mean(grouped, axis=-1, keepdims=True)
    centred = grouped - center
    spread = jnp.mean(centred * centred, axis=-1, keepdims=True)
    normed = (centred * lax.rsqrt(spread + group_floor)).reshape(number, -1)
    return jax.nn.silu(gate_pre) * normed


def smooth_act(values):
    return jax.nn.gelu(values, approximate=False)


def stored_positions(block_deal, full_length, block_size):
    stored = jnp.arange(full_length, dtype=jnp.int32)
    block_ids = stored // block_size
    slots_all = jnp.arange(block_deal.shape[0], dtype=jnp.int32)
    picked = jnp.sum(
        jnp.where(block_ids[:, None] == slots_all[None, :], block_deal[None, :], 0),
        axis=1,
        dtype=jnp.int32,
    )
    return picked * block_size + stored % block_size


def document_ids(positions, doc_sizes):
    starts = jnp.cumsum(doc_sizes, dtype=jnp.int32) - doc_sizes
    return (
        jnp.sum((positions[:, None] >= starts[None, :]).astype(jnp.int32), axis=1, dtype=jnp.int32)
        - 1
    )


def decay_table(query_pos, query_doc, key_pos, key_doc, decay_log, scaling):
    keeping = (query_pos[:, None] >= key_pos[None, :]) & (query_doc[:, None] == key_doc[None, :])
    spacing = jnp.where(keeping, (query_pos[:, None] - key_pos[None, :]).astype(jnp.float32), 0.0)
    factor = jnp.exp(decay_log[:, None, None] * spacing[None])
    return jnp.where(keeping[None], factor * scaling, 0.0)


def contract_rows(left, right):
    return lax.dot_general(
        left, right, (((1,), (1,)), ((), ())), preferred_element_type=jnp.float32
    )


def contract_cols(left, right):
    return lax.dot_general(
        left, right, (((0,), (0,)), ((), ())), preferred_element_type=jnp.float32
    )


def add_single(left, weight_piece):
    return jnp.dot(left, weight_piece, preferred_element_type=jnp.float32)


def back_rows(left, weight_piece):
    return contract_rows(left, weight_piece)


def weight_term(kept_acts, number):
    normed_one, grads_in, normed_two, grads_up, mixed_all, grads_attn, active_all, grads_ffn = (
        kept_acts
    )
    pieces = [
        contract_cols(normed_one, grads_in),
        contract_cols(normed_two, grads_up),
        contract_cols(mixed_all, grads_attn).reshape(number, -1),
        contract_cols(active_all, grads_ffn).reshape(number, -1),
    ]
    return jnp.concatenate(pieces, axis=1)


def body(
    tokens,
    cotangent,
    w_query,
    w_key,
    w_value,
    w_gate,
    w_out,
    w_up,
    w_down,
    norm_gains,
    norm_biases,
    block_deal,
    doc_lengths,
):
    ctx_size = lax.axis_size("ctx")
    tok_rows = tokens.shape[2]
    full_length = tok_rows * ctx_size
    model_width = tokens.shape[3]
    share_rows = model_width // lax.axis_size(("ctx", "fsdp"))
    grad_scale = float(MICRO * lax.axis_size("fsdp") * full_length) ** (-0.5)
    own_start = lax.axis_index("ctx") * tok_rows
    key_pos = stored_positions(block_deal, full_length, BLOCK)
    query_pos = lax.dynamic_slice_in_dim(key_pos, own_start, tok_rows)
    decay_log = jnp.log1p(-jnp.exp2(-5.0 - jnp.arange(HEADS).astype(jnp.float32)))
    scaling = DK ** (-0.5)
    out_list = []
    grad_list = []
    weight_sum = None
    gain_sum = jnp.zeros((2, model_width), jnp.float32)
    bias_sum = jnp.zeros((2, model_width), jnp.float32)
    for batch_index in range(MICRO):
        rows_in = tokens[batch_index, 0].astype(jnp.float32)
        grad_rows = cotangent[batch_index, 0].astype(jnp.float32)
        key_doc = document_ids(key_pos, doc_lengths[batch_index, 0])
        query_doc = lax.dynamic_slice_in_dim(key_doc, own_start, tok_rows)
        table = decay_table(query_pos, query_doc, key_pos, key_doc, decay_log, scaling)
        normed_one, norm_pull_one = jax.vjp(layer_norm, rows_in, norm_gains[0], norm_biases[0])
        low_one = normed_one.astype(jnp.bfloat16)
        pieces = (
            lax.all_gather(w_query, "fsdp", axis=0, tiled=True),
            lax.all_gather(w_key, "fsdp", axis=0, tiled=True),
            lax.all_gather(w_value, "fsdp", axis=0, tiled=True),
            lax.all_gather(w_gate, "fsdp", axis=0, tiled=True),
        )
        query_f, key_f, value_f, gate_pre = tuple(
            (
                jnp.dot(low_one, weight_piece, preferred_element_type=jnp.float32)
                for weight_piece in pieces
            )
        )
        query_low = query_f.astype(jnp.bfloat16)
        key_low = key_f.astype(jnp.bfloat16)
        value_low = value_f.astype(jnp.bfloat16)
        keys_all, values_all = (
            lax.all_gather(key_low, "ctx", axis=0, tiled=True),
            lax.all_gather(value_low, "ctx", axis=0, tiled=True),
        )
        query_heads = query_low.reshape(tok_rows, HEADS, DK)
        key_heads = keys_all.reshape(full_length, HEADS, DK)
        value_heads = values_all.reshape(full_length, HEADS, DV)
        scores = jnp.einsum(
            "thd,shd->hts", query_heads, key_heads, preferred_element_type=jnp.float32
        )
        attend = (scores * table).astype(jnp.bfloat16)
        retained = jnp.einsum(
            "hts,shd->thd", attend, value_heads, preferred_element_type=jnp.float32
        ).reshape(tok_rows, VW)
        mixed, mix_pull = jax.vjp(gated_mix, gate_pre, retained)
        mixed_low = mixed.astype(jnp.bfloat16)
        attn_out = add_single(mixed_low, lax.all_gather(w_out, "fsdp", axis=0, tiled=True))
        hidden = rows_in + attn_out
        normed_two, norm_pull_two = jax.vjp(layer_norm, hidden, norm_gains[1], norm_biases[1])
        low_two = normed_two.astype(jnp.bfloat16)
        up_pre = add_single(low_two, lax.all_gather(w_up, "fsdp", axis=0, tiled=True))
        active, act_pull = jax.vjp(smooth_act, up_pre)
        active_low = active.astype(jnp.bfloat16)
        ffn_out = add_single(active_low, lax.all_gather(w_down, "fsdp", axis=0, tiled=True))
        out_list.append((hidden + ffn_out).astype(jnp.bfloat16))
        grad_ffn = grad_rows.astype(jnp.bfloat16)
        grad_act = back_rows(grad_ffn, lax.all_gather(w_down, "fsdp", axis=0, tiled=True))
        grad_up = act_pull(grad_act)[0].astype(jnp.bfloat16)
        grad_norm_two = back_rows(grad_up, lax.all_gather(w_up, "fsdp", axis=0, tiled=True))
        grad_hidden_ln, grad_gain_two, grad_bias_two = norm_pull_two(grad_norm_two)
        grad_hidden = grad_rows + grad_hidden_ln
        grad_attn = grad_hidden.astype(jnp.bfloat16)
        grad_mixed = back_rows(grad_attn, lax.all_gather(w_out, "fsdp", axis=0, tiled=True))
        grad_gate_f, grad_ret_f = mix_pull(grad_mixed)
        grad_gate = grad_gate_f.astype(jnp.bfloat16)
        ret_low = grad_ret_f.astype(jnp.bfloat16)
        ret_heads = ret_low.reshape(tok_rows, HEADS, DV)
        grad_attend = jnp.einsum(
            "thd,shd->hts", ret_heads, value_heads, preferred_element_type=jnp.float32
        )
        grad_scores = (grad_attend * table).astype(jnp.bfloat16)
        grad_query = (
            jnp.einsum("hts,shd->thd", grad_scores, key_heads, preferred_element_type=jnp.float32)
            .reshape(tok_rows, QW)
            .astype(jnp.bfloat16)
        )
        key_part = jnp.einsum(
            "hts,thd->shd", grad_scores, query_heads, preferred_element_type=jnp.float32
        ).reshape(tok_rows * lax.axis_size("ctx"), QW)
        value_part = jnp.einsum(
            "hts,thd->shd", attend, ret_heads, preferred_element_type=jnp.float32
        ).reshape(tok_rows * lax.axis_size("ctx"), VW)
        key_value_sum = lax.psum_scatter(
            jnp.concatenate([key_part, value_part], axis=1).astype(jnp.bfloat16),
            "ctx",
            scatter_dimension=0,
            tiled=True,
        ).astype(jnp.float32)
        grad_key = key_value_sum[:, :QW].astype(jnp.bfloat16)
        grad_value = key_value_sum[:, QW:].astype(jnp.bfloat16)
        term_now = (
            contract_rows(grad_query, lax.all_gather(w_query, "fsdp", axis=0, tiled=True))
            + contract_rows(grad_key, lax.all_gather(w_key, "fsdp", axis=0, tiled=True))
            + contract_rows(grad_value, lax.all_gather(w_value, "fsdp", axis=0, tiled=True))
            + contract_rows(grad_gate, lax.all_gather(w_gate, "fsdp", axis=0, tiled=True))
        )
        grad_rows_ln, grad_gain_one, grad_bias_one = norm_pull_one(term_now)
        grad_list.append(grad_hidden + grad_rows_ln)
        gain_sum = gain_sum + jnp.stack([grad_gain_one, grad_gain_two])
        bias_sum = bias_sum + jnp.stack([grad_bias_one, grad_bias_two])
        kept_now = (
            low_one,
            jnp.concatenate([grad_query, grad_key, grad_value, grad_gate], axis=1),
            low_two,
            grad_up,
            mixed_low,
            grad_attn,
            active_low,
            grad_ffn,
        )
        term_sum = lax.psum_scatter(
            weight_term(kept_now, share_rows * lax.axis_size(("ctx", "fsdp"))),
            ("ctx", "fsdp"),
            scatter_dimension=0,
            tiled=True,
        )
        weight_sum = term_sum if weight_sum is None else weight_sum + term_sum
    weight_sum = weight_sum * grad_scale
    bounds = [QW, 2 * QW, 2 * QW + VW, 2 * QW + 2 * VW, 2 * QW + 2 * VW + FF, 2 * QW + 3 * VW + FF]
    g_query, g_key, g_value, g_gate, g_up, g_out_flat, g_down_flat = jnp.split(
        weight_sum, bounds, axis=1
    )
    g_out = g_out_flat.reshape(share_rows * (VW // model_width), model_width)
    g_down = g_down_flat.reshape(share_rows * (FF // model_width), model_width)
    gain_grads, bias_grads = (
        lax.psum_scatter(gain_sum, ("ctx", "fsdp"), scatter_dimension=1, tiled=True),
        lax.psum_scatter(bias_sum, ("ctx", "fsdp"), scatter_dimension=1, tiled=True),
    )
    gain_grads = gain_grads * grad_scale
    bias_grads = bias_grads * grad_scale
    output = jnp.stack(out_list)[:, None]
    grad_tokens = jnp.stack(grad_list)[:, None]
    return (
        output,
        grad_tokens,
        g_query,
        g_key,
        g_value,
        g_gate,
        g_out,
        g_up,
        g_down,
        gain_grads,
        bias_grads,
    )


def xy_swap(x, bit):
    return lax.ppermute(x, "fsdp", [(i, i ^ bit) for i in range(lax.axis_size("fsdp"))])


def core_swap(x):
    return lax.ppermute(x, "ctx", [(i, i ^ 1) for i in range(lax.axis_size("ctx"))])


def after(x, *earlier):
    return lax.optimization_barrier((x,) + tuple(earlier))[0]


def place(shape, items):
    arrays = []
    for item in items:
        if not any(item[0] is a for a in arrays):
            arrays.append(item[0])
    slots = [[item[0] is a for a in arrays].index(True) for item in items]
    kind = arrays[0].dtype

    def kernel(*refs):
        out = refs[len(arrays)]
        rank = lax.axis_index("fsdp")
        core = lax.axis_index("ctx") % 2
        for number, (array, start, rows, row, column) in enumerate(items):
            width = array.shape[1]
            step = min(rows, 64)
            source = refs[slots[number]]
            base = row(rank, core) if callable(row) else row

            def copy(first, width=width, step=step, source=source, base=base, start=start, rows=rows):
                def one(turn, carry):
                    place_in = pl.multiple_of(start + turn * step, step)
                    place_out = pl.multiple_of(base + turn * step, step)
                    out[pl.ds(place_out, step), first : first + width] = source[
                        pl.ds(place_in, step), :
                    ]
                    return carry

                lax.fori_loop(0, rows // step, one, 0)

            if callable(column):
                for which in range(2):
                    pl.when(core == which)(lambda which=which: copy(column(rank, which)))
            else:
                copy(column)

    size = shape[0] * shape[1] * jnp.dtype(kind).itemsize
    return pl.pallas_call(
        kernel,
        out_shape=jax.ShapeDtypeStruct(shape, kind),
        cost_estimate=pl.CostEstimate(flops=0, bytes_accessed=2 * size, transcendentals=0),
    )(*arrays)


def gather_first(x):
    return xy_swap(x, 1), xy_swap(x, 2)


def gather_second(first, second):
    half = first.shape[0] // 2
    return xy_swap(first[:half], 2), xy_swap(second[half:], 1)


def by_offset(x, first, second, low_part, high_part):
    rows, half = x.shape[0], x.shape[0] // 2
    return place(
        (4 * rows, x.shape[1]),
        [
            (x, 0, rows, 0, 0),
            (first, 0, rows, rows, 0),
            (low_part, 0, half, 2 * rows, 0),
            (high_part, 0, half, 2 * rows + half, 0),
            (second, 0, rows, 3 * rows, 0),
        ],
    )


def by_rank(x, first, second, low_part, high_part):
    rows, half = x.shape[0], x.shape[0] // 2
    return place(
        (4 * rows, x.shape[1]),
        [
            (x, 0, rows, lambda f, c: f * rows, 0),
            (first, 0, rows, lambda f, c: (f ^ 1) * rows, 0),
            (low_part, 0, half, lambda f, c: (f ^ 3) * rows, 0),
            (high_part, 0, half, lambda f, c: (f ^ 3) * rows + half, 0),
            (second, 0, rows, lambda f, c: (f ^ 2) * rows, 0),
        ],
    )


def rows_first(part):
    rows, half = part.shape[0] // 4, part.shape[1] // 2
    return xy_swap(part[rows : 3 * rows, :half], 1), xy_swap(part[2 * rows :, half:], 2)


def rows_second(part, left_in, right_in):
    rows, half = part.shape[0] // 4, part.shape[1] // 2
    wide = lambda v: v.astype(jnp.float32)
    left_far = wide(part[3 * rows :, :half]) + wide(left_in[rows:])
    right_far = wide(part[rows : 2 * rows, half:]) + wide(right_in[:rows])
    left_last = xy_swap(left_far.astype(jnp.bfloat16), 2)
    right_last = xy_swap(right_far.astype(jnp.bfloat16), 1)
    left = wide(part[:rows, :half]) + wide(left_in[:rows]) + wide(left_last)
    right = wide(part[:rows, half:]) + wide(right_in[rows:]) + wide(right_last)
    return jnp.concatenate([left, right], axis=1)


def reduce_first(blocks):
    half = blocks[0].shape[-1] // 2
    left_in = xy_swap(jnp.stack([blocks[1][..., :half], blocks[3][..., :half]]), 1)
    right_in = xy_swap(jnp.stack([blocks[2][..., half:], blocks[3][..., half:]]), 2)
    return left_in, right_in


def reduce_second(blocks, left_in, right_in):
    half = blocks[0].shape[-1] // 2
    wide = lambda v: v.astype(jnp.float32)
    left_far = wide(blocks[2][..., :half]) + wide(left_in[1])
    right_far = wide(blocks[1][..., half:]) + wide(right_in[1])
    left_last = xy_swap(left_far.astype(jnp.bfloat16), 2)
    right_last = xy_swap(right_far.astype(jnp.bfloat16), 1)
    left = wide(blocks[0][..., :half]) + wide(left_in[0]) + wide(left_last)
    right = wide(blocks[0][..., half:]) + wide(right_in[0]) + wide(right_last)
    return jnp.concatenate([left, right], axis=-1)


def sum_everywhere(x):
    for axis in ("ctx", "fsdp"):
        size = lax.axis_size(axis)
        bit = 1
        while bit < size:
            x = x + lax.ppermute(x, axis, [(i, i ^ bit) for i in range(size)])
            bit *= 2
    return x


def in_rank_order(blocks, rank):
    odd = (rank % 2) == 1
    upper = (rank // 2) == 1
    one = [
        jnp.where(odd, blocks[1], blocks[0]),
        jnp.where(odd, blocks[0], blocks[1]),
        jnp.where(odd, blocks[3], blocks[2]),
        jnp.where(odd, blocks[2], blocks[3]),
    ]
    return [
        jnp.where(upper, one[2], one[0]),
        jnp.where(upper, one[3], one[1]),
        jnp.where(upper, one[0], one[2]),
        jnp.where(upper, one[1], one[3]),
    ]


def pick(x, index, size, axis):
    return lax.dynamic_slice_in_dim(x, index * size, size, axis)


def head_columns(w_query, w_key, w_value, w_gate, ctx_rank):
    return jnp.concatenate(
        [
            pick(w_query, ctx_rank, DK, 1),
            pick(w_key, ctx_rank, DK, 1),
            pick(w_value, ctx_rank, DV, 1),
            pick(w_gate, ctx_rank, DV, 1),
        ],
        axis=1,
    )


def out_pieces(w_out, ctx_rank, fsdp_rank, fsdp_size):
    rows = DV // fsdp_size
    start = (ctx_rank % 2) * DV
    return [
        lax.dynamic_slice_in_dim(w_out, start + (fsdp_rank ^ bit) * rows, rows, 0)
        for bit in range(fsdp_size)
    ]


def scatter_quarters(cuts, ctx_size, fsdp_size):
    parts = [cuts[0]]
    for bit in range(1, fsdp_size):
        pairs = [
            (c * fsdp_size + c // 2, c * fsdp_size + ((c // 2) ^ bit)) for c in range(ctx_size)
        ]
        parts.append(lax.ppermute(cuts[bit], ("ctx", "fsdp"), pairs))
    return parts


def choose_quarter(parts, ctx_rank, fsdp_rank):
    quarter = parts[0]
    for bit in range(1, len(parts)):
        quarter = jnp.where((fsdp_rank ^ (ctx_rank // 2)) == bit, parts[bit], quarter)
    return quarter


def copy_block(target, row, column, source, row_in, column_in, rows, width):
    step = min(rows, 64)

    def one(turn, carry):
        place_in = pl.multiple_of(row_in + turn * step, step)
        place_out = pl.multiple_of(row + turn * step, step)
        taken = source[pl.ds(place_in, step), pl.ds(column_in, width)]
        target[pl.ds(place_out, step), pl.ds(column, width)] = taken
        return carry

    lax.fori_loop(0, rows // step, one, 0)


def cut_ffn(w_up, w_down):
    ctx_size, fsdp_size = lax.axis_size("ctx"), lax.axis_size("fsdp")
    rows, width = w_up.shape[0], w_down.shape[1]
    unit, half = FF // (ctx_size * fsdp_size), ctx_size // 2
    wide = half * unit
    fourth = width // 4

    def kernel(up, down, *outs):
        rank = lax.axis_index("fsdp")
        core = lax.axis_index("ctx") % 2
        for number in range(fsdp_size - 1):
            other = rank ^ (number + 1)
            for i in range(half):
                column = pl.multiple_of(((core * half + i) * fsdp_size + other) * unit, unit)
                copy_block(outs[number], 0, i * unit, up, 0, column, rows, unit)
            for i in range(2):
                for q in range(2):
                    column = pl.multiple_of(core * 2 * fourth + q * fourth, fourth)
                    row = (i * fsdp_size + other) * unit
                    copy_block(
                        outs[number], (2 * i + q) * unit, wide, down, row, column, unit, fourth
                    )

    kind = jax.ShapeDtypeStruct((rows, wide + fourth), w_up.dtype)
    return list(pl.pallas_call(kernel, out_shape=[kind] * (fsdp_size - 1))(w_up, w_down))


def join_ffn(w_up, w_down, mine, other):
    ctx_size, fsdp_size = lax.axis_size("ctx"), lax.axis_size("fsdp")
    rows, width = w_up.shape[0], w_down.shape[1]
    unit, half = FF // (ctx_size * fsdp_size), ctx_size // 2
    wide = half * unit
    fourth = width // 4

    def kernel(up, down, *refs):
        up_out, down_out = refs[2 * len(mine) :]
        rank = lax.axis_index("fsdp")
        core = lax.axis_index("ctx") % 2
        for i in range(ctx_size):
            column = pl.multiple_of((i * fsdp_size + rank) * unit, unit)
            copy_block(up_out, rank * rows, i * unit, up, 0, column, rows, unit)
        for i in range(2):
            copy_block(
                down_out, (2 * rank + i) * unit, 0, down, (i * fsdp_size + rank) * unit, 0, unit, width
            )
        for number in range(2 * len(mine)):
            source = rank ^ (number % len(mine) + 1)
            part = core if number < len(mine) else 1 - core
            column = pl.multiple_of(part * wide, wide)
            copy_block(up_out, source * rows, column, refs[number], 0, 0, rows, wide)
            for i in range(2):
                for q in range(2):
                    column = pl.multiple_of(part * 2 * fourth + q * fourth, fourth)
                    row = (2 * source + i) * unit
                    copy_block(
                        down_out, row, column, refs[number], (2 * i + q) * unit, wide, unit, fourth
                    )

    shapes = [
        jax.ShapeDtypeStruct((fsdp_size * rows, FF // fsdp_size), w_up.dtype),
        jax.ShapeDtypeStruct((FF // fsdp_size, width), w_up.dtype),
    ]
    return pl.pallas_call(kernel, out_shape=shapes)(w_up, w_down, *mine, *other)


def smooth_parts(values):
    share = 0.5 + 0.5 * lax.erf(values * (0.5**0.5))
    density = jnp.exp(-0.5 * values * values) * ((0.5 / jnp.pi) ** 0.5)
    return values * share, share + values * density


def one_table(pos, doc, rate, scaling):
    keeping = (pos[:, None] >= pos[None, :]) & (doc[:, None] == doc[None, :])
    spacing = jnp.where(keeping, (pos[:, None] - pos[None, :]).astype(jnp.float32), 0.0)
    return jnp.where(keeping, jnp.exp(rate * spacing) * scaling, 0.0)


def ctx_sum(x):
    return lax.psum_scatter(x, "ctx", scatter_dimension=0, tiled=True)


def body_heads(
    tokens,
    cotangent,
    w_query,
    w_key,
    w_value,
    w_gate,
    w_out,
    w_up,
    w_down,
    norm_gains,
    norm_biases,
    block_deal,
    doc_lengths,
):
    low = jnp.bfloat16
    ctx_size = lax.axis_size("ctx")
    fsdp_size = lax.axis_size("fsdp")
    tok_rows = tokens.shape[2]
    full_length = tok_rows * ctx_size
    width = tokens.shape[3]
    share = width // (ctx_size * fsdp_size)
    grad_scale = float(MICRO * fsdp_size * full_length) ** (-0.5)
    ctx_rank = lax.axis_index("ctx")
    fsdp_rank = lax.axis_index("fsdp")
    pos = stored_positions(block_deal, full_length, BLOCK)
    rate = jnp.log1p(-jnp.exp2(-5.0 - ctx_rank.astype(jnp.float32)))
    scaling = DK ** (-0.5)

    own_in = head_columns(w_query, w_key, w_value, w_gate, ctx_rank)
    tokens = after(tokens, own_in)
    rows_in = []
    norm_one = []
    x_own = []
    for m in range(MICRO):
        rows_in.append(after(tokens[m, 0], *x_own[-1:]).astype(jnp.float32))
        norm_one.append(jax.vjp(layer_norm, rows_in[m], norm_gains[0], norm_biases[0]))
        x_own.append(norm_one[m][0].astype(low))
    grad_rows = [cotangent[m, 0].astype(jnp.float32) for m in range(MICRO)]
    x_all = [lax.all_gather(x, "ctx", axis=0, tiled=True) for x in x_own]
    in_first = gather_first(own_in)
    ffn_cut = cut_ffn(w_up, w_down)
    out_cut = out_pieces(w_out, ctx_rank, fsdp_rank, fsdp_size)
    in_first = lax.optimization_barrier(tuple(in_first) + tuple(ffn_cut) + tuple(out_cut))[:2]
    in_second = gather_second(*in_first)
    w_in = by_rank(own_in, *in_first, *in_second)
    out_cut = lax.optimization_barrier(tuple(out_cut) + tuple(in_first))[: len(out_cut)]
    out_parts = scatter_quarters(out_cut, ctx_size, fsdp_size)

    def mix(m, x_now, *earlier):
        doc = document_ids(pos, doc_lengths[m, 0])
        table = one_table(pos, doc, rate, scaling)
        joint = jnp.dot(x_now, w_in[:, : 2 * DK + DV], preferred_element_type=jnp.float32).astype(low)
        joint = after(joint, *earlier)
        gate_pre = jnp.dot(x_now, w_in[:, 2 * DK + DV :], preferred_element_type=jnp.float32)
        query, key, value = joint[:, :DK], joint[:, DK : 2 * DK], joint[:, 2 * DK :]
        attend = (contract_rows(query, key) * table).astype(low)
        retained = add_single(attend, value)
        mixed, mix_pull = jax.vjp(gated_mix, gate_pre, retained)
        return table, query, key, value, attend, mix_pull, mixed.astype(low)

    kept = [mix(0, x_all[0])]
    out_parts = lax.optimization_barrier(tuple(out_parts) + (kept[0][4],))[:-1]
    quarter = choose_quarter(out_parts, ctx_rank, fsdp_rank)
    out_first = gather_first(quarter)
    out_second = gather_second(*out_first)
    w_head = by_rank(quarter, *out_first, *out_second)
    cot_own = after(cotangent.reshape(MICRO * tok_rows, width), *out_first)
    cot_first = gather_first(cot_own)
    ffn_cut = lax.optimization_barrier(tuple(ffn_cut) + tuple(out_second))[: len(ffn_cut)]
    ffn_mine = [xy_swap(ffn_cut[bit - 1], bit) for bit in range(1, fsdp_size)]
    part = add_single(kept[0][6], w_head).astype(low)
    attn_out = [ctx_sum(after(part, *x_all[1:], *cot_first))]
    for m in range(1, MICRO):
        kept.append(mix(m, after(x_all[m], *cot_first), *ffn_mine[:1]))
        part = add_single(kept[m][6], w_head).astype(low)
        attn_out.append(ctx_sum(after(part, *ffn_mine)))
    cot_second = gather_second(*cot_first)
    def enter(m):
        hidden = rows_in[m] + attn_out[m].astype(jnp.float32)
        normed_two, pull_two = jax.vjp(layer_norm, hidden, norm_gains[1], norm_biases[1])
        two_own = normed_two.astype(low)
        return hidden, pull_two, two_own, gather_first(two_own)

    ffn_other = [core_swap(x) for x in ffn_mine]
    attn_out[0] = after(attn_out[0], *ffn_other, *cot_second)
    entered = [enter(0)]
    up_own, down_own = join_ffn(w_up, w_down, ffn_mine, ffn_other)
    cot_all = [
        place(
            (fsdp_size * tok_rows, width),
            [
                (cot_own, m * tok_rows, tok_rows, 0, 0),
                (cot_first[0], m * tok_rows, tok_rows, tok_rows, 0),
                (cot_second[m], 0, tok_rows, 2 * tok_rows, 0),
                (cot_first[1], m * tok_rows, tok_rows, 3 * tok_rows, 0),
            ],
        )
        for m in range(MICRO)
    ]

    outs = [None] * MICRO
    grad_attn = []
    grad_hidden = []
    ffn_kept = []
    norm_two_terms = []

    for m in range(MICRO):
        hidden, pull_two, two_own, two_first = entered[m]
        if m == 0:
            two_first = lax.optimization_barrier(tuple(two_first) + (up_own, down_own))[:2]
            two_second = gather_second(*two_first)
        two_second = lax.optimization_barrier(tuple(two_second) + (cot_all[m],))[:2]
        two_all = by_offset(two_own, *two_first, *two_second)
        active, slope = smooth_parts(add_single(two_all, up_own))
        active_low, slope = lax.optimization_barrier((active.astype(low), slope))
        grad_up = (back_rows(cot_all[m], down_own) * slope).astype(low)
        norm_part = back_rows(grad_up, up_own).astype(low)
        sent = rows_first(norm_part)
        later = ()
        if m + 1 < MICRO:
            attn_out[m + 1] = after(attn_out[m + 1], *sent)
            entered.append(enter(m + 1))
            sent = lax.optimization_barrier(tuple(sent) + (entered[m + 1][2],))[:2]
            two_second = gather_second(*entered[m + 1][3])
            later = two_second
        grad_norm_two = after(rows_second(norm_part, *sent), *grad_attn[-1:], *later)
        grad_ln, gain_two, bias_two = pull_two(grad_norm_two)
        norm_two_terms.append((gain_two, bias_two))
        total = grad_rows[m] + grad_ln
        grad_hidden.append(total)
        grad_attn.append(total.astype(low))
        ffn_kept.append((two_all, grad_up, active_low, hidden))

    grad_all = [lax.all_gather(grad_attn[m], "ctx", axis=0, tiled=True) for m in range(MICRO)]

    def unmix(m, grad_now):
        table, query, key, value, attend, mix_pull, mixed_low = kept[m]
        grad_mixed = back_rows(grad_now, w_head)
        grad_gate, grad_ret = mix_pull(grad_mixed)
        ret_low = grad_ret.astype(low)
        grad_scores = (contract_rows(ret_low, value) * table).astype(low)
        grad_query = add_single(grad_scores, key).astype(low)
        grad_key = contract_cols(grad_scores, query).astype(low)
        grad_value = contract_cols(attend, ret_low).astype(low)
        return jnp.concatenate([grad_query, grad_key, grad_value, grad_gate.astype(low)], axis=1)

    terms = []
    sums = []
    fill = ()
    for m in range(MICRO):
        grad_now = after(grad_all[m], *(grad_attn[1:] if m == 0 else terms[-1:]), *fill)
        grad_in = unmix(m, grad_now)
        part = back_rows(grad_in, w_in).astype(low)
        terms.append(part)
        sums.append(ctx_sum(after(part, *grad_all[m + 1 :], *sums[-1:])))
        x_now, grad_in = lax.optimization_barrier((x_all[m], grad_in, part))[:2]
        in_now = contract_cols(x_now, grad_in)
        if m == 0:
            in_term = in_now
            sums[m] = after(sums[m], in_term)
            ready = [after(ffn_kept[n][2], part, grad_attn[n]) for n in range(MICRO)]
            fill = tuple(add_single(ready[n], down_own).astype(low) for n in range(MICRO))
        else:
            in_term = (in_term + in_now).astype(low)
    in_view = in_term.reshape(ctx_size, fsdp_size, share, -1)
    in_blocks_out = [pick(in_view, fsdp_rank ^ j, 1, 1)[:, 0] for j in range(fsdp_size)]
    in_sent = reduce_first(in_blocks_out)
    up_grad = sum(contract_cols(k[0], after(k[1], in_term)) for k in ffn_kept).astype(low)
    down_grad = sum(
        contract_cols(after(ready[n], up_grad), cot_all[n]) for n in range(MICRO)
    ).astype(low)
    sums[-1] = after(sums[-1], up_grad, down_grad, *in_sent)
    up_sum = ctx_sum(after(up_grad, sums[-1]))
    down_sum = ctx_sum(after(down_grad, sums[-1]))
    in_sum = reduce_second(in_blocks_out, *in_sent).astype(low)
    in_mine = lax.all_to_all(in_sum, "ctx", split_axis=0, concat_axis=0, tiled=True)
    out_term = sum(
        contract_cols(after(kept[m][6], down_grad), grad_all[m]) for m in range(MICRO)
    ).astype(low)

    grad_tokens = []
    norm_one_terms = []
    for m in range(MICRO):
        grad_ln, gain_one, bias_one = norm_one[m][1](sums[m].astype(jnp.float32))
        norm_one_terms.append((gain_one, bias_one))
        grad_tokens.append(grad_hidden[m] + grad_ln)

    gain_rows = [sum(t[0] for t in norm_one_terms), sum(t[0] for t in norm_two_terms)]
    bias_rows = [sum(t[1] for t in norm_one_terms), sum(t[1] for t in norm_two_terms)]
    norm_sums = sum_everywhere(jnp.stack(gain_rows + bias_rows))
    for n in range(MICRO):
        ffn_part = after(fill[n], norm_sums)
        outs[n] = (ffn_kept[n][3] + rows_second(ffn_part, *rows_first(ffn_part))).astype(low)
    out_term = after(out_term, in_sum, norm_sums)
    rows = DV // fsdp_size
    out_blocks = [pick(out_term, fsdp_rank ^ j, rows, 0) for j in range(fsdp_size)]
    g_out = reduce_second(out_blocks, *reduce_first(out_blocks))

    up_view = up_sum.reshape(fsdp_size, share, -1)
    pieces = [lax.dynamic_index_in_dim(up_view, fsdp_rank, 0, keepdims=False)]
    for bit in range(1, fsdp_size):
        pieces.append(
            xy_swap(lax.dynamic_index_in_dim(up_view, fsdp_rank ^ bit, 0, keepdims=False), bit)
        )
    in_mine = lax.optimization_barrier((in_mine, norm_sums) + tuple(pieces))[0]
    down_sum = after(down_sum, in_mine)
    def by_head(first, size):
        part = in_mine[:, :, first : first + size].transpose(1, 0, 2)
        return part.reshape(share, -1).astype(jnp.float32) * grad_scale

    g_query = by_head(0, DK)
    g_key = by_head(DK, DK)
    g_value = by_head(2 * DK, DV)
    g_gate = by_head(2 * DK + DV, DV)

    pieces = [p.reshape(share, ctx_size, -1) for p in in_rank_order(pieces, fsdp_rank)]
    g_up = jnp.stack(pieces, axis=2).reshape(share, FF).astype(jnp.float32) * grad_scale

    norm_sums = pick(norm_sums, ctx_rank * fsdp_size + fsdp_rank, share, 1) * grad_scale
    return (
        jnp.stack(outs)[:, None],
        jnp.stack(grad_tokens)[:, None],
        g_query,
        g_key,
        g_value,
        g_gate,
        g_out * grad_scale,
        g_up,
        down_sum.astype(jnp.float32) * grad_scale,
        norm_sums[:2],
        norm_sums[2:],
    )


def solution(mesh):
    in_specs = (
        P(None, "fsdp", "ctx", None),
        P(None, "fsdp", "ctx", None),
        P("fsdp", None),
        P("fsdp", None),
        P("fsdp", None),
        P("fsdp", None),
        P("fsdp", None),
        P("fsdp", None),
        P("fsdp", None),
        P(),
        P(),
        P(),
        P(None, "fsdp", None),
    )
    out_specs = (
        P(None, "fsdp", "ctx", None),
        P(None, "fsdp", "ctx", None),
        P(("ctx", "fsdp"), None),
        P(("ctx", "fsdp"), None),
        P(("ctx", "fsdp"), None),
        P(("ctx", "fsdp"), None),
        P(("ctx", "fsdp"), None),
        P(("ctx", "fsdp"), None),
        P(("ctx", "fsdp"), None),
        P(None, ("ctx", "fsdp")),
        P(None, ("ctx", "fsdp")),
    )
    by_heads = mesh.shape["ctx"] == HEADS and mesh.shape["fsdp"] == 4
    chosen = body_heads if by_heads else body
    return jax.shard_map(chosen, mesh=mesh, in_specs=in_specs, out_specs=out_specs, check_vma=False)
```

```python
import jax
import jax.numpy as jnp
from jax import lax
from jax.experimental import pallas as pl
from jax.sharding import PartitionSpec as P

HEADS = 8
DK = 256
DV = 512
FF = 4096
MICRO = 2
QW = 2048
VW = 4096
BLOCK = 64


epsilon = 1e-05
group_floor = 1.0


def layer_norm(values, gain_row, offset):
    center = jnp.mean(values, axis=-1, keepdims=True)
    centred = values - center
    spread = jnp.mean(centred * centred, axis=-1, keepdims=True)
    return centred * lax.rsqrt(spread + epsilon) * gain_row + offset


def gated_mix(gate_pre, retained):
    number = retained.shape[0]
    grouped = retained.reshape(number, -1, DV)
    center = jnp.mean(grouped, axis=-1, keepdims=True)
    centred = grouped - center
    spread = jnp.mean(centred * centred, axis=-1, keepdims=True)
    normed = (centred * lax.rsqrt(spread + group_floor)).reshape(number, -1)
    return jax.nn.silu(gate_pre) * normed


def smooth_act(values):
    return jax.nn.gelu(values, approximate=False)


def stored_positions(block_deal, full_length, block_size):
    stored = jnp.arange(full_length, dtype=jnp.int32)
    block_ids = stored // block_size
    slots_all = jnp.arange(block_deal.shape[0], dtype=jnp.int32)
    picked = jnp.sum(
        jnp.where(block_ids[:, None] == slots_all[None, :], block_deal[None, :], 0),
        axis=1,
        dtype=jnp.int32,
    )
    return picked * block_size + stored % block_size


def document_ids(positions, doc_sizes):
    starts = jnp.cumsum(doc_sizes, dtype=jnp.int32) - doc_sizes
    return (
        jnp.sum((positions[:, None] >= starts[None, :]).astype(jnp.int32), axis=1, dtype=jnp.int32)
        - 1
    )


def decay_table(query_pos, query_doc, key_pos, key_doc, decay_log, scaling):
    keeping = (query_pos[:, None] >= key_pos[None, :]) & (query_doc[:, None] == key_doc[None, :])
    spacing = jnp.where(keeping, (query_pos[:, None] - key_pos[None, :]).astype(jnp.float32), 0.0)
    factor = jnp.exp(decay_log[:, None, None] * spacing[None])
    return jnp.where(keeping[None], factor * scaling, 0.0)


def contract_rows(left, right):
    return lax.dot_general(
        left, right, (((1,), (1,)), ((), ())), preferred_element_type=jnp.float32
    )


def contract_cols(left, right):
    return lax.dot_general(
        left, right, (((0,), (0,)), ((), ())), preferred_element_type=jnp.float32
    )


def add_single(left, weight_piece):
    return jnp.dot(left, weight_piece, preferred_element_type=jnp.float32)


def back_rows(left, weight_piece):
    return contract_rows(left, weight_piece)


def weight_term(kept_acts, number):
    normed_one, grads_in, normed_two, grads_up, mixed_all, grads_attn, active_all, grads_ffn = (
        kept_acts
    )
    pieces = [
        contract_cols(normed_one, grads_in),
        contract_cols(normed_two, grads_up),
        contract_cols(mixed_all, grads_attn).reshape(number, -1),
        contract_cols(active_all, grads_ffn).reshape(number, -1),
    ]
    return jnp.concatenate(pieces, axis=1)


def body(
    tokens,
    cotangent,
    w_query,
    w_key,
    w_value,
    w_gate,
    w_out,
    w_up,
    w_down,
    norm_gains,
    norm_biases,
    block_deal,
    doc_lengths,
):
    ctx_size = lax.axis_size("ctx")
    tok_rows = tokens.shape[2]
    full_length = tok_rows * ctx_size
    model_width = tokens.shape[3]
    share_rows = model_width // lax.axis_size(("ctx", "fsdp"))
    grad_scale = float(MICRO * lax.axis_size("fsdp") * full_length) ** (-0.5)
    own_start = lax.axis_index("ctx") * tok_rows
    key_pos = stored_positions(block_deal, full_length, BLOCK)
    query_pos = lax.dynamic_slice_in_dim(key_pos, own_start, tok_rows)
    decay_log = jnp.log1p(-jnp.exp2(-5.0 - jnp.arange(HEADS).astype(jnp.float32)))
    scaling = DK ** (-0.5)
    out_list = []
    grad_list = []
    weight_sum = None
    gain_sum = jnp.zeros((2, model_width), jnp.float32)
    bias_sum = jnp.zeros((2, model_width), jnp.float32)
    for batch_index in range(MICRO):
        rows_in = tokens[batch_index, 0].astype(jnp.float32)
        grad_rows = cotangent[batch_index, 0].astype(jnp.float32)
        key_doc = document_ids(key_pos, doc_lengths[batch_index, 0])
        query_doc = lax.dynamic_slice_in_dim(key_doc, own_start, tok_rows)
        table = decay_table(query_pos, query_doc, key_pos, key_doc, decay_log, scaling)
        normed_one, norm_pull_one = jax.vjp(layer_norm, rows_in, norm_gains[0], norm_biases[0])
        low_one = normed_one.astype(jnp.bfloat16)
        pieces = (
            lax.all_gather(w_query, "fsdp", axis=0, tiled=True),
            lax.all_gather(w_key, "fsdp", axis=0, tiled=True),
            lax.all_gather(w_value, "fsdp", axis=0, tiled=True),
            lax.all_gather(w_gate, "fsdp", axis=0, tiled=True),
        )
        query_f, key_f, value_f, gate_pre = tuple(
            (
                jnp.dot(low_one, weight_piece, preferred_element_type=jnp.float32)
                for weight_piece in pieces
            )
        )
        query_low = query_f.astype(jnp.bfloat16)
        key_low = key_f.astype(jnp.bfloat16)
        value_low = value_f.astype(jnp.bfloat16)
        keys_all, values_all = (
            lax.all_gather(key_low, "ctx", axis=0, tiled=True),
            lax.all_gather(value_low, "ctx", axis=0, tiled=True),
        )
        query_heads = query_low.reshape(tok_rows, HEADS, DK)
        key_heads = keys_all.reshape(full_length, HEADS, DK)
        value_heads = values_all.reshape(full_length, HEADS, DV)
        scores = jnp.einsum(
            "thd,shd->hts", query_heads, key_heads, preferred_element_type=jnp.float32
        )
        attend = (scores * table).astype(jnp.bfloat16)
        retained = jnp.einsum(
            "hts,shd->thd", attend, value_heads, preferred_element_type=jnp.float32
        ).reshape(tok_rows, VW)
        mixed, mix_pull = jax.vjp(gated_mix, gate_pre, retained)
        mixed_low = mixed.astype(jnp.bfloat16)
        attn_out = add_single(mixed_low, lax.all_gather(w_out, "fsdp", axis=0, tiled=True))
        hidden = rows_in + attn_out
        normed_two, norm_pull_two = jax.vjp(layer_norm, hidden, norm_gains[1], norm_biases[1])
        low_two = normed_two.astype(jnp.bfloat16)
        up_pre = add_single(low_two, lax.all_gather(w_up, "fsdp", axis=0, tiled=True))
        active, act_pull = jax.vjp(smooth_act, up_pre)
        active_low = active.astype(jnp.bfloat16)
        ffn_out = add_single(active_low, lax.all_gather(w_down, "fsdp", axis=0, tiled=True))
        out_list.append((hidden + ffn_out).astype(jnp.bfloat16))
        grad_ffn = grad_rows.astype(jnp.bfloat16)
        grad_act = back_rows(grad_ffn, lax.all_gather(w_down, "fsdp", axis=0, tiled=True))
        grad_up = act_pull(grad_act)[0].astype(jnp.bfloat16)
        grad_norm_two = back_rows(grad_up, lax.all_gather(w_up, "fsdp", axis=0, tiled=True))
        grad_hidden_ln, grad_gain_two, grad_bias_two = norm_pull_two(grad_norm_two)
        grad_hidden = grad_rows + grad_hidden_ln
        grad_attn = grad_hidden.astype(jnp.bfloat16)
        grad_mixed = back_rows(grad_attn, lax.all_gather(w_out, "fsdp", axis=0, tiled=True))
        grad_gate_f, grad_ret_f = mix_pull(grad_mixed)
        grad_gate = grad_gate_f.astype(jnp.bfloat16)
        ret_low = grad_ret_f.astype(jnp.bfloat16)
        ret_heads = ret_low.reshape(tok_rows, HEADS, DV)
        grad_attend = jnp.einsum(
            "thd,shd->hts", ret_heads, value_heads, preferred_element_type=jnp.float32
        )
        grad_scores = (grad_attend * table).astype(jnp.bfloat16)
        grad_query = (
            jnp.einsum("hts,shd->thd", grad_scores, key_heads, preferred_element_type=jnp.float32)
            .reshape(tok_rows, QW)
            .astype(jnp.bfloat16)
        )
        key_part = jnp.einsum(
            "hts,thd->shd", grad_scores, query_heads, preferred_element_type=jnp.float32
        ).reshape(tok_rows * lax.axis_size("ctx"), QW)
        value_part = jnp.einsum(
            "hts,thd->shd", attend, ret_heads, preferred_element_type=jnp.float32
        ).reshape(tok_rows * lax.axis_size("ctx"), VW)
        key_value_sum = lax.psum_scatter(
            jnp.concatenate([key_part, value_part], axis=1).astype(jnp.bfloat16),
            "ctx",
            scatter_dimension=0,
            tiled=True,
        ).astype(jnp.float32)
        grad_key = key_value_sum[:, :QW].astype(jnp.bfloat16)
        grad_value = key_value_sum[:, QW:].astype(jnp.bfloat16)
        term_now = (
            contract_rows(grad_query, lax.all_gather(w_query, "fsdp", axis=0, tiled=True))
            + contract_rows(grad_key, lax.all_gather(w_key, "fsdp", axis=0, tiled=True))
            + contract_rows(grad_value, lax.all_gather(w_value, "fsdp", axis=0, tiled=True))
            + contract_rows(grad_gate, lax.all_gather(w_gate, "fsdp", axis=0, tiled=True))
        )
        grad_rows_ln, grad_gain_one, grad_bias_one = norm_pull_one(term_now)
        grad_list.append(grad_hidden + grad_rows_ln)
        gain_sum = gain_sum + jnp.stack([grad_gain_one, grad_gain_two])
        bias_sum = bias_sum + jnp.stack([grad_bias_one, grad_bias_two])
        kept_now = (
            low_one,
            jnp.concatenate([grad_query, grad_key, grad_value, grad_gate], axis=1),
            low_two,
            grad_up,
            mixed_low,
            grad_attn,
            active_low,
            grad_ffn,
        )
        term_sum = lax.psum_scatter(
            weight_term(kept_now, share_rows * lax.axis_size(("ctx", "fsdp"))),
            ("ctx", "fsdp"),
            scatter_dimension=0,
            tiled=True,
        )
        weight_sum = term_sum if weight_sum is None else weight_sum + term_sum
    weight_sum = weight_sum * grad_scale
    bounds = [QW, 2 * QW, 2 * QW + VW, 2 * QW + 2 * VW, 2 * QW + 2 * VW + FF, 2 * QW + 3 * VW + FF]
    g_query, g_key, g_value, g_gate, g_up, g_out_flat, g_down_flat = jnp.split(
        weight_sum, bounds, axis=1
    )
    g_out = g_out_flat.reshape(share_rows * (VW // model_width), model_width)
    g_down = g_down_flat.reshape(share_rows * (FF // model_width), model_width)
    gain_grads, bias_grads = (
        lax.psum_scatter(gain_sum, ("ctx", "fsdp"), scatter_dimension=1, tiled=True),
        lax.psum_scatter(bias_sum, ("ctx", "fsdp"), scatter_dimension=1, tiled=True),
    )
    gain_grads = gain_grads * grad_scale
    bias_grads = bias_grads * grad_scale
    output = jnp.stack(out_list)[:, None]
    grad_tokens = jnp.stack(grad_list)[:, None]
    return (
        output,
        grad_tokens,
        g_query,
        g_key,
        g_value,
        g_gate,
        g_out,
        g_up,
        g_down,
        gain_grads,
        bias_grads,
    )


def xy_swap(x, bit):
    return lax.ppermute(x, "fsdp", [(i, i ^ bit) for i in range(lax.axis_size("fsdp"))])


def core_swap(x):
    return lax.ppermute(x, "ctx", [(i, i ^ 1) for i in range(lax.axis_size("ctx"))])


def after(x, *earlier):
    return lax.optimization_barrier((x,) + tuple(earlier))[0]


def place(shape, items):
    arrays = []
    for item in items:
        if not any(item[0] is a for a in arrays):
            arrays.append(item[0])
    slots = [[item[0] is a for a in arrays].index(True) for item in items]
    kind = arrays[0].dtype

    def kernel(*refs):
        out = refs[len(arrays)]
        rank = lax.axis_index("fsdp")
        core = lax.axis_index("ctx") % 2
        for number, (array, start, rows, row, column) in enumerate(items):
            width = array.shape[1]
            step = min(rows, 64)
            source = refs[slots[number]]
            base = row(rank, core) if callable(row) else row

            def copy(first, width=width, step=step, source=source, base=base, start=start, rows=rows):
                def one(turn, carry):
                    place_in = pl.multiple_of(start + turn * step, step)
                    place_out = pl.multiple_of(base + turn * step, step)
                    out[pl.ds(place_out, step), first : first + width] = source[
                        pl.ds(place_in, step), :
                    ]
                    return carry

                lax.fori_loop(0, rows // step, one, 0)

            if callable(column):
                for which in range(2):
                    pl.when(core == which)(lambda which=which: copy(column(rank, which)))
            else:
                copy(column)

    size = shape[0] * shape[1] * jnp.dtype(kind).itemsize
    return pl.pallas_call(
        kernel,
        out_shape=jax.ShapeDtypeStruct(shape, kind),
        cost_estimate=pl.CostEstimate(flops=0, bytes_accessed=2 * size, transcendentals=0),
    )(*arrays)


def gather_first(x):
    return xy_swap(x, 1), xy_swap(x, 2)


def gather_second(first, second):
    half = first.shape[0] // 2
    return xy_swap(first[:half], 2), xy_swap(second[half:], 1)


def by_offset(x, first, second, low_part, high_part):
    rows, half = x.shape[0], x.shape[0] // 2
    return place(
        (4 * rows, x.shape[1]),
        [
            (x, 0, rows, 0, 0),
            (first, 0, rows, rows, 0),
            (low_part, 0, half, 2 * rows, 0),
            (high_part, 0, half, 2 * rows + half, 0),
            (second, 0, rows, 3 * rows, 0),
        ],
    )


def by_rank(x, first, second, low_part, high_part):
    rows, half = x.shape[0], x.shape[0] // 2
    return place(
        (4 * rows, x.shape[1]),
        [
            (x, 0, rows, lambda f, c: f * rows, 0),
            (first, 0, rows, lambda f, c: (f ^ 1) * rows, 0),
            (low_part, 0, half, lambda f, c: (f ^ 3) * rows, 0),
            (high_part, 0, half, lambda f, c: (f ^ 3) * rows + half, 0),
            (second, 0, rows, lambda f, c: (f ^ 2) * rows, 0),
        ],
    )


def rows_first(part):
    rows, half = part.shape[0] // 4, part.shape[1] // 2
    return xy_swap(part[rows : 3 * rows, :half], 1), xy_swap(part[2 * rows :, half:], 2)


def rows_second(part, left_in, right_in):
    rows, half = part.shape[0] // 4, part.shape[1] // 2
    wide = lambda v: v.astype(jnp.float32)
    left_far = wide(part[3 * rows :, :half]) + wide(left_in[rows:])
    right_far = wide(part[rows : 2 * rows, half:]) + wide(right_in[:rows])
    left_last = xy_swap(left_far.astype(jnp.bfloat16), 2)
    right_last = xy_swap(right_far.astype(jnp.bfloat16), 1)
    left = wide(part[:rows, :half]) + wide(left_in[:rows]) + wide(left_last)
    right = wide(part[:rows, half:]) + wide(right_in[rows:]) + wide(right_last)
    return jnp.concatenate([left, right], axis=1)


def reduce_first(blocks):
    half = blocks[0].shape[-1] // 2
    left_in = xy_swap(jnp.stack([blocks[1][..., :half], blocks[3][..., :half]]), 1)
    right_in = xy_swap(jnp.stack([blocks[2][..., half:], blocks[3][..., half:]]), 2)
    return left_in, right_in


def reduce_second(blocks, left_in, right_in):
    half = blocks[0].shape[-1] // 2
    wide = lambda v: v.astype(jnp.float32)
    left_far = wide(blocks[2][..., :half]) + wide(left_in[1])
    right_far = wide(blocks[1][..., half:]) + wide(right_in[1])
    left_last = xy_swap(left_far.astype(jnp.bfloat16), 2)
    right_last = xy_swap(right_far.astype(jnp.bfloat16), 1)
    left = wide(blocks[0][..., :half]) + wide(left_in[0]) + wide(left_last)
    right = wide(blocks[0][..., half:]) + wide(right_in[0]) + wide(right_last)
    return jnp.concatenate([left, right], axis=-1)


def sum_over(x, axis):
    size = lax.axis_size(axis)
    bit = 1
    while bit < size:
        x = x + lax.ppermute(x, axis, [(i, i ^ bit) for i in range(size)])
        bit *= 2
    return x


def in_rank_order(blocks, rank):
    odd = (rank % 2) == 1
    upper = (rank // 2) == 1
    one = [
        jnp.where(odd, blocks[1], blocks[0]),
        jnp.where(odd, blocks[0], blocks[1]),
        jnp.where(odd, blocks[3], blocks[2]),
        jnp.where(odd, blocks[2], blocks[3]),
    ]
    return [
        jnp.where(upper, one[2], one[0]),
        jnp.where(upper, one[3], one[1]),
        jnp.where(upper, one[0], one[2]),
        jnp.where(upper, one[1], one[3]),
    ]


def pick(x, index, size, axis):
    return lax.dynamic_slice_in_dim(x, index * size, size, axis)


def head_columns(w_query, w_key, w_value, w_gate, ctx_rank):
    return jnp.concatenate(
        [
            pick(w_query, ctx_rank, DK, 1),
            pick(w_key, ctx_rank, DK, 1),
            pick(w_value, ctx_rank, DV, 1),
            pick(w_gate, ctx_rank, DV, 1),
        ],
        axis=1,
    )


def out_pieces(w_out, ctx_rank, fsdp_rank, fsdp_size):
    rows = DV // fsdp_size
    start = (ctx_rank % 2) * DV
    return [
        lax.dynamic_slice_in_dim(w_out, start + (fsdp_rank ^ bit) * rows, rows, 0)
        for bit in range(fsdp_size)
    ]


def scatter_quarters(cuts, ctx_size, fsdp_size):
    parts = [cuts[0]]
    for bit in range(1, fsdp_size):
        pairs = [
            (c * fsdp_size + c // 2, c * fsdp_size + ((c // 2) ^ bit)) for c in range(ctx_size)
        ]
        parts.append(lax.ppermute(cuts[bit], ("ctx", "fsdp"), pairs))
    return parts


def choose_quarter(parts, ctx_rank, fsdp_rank):
    quarter = parts[0]
    for bit in range(1, len(parts)):
        quarter = jnp.where((fsdp_rank ^ (ctx_rank // 2)) == bit, parts[bit], quarter)
    return quarter


def copy_block(target, row, column, source, row_in, column_in, rows, width):
    step = min(rows, 64)

    def one(turn, carry):
        place_in = pl.multiple_of(row_in + turn * step, step)
        place_out = pl.multiple_of(row + turn * step, step)
        taken = source[pl.ds(place_in, step), pl.ds(column_in, width)]
        target[pl.ds(place_out, step), pl.ds(column, width)] = taken
        return carry

    lax.fori_loop(0, rows // step, one, 0)


def cut_ffn(w_up, w_down):
    ctx_size, fsdp_size = lax.axis_size("ctx"), lax.axis_size("fsdp")
    rows, width = w_up.shape[0], w_down.shape[1]
    unit, half = FF // (ctx_size * fsdp_size), ctx_size // 2
    wide = half * unit
    fourth = width // 4

    def kernel(up, down, *outs):
        rank = lax.axis_index("fsdp")
        core = lax.axis_index("ctx") % 2
        for number in range(fsdp_size - 1):
            other = rank ^ (number + 1)
            for i in range(half):
                column = pl.multiple_of(((core * half + i) * fsdp_size + other) * unit, unit)
                copy_block(outs[number], 0, i * unit, up, 0, column, rows, unit)
            for i in range(2):
                for q in range(2):
                    column = pl.multiple_of(core * 2 * fourth + q * fourth, fourth)
                    row = (i * fsdp_size + other) * unit
                    copy_block(
                        outs[number], (2 * i + q) * unit, wide, down, row, column, unit, fourth
                    )

    kind = jax.ShapeDtypeStruct((rows, wide + fourth), w_up.dtype)
    return list(pl.pallas_call(kernel, out_shape=[kind] * (fsdp_size - 1))(w_up, w_down))


def join_ffn(w_up, w_down, mine, other):
    ctx_size, fsdp_size = lax.axis_size("ctx"), lax.axis_size("fsdp")
    rows, width = w_up.shape[0], w_down.shape[1]
    unit, half = FF // (ctx_size * fsdp_size), ctx_size // 2
    wide = half * unit
    fourth = width // 4

    def kernel(up, down, *refs):
        up_out, down_out = refs[2 * len(mine) :]
        rank = lax.axis_index("fsdp")
        core = lax.axis_index("ctx") % 2
        for i in range(ctx_size):
            column = pl.multiple_of((i * fsdp_size + rank) * unit, unit)
            copy_block(up_out, rank * rows, i * unit, up, 0, column, rows, unit)
        for i in range(2):
            copy_block(
                down_out, (2 * rank + i) * unit, 0, down, (i * fsdp_size + rank) * unit, 0, unit, width
            )
        for number in range(2 * len(mine)):
            source = rank ^ (number % len(mine) + 1)
            part = core if number < len(mine) else 1 - core
            column = pl.multiple_of(part * wide, wide)
            copy_block(up_out, source * rows, column, refs[number], 0, 0, rows, wide)
            for i in range(2):
                for q in range(2):
                    column = pl.multiple_of(part * 2 * fourth + q * fourth, fourth)
                    row = (2 * source + i) * unit
                    copy_block(
                        down_out, row, column, refs[number], (2 * i + q) * unit, wide, unit, fourth
                    )

    shapes = [
        jax.ShapeDtypeStruct((fsdp_size * rows, FF // fsdp_size), w_up.dtype),
        jax.ShapeDtypeStruct((FF // fsdp_size, width), w_up.dtype),
    ]
    return pl.pallas_call(kernel, out_shape=shapes)(w_up, w_down, *mine, *other)


def smooth_parts(values):
    share = 0.5 + 0.5 * lax.erf(values * (0.5**0.5))
    density = jnp.exp(-0.5 * values * values) * ((0.5 / jnp.pi) ** 0.5)
    return values * share, share + values * density


def one_table(pos, doc, rate, scaling):
    keeping = (pos[:, None] >= pos[None, :]) & (doc[:, None] == doc[None, :])
    spacing = jnp.where(keeping, (pos[:, None] - pos[None, :]).astype(jnp.float32), 0.0)
    return jnp.where(keeping, jnp.exp(rate * spacing) * scaling, 0.0)


def ctx_sum(x):
    return lax.psum_scatter(x, "ctx", scatter_dimension=0, tiled=True)


def body_heads(
    tokens,
    cotangent,
    w_query,
    w_key,
    w_value,
    w_gate,
    w_out,
    w_up,
    w_down,
    norm_gains,
    norm_biases,
    block_deal,
    doc_lengths,
):
    low = jnp.bfloat16
    ctx_size = lax.axis_size("ctx")
    fsdp_size = lax.axis_size("fsdp")
    tok_rows = tokens.shape[2]
    full_length = tok_rows * ctx_size
    width = tokens.shape[3]
    share = width // (ctx_size * fsdp_size)
    grad_scale = float(MICRO * fsdp_size * full_length) ** (-0.5)
    ctx_rank = lax.axis_index("ctx")
    fsdp_rank = lax.axis_index("fsdp")
    pos = stored_positions(block_deal, full_length, BLOCK)
    rate = jnp.log1p(-jnp.exp2(-5.0 - ctx_rank.astype(jnp.float32)))
    scaling = DK ** (-0.5)

    own_in = head_columns(w_query, w_key, w_value, w_gate, ctx_rank)
    tokens = after(tokens, own_in)
    rows_in = []
    norm_one = []
    x_own = []
    for m in range(MICRO):
        rows_in.append(after(tokens[m, 0], *x_own[-1:]).astype(jnp.float32))
        norm_one.append(jax.vjp(layer_norm, rows_in[m], norm_gains[0], norm_biases[0]))
        x_own.append(norm_one[m][0].astype(low))
    grad_rows = [cotangent[m, 0].astype(jnp.float32) for m in range(MICRO)]
    x_all = [lax.all_gather(x, "ctx", axis=0, tiled=True) for x in x_own]
    in_first = gather_first(own_in)
    ffn_cut = cut_ffn(w_up, w_down)
    out_cut = out_pieces(w_out, ctx_rank, fsdp_rank, fsdp_size)
    in_first = lax.optimization_barrier(tuple(in_first) + tuple(ffn_cut) + tuple(out_cut))[:2]
    in_second = gather_second(*in_first)
    w_in = by_rank(own_in, *in_first, *in_second)
    out_cut = lax.optimization_barrier(tuple(out_cut) + tuple(in_first))[: len(out_cut)]
    out_parts = scatter_quarters(out_cut, ctx_size, fsdp_size)

    def mix(m, x_now, *earlier):
        doc = document_ids(pos, doc_lengths[m, 0])
        table = one_table(pos, doc, rate, scaling)
        joint = jnp.dot(x_now, w_in[:, : 2 * DK + DV], preferred_element_type=jnp.float32).astype(low)
        joint = after(joint, *earlier)
        gate_pre = jnp.dot(x_now, w_in[:, 2 * DK + DV :], preferred_element_type=jnp.float32)
        query, key, value = joint[:, :DK], joint[:, DK : 2 * DK], joint[:, 2 * DK :]
        attend = (contract_rows(query, key) * table).astype(low)
        retained = add_single(attend, value)
        mixed, mix_pull = jax.vjp(gated_mix, gate_pre, retained)
        return table, query, key, value, attend, mix_pull, mixed.astype(low)

    kept = [mix(0, x_all[0])]
    out_parts = lax.optimization_barrier(tuple(out_parts) + (kept[0][4],))[:-1]
    quarter = choose_quarter(out_parts, ctx_rank, fsdp_rank)
    out_first = gather_first(quarter)
    out_second = gather_second(*out_first)
    w_head = by_rank(quarter, *out_first, *out_second)
    cot_own = after(cotangent.reshape(MICRO * tok_rows, width), *out_first)
    cot_first = gather_first(cot_own)
    ffn_cut = lax.optimization_barrier(tuple(ffn_cut) + tuple(out_second))[: len(ffn_cut)]
    ffn_mine = [xy_swap(ffn_cut[bit - 1], bit) for bit in range(1, fsdp_size)]
    part = add_single(kept[0][6], w_head).astype(low)
    attn_out = [ctx_sum(after(part, *x_all[1:], *cot_first))]
    for m in range(1, MICRO):
        kept.append(mix(m, after(x_all[m], *cot_first), *ffn_mine[:1]))
        part = add_single(kept[m][6], w_head).astype(low)
        attn_out.append(ctx_sum(after(part, *ffn_mine)))
    cot_second = gather_second(*cot_first)
    def enter(m):
        hidden = rows_in[m] + attn_out[m].astype(jnp.float32)
        normed_two, pull_two = jax.vjp(layer_norm, hidden, norm_gains[1], norm_biases[1])
        two_own = normed_two.astype(low)
        return hidden, pull_two, two_own, gather_first(two_own)

    ffn_other = [core_swap(x) for x in ffn_mine]
    attn_out[0] = after(attn_out[0], *ffn_other, *cot_second)
    entered = [enter(0)]
    up_own, down_own = join_ffn(w_up, w_down, ffn_mine, ffn_other)
    cot_all = [
        place(
            (fsdp_size * tok_rows, width),
            [
                (cot_own, m * tok_rows, tok_rows, 0, 0),
                (cot_first[0], m * tok_rows, tok_rows, tok_rows, 0),
                (cot_second[m], 0, tok_rows, 2 * tok_rows, 0),
                (cot_first[1], m * tok_rows, tok_rows, 3 * tok_rows, 0),
            ],
        )
        for m in range(MICRO)
    ]

    outs = [None] * MICRO
    grad_attn = []
    grad_hidden = []
    ffn_kept = []
    norm_two_terms = []

    for m in range(MICRO):
        hidden, pull_two, two_own, two_first = entered[m]
        if m == 0:
            two_first = lax.optimization_barrier(tuple(two_first) + (up_own, down_own))[:2]
            two_second = gather_second(*two_first)
        two_second = lax.optimization_barrier(tuple(two_second) + (cot_all[m],))[:2]
        two_all = by_offset(two_own, *two_first, *two_second)
        active, slope = smooth_parts(add_single(two_all, up_own))
        active_low, slope = lax.optimization_barrier((active.astype(low), slope))
        grad_up = (back_rows(cot_all[m], down_own) * slope).astype(low)
        norm_part = back_rows(grad_up, up_own).astype(low)
        sent = rows_first(norm_part)
        later = ()
        if m + 1 < MICRO:
            attn_out[m + 1] = after(attn_out[m + 1], *sent)
            entered.append(enter(m + 1))
            sent = lax.optimization_barrier(tuple(sent) + (entered[m + 1][2],))[:2]
            two_second = gather_second(*entered[m + 1][3])
            later = two_second
        grad_norm_two = after(rows_second(norm_part, *sent), *grad_attn[-1:], *later)
        grad_ln, gain_two, bias_two = pull_two(grad_norm_two)
        norm_two_terms.append((gain_two, bias_two))
        total = grad_rows[m] + grad_ln
        grad_hidden.append(total)
        grad_attn.append(total.astype(low))
        ffn_kept.append((two_all, grad_up, active_low, hidden))

    grad_all = [lax.all_gather(grad_attn[m], "ctx", axis=0, tiled=True) for m in range(MICRO)]

    def unmix(m, grad_now):
        table, query, key, value, attend, mix_pull, mixed_low = kept[m]
        grad_mixed = back_rows(grad_now, w_head)
        grad_gate, grad_ret = mix_pull(grad_mixed)
        ret_low = grad_ret.astype(low)
        grad_scores = (contract_rows(ret_low, value) * table).astype(low)
        grad_query = add_single(grad_scores, key).astype(low)
        grad_key = contract_cols(grad_scores, query).astype(low)
        grad_value = contract_cols(attend, ret_low).astype(low)
        return jnp.concatenate([grad_query, grad_key, grad_value, grad_gate.astype(low)], axis=1)

    terms = []
    sums = []
    fill = ()
    for m in range(MICRO):
        grad_now = after(grad_all[m], *(grad_attn[1:] if m == 0 else terms[-1:]), *fill)
        grad_in = unmix(m, grad_now)
        part = back_rows(grad_in, w_in).astype(low)
        terms.append(part)
        sums.append(ctx_sum(after(part, *grad_all[m + 1 :], *sums[-1:])))
        x_now, grad_in = lax.optimization_barrier((x_all[m], grad_in, part))[:2]
        in_now = contract_cols(x_now, grad_in)
        if m == 0:
            in_term = in_now
            sums[m] = after(sums[m], in_term)
            ready = [after(ffn_kept[n][2], part, grad_attn[n]) for n in range(MICRO)]
            fill = tuple(add_single(ready[n], down_own).astype(low) for n in range(MICRO))
        else:
            in_term = (in_term + in_now).astype(low)
    in_view = in_term.reshape(ctx_size, fsdp_size, share, -1)
    in_blocks_out = [pick(in_view, fsdp_rank ^ j, 1, 1)[:, 0] for j in range(fsdp_size)]
    in_sent = reduce_first(in_blocks_out)
    up_grad = sum(contract_cols(k[0], after(k[1], in_term)) for k in ffn_kept).astype(low)
    down_grad = sum(
        contract_cols(after(ready[n], up_grad), cot_all[n]) for n in range(MICRO)
    ).astype(low)
    sums[-1] = after(sums[-1], up_grad, down_grad, *in_sent)
    up_sum = ctx_sum(after(up_grad, sums[-1]))
    down_sum = ctx_sum(after(down_grad, sums[-1]))
    in_sum = reduce_second(in_blocks_out, *in_sent).astype(low)
    out_term = sum(
        contract_cols(after(kept[m][6], down_grad), grad_all[m]) for m in range(MICRO)
    ).astype(low)

    grad_tokens = []
    norm_one_terms = []
    for m in range(MICRO):
        grad_ln, gain_one, bias_one = norm_one[m][1](sums[m].astype(jnp.float32))
        norm_one_terms.append((gain_one, bias_one))
        grad_tokens.append(grad_hidden[m] + grad_ln)

    gain_rows = [sum(t[0] for t in norm_one_terms), sum(t[0] for t in norm_two_terms)]
    bias_rows = [sum(t[1] for t in norm_one_terms), sum(t[1] for t in norm_two_terms)]
    norm_lines = sum_over(jnp.stack(gain_rows + bias_rows), "ctx")
    in_mine = lax.all_to_all(
        after(in_sum, norm_lines), "ctx", split_axis=0, concat_axis=0, tiled=True
    )
    norm_sums = sum_over(norm_lines, "fsdp")
    for n in range(MICRO):
        ffn_part = after(fill[n], in_sum, norm_lines)
        outs[n] = (ffn_kept[n][3] + rows_second(ffn_part, *rows_first(ffn_part))).astype(low)
    out_term = after(out_term, in_sum, norm_lines)
    rows = DV // fsdp_size
    out_blocks = [pick(out_term, fsdp_rank ^ j, rows, 0) for j in range(fsdp_size)]
    g_out = reduce_second(out_blocks, *reduce_first(out_blocks))

    up_view = up_sum.reshape(fsdp_size, share, -1)
    pieces = [lax.dynamic_index_in_dim(up_view, fsdp_rank, 0, keepdims=False)]
    for bit in range(1, fsdp_size):
        pieces.append(
            xy_swap(lax.dynamic_index_in_dim(up_view, fsdp_rank ^ bit, 0, keepdims=False), bit)
        )
    in_mine = lax.optimization_barrier((in_mine, norm_sums) + tuple(pieces))[0]
    down_sum = after(down_sum, in_mine)
    def by_head(first, size):
        part = in_mine[:, :, first : first + size].transpose(1, 0, 2)
        return part.reshape(share, -1).astype(jnp.float32) * grad_scale

    g_query = by_head(0, DK)
    g_key = by_head(DK, DK)
    g_value = by_head(2 * DK, DV)
    g_gate = by_head(2 * DK + DV, DV)

    pieces = [p.reshape(share, ctx_size, -1) for p in in_rank_order(pieces, fsdp_rank)]
    g_up = jnp.stack(pieces, axis=2).reshape(share, FF).astype(jnp.float32) * grad_scale

    norm_sums = pick(norm_sums, ctx_rank * fsdp_size + fsdp_rank, share, 1) * grad_scale
    return (
        jnp.stack(outs)[:, None],
        jnp.stack(grad_tokens)[:, None],
        g_query,
        g_key,
        g_value,
        g_gate,
        g_out * grad_scale,
        g_up,
        down_sum.astype(jnp.float32) * grad_scale,
        norm_sums[:2],
        norm_sums[2:],
    )


def solution(mesh):
    in_specs = (
        P(None, "fsdp", "ctx", None),
        P(None, "fsdp", "ctx", None),
        P("fsdp", None),
        P("fsdp", None),
        P("fsdp", None),
        P("fsdp", None),
        P("fsdp", None),
        P("fsdp", None),
        P("fsdp", None),
        P(),
        P(),
        P(),
        P(None, "fsdp", None),
    )
    out_specs = (
        P(None, "fsdp", "ctx", None),
        P(None, "fsdp", "ctx", None),
        P(("ctx", "fsdp"), None),
        P(("ctx", "fsdp"), None),
        P(("ctx", "fsdp"), None),
        P(("ctx", "fsdp"), None),
        P(("ctx", "fsdp"), None),
        P(("ctx", "fsdp"), None),
        P(("ctx", "fsdp"), None),
        P(None, ("ctx", "fsdp")),
        P(None, ("ctx", "fsdp")),
    )
    by_heads = mesh.shape["ctx"] == HEADS and mesh.shape["fsdp"] == 4
    chosen = body_heads if by_heads else body
    return jax.shard_map(chosen, mesh=mesh, in_specs=in_specs, out_specs=out_specs, check_vma=False)
```

```python
import jax
import jax.numpy as jnp
from jax import lax
from jax.experimental import pallas as pl
from jax.sharding import PartitionSpec as P

HEADS = 8
DK = 256
DV = 512
FF = 4096
MICRO = 2
QW = 2048
VW = 4096
BLOCK = 64


epsilon = 1e-05
group_floor = 1.0


def layer_norm(values, gain_row, offset):
    center = jnp.mean(values, axis=-1, keepdims=True)
    centred = values - center
    spread = jnp.mean(centred * centred, axis=-1, keepdims=True)
    return centred * lax.rsqrt(spread + epsilon) * gain_row + offset


def gated_mix(gate_pre, retained):
    number = retained.shape[0]
    grouped = retained.reshape(number, -1, DV)
    center = jnp.mean(grouped, axis=-1, keepdims=True)
    centred = grouped - center
    spread = jnp.mean(centred * centred, axis=-1, keepdims=True)
    normed = (centred * lax.rsqrt(spread + group_floor)).reshape(number, -1)
    return jax.nn.silu(gate_pre) * normed


def smooth_act(values):
    return jax.nn.gelu(values, approximate=False)


def stored_positions(block_deal, full_length, block_size):
    stored = jnp.arange(full_length, dtype=jnp.int32)
    block_ids = stored // block_size
    slots_all = jnp.arange(block_deal.shape[0], dtype=jnp.int32)
    picked = jnp.sum(
        jnp.where(block_ids[:, None] == slots_all[None, :], block_deal[None, :], 0),
        axis=1,
        dtype=jnp.int32,
    )
    return picked * block_size + stored % block_size


def document_ids(positions, doc_sizes):
    starts = jnp.cumsum(doc_sizes, dtype=jnp.int32) - doc_sizes
    return (
        jnp.sum((positions[:, None] >= starts[None, :]).astype(jnp.int32), axis=1, dtype=jnp.int32)
        - 1
    )


def decay_table(query_pos, query_doc, key_pos, key_doc, decay_log, scaling):
    keeping = (query_pos[:, None] >= key_pos[None, :]) & (query_doc[:, None] == key_doc[None, :])
    spacing = jnp.where(keeping, (query_pos[:, None] - key_pos[None, :]).astype(jnp.float32), 0.0)
    factor = jnp.exp(decay_log[:, None, None] * spacing[None])
    return jnp.where(keeping[None], factor * scaling, 0.0)


def contract_rows(left, right):
    return lax.dot_general(
        left, right, (((1,), (1,)), ((), ())), preferred_element_type=jnp.float32
    )


def contract_cols(left, right):
    return lax.dot_general(
        left, right, (((0,), (0,)), ((), ())), preferred_element_type=jnp.float32
    )


def add_single(left, weight_piece):
    return jnp.dot(left, weight_piece, preferred_element_type=jnp.float32)


def back_rows(left, weight_piece):
    return contract_rows(left, weight_piece)


def weight_term(kept_acts, number):
    normed_one, grads_in, normed_two, grads_up, mixed_all, grads_attn, active_all, grads_ffn = (
        kept_acts
    )
    pieces = [
        contract_cols(normed_one, grads_in),
        contract_cols(normed_two, grads_up),
        contract_cols(mixed_all, grads_attn).reshape(number, -1),
        contract_cols(active_all, grads_ffn).reshape(number, -1),
    ]
    return jnp.concatenate(pieces, axis=1)


def body(
    tokens,
    cotangent,
    w_query,
    w_key,
    w_value,
    w_gate,
    w_out,
    w_up,
    w_down,
    norm_gains,
    norm_biases,
    block_deal,
    doc_lengths,
):
    ctx_size = lax.axis_size("ctx")
    tok_rows = tokens.shape[2]
    full_length = tok_rows * ctx_size
    model_width = tokens.shape[3]
    share_rows = model_width // lax.axis_size(("ctx", "fsdp"))
    grad_scale = float(MICRO * lax.axis_size("fsdp") * full_length) ** (-0.5)
    own_start = lax.axis_index("ctx") * tok_rows
    key_pos = stored_positions(block_deal, full_length, BLOCK)
    query_pos = lax.dynamic_slice_in_dim(key_pos, own_start, tok_rows)
    decay_log = jnp.log1p(-jnp.exp2(-5.0 - jnp.arange(HEADS).astype(jnp.float32)))
    scaling = DK ** (-0.5)
    out_list = []
    grad_list = []
    weight_sum = None
    gain_sum = jnp.zeros((2, model_width), jnp.float32)
    bias_sum = jnp.zeros((2, model_width), jnp.float32)
    for batch_index in range(MICRO):
        rows_in = tokens[batch_index, 0].astype(jnp.float32)
        grad_rows = cotangent[batch_index, 0].astype(jnp.float32)
        key_doc = document_ids(key_pos, doc_lengths[batch_index, 0])
        query_doc = lax.dynamic_slice_in_dim(key_doc, own_start, tok_rows)
        table = decay_table(query_pos, query_doc, key_pos, key_doc, decay_log, scaling)
        normed_one, norm_pull_one = jax.vjp(layer_norm, rows_in, norm_gains[0], norm_biases[0])
        low_one = normed_one.astype(jnp.bfloat16)
        pieces = (
            lax.all_gather(w_query, "fsdp", axis=0, tiled=True),
            lax.all_gather(w_key, "fsdp", axis=0, tiled=True),
            lax.all_gather(w_value, "fsdp", axis=0, tiled=True),
            lax.all_gather(w_gate, "fsdp", axis=0, tiled=True),
        )
        query_f, key_f, value_f, gate_pre = tuple(
            (
                jnp.dot(low_one, weight_piece, preferred_element_type=jnp.float32)
                for weight_piece in pieces
            )
        )
        query_low = query_f.astype(jnp.bfloat16)
        key_low = key_f.astype(jnp.bfloat16)
        value_low = value_f.astype(jnp.bfloat16)
        keys_all, values_all = (
            lax.all_gather(key_low, "ctx", axis=0, tiled=True),
            lax.all_gather(value_low, "ctx", axis=0, tiled=True),
        )
        query_heads = query_low.reshape(tok_rows, HEADS, DK)
        key_heads = keys_all.reshape(full_length, HEADS, DK)
        value_heads = values_all.reshape(full_length, HEADS, DV)
        scores = jnp.einsum(
            "thd,shd->hts", query_heads, key_heads, preferred_element_type=jnp.float32
        )
        attend = (scores * table).astype(jnp.bfloat16)
        retained = jnp.einsum(
            "hts,shd->thd", attend, value_heads, preferred_element_type=jnp.float32
        ).reshape(tok_rows, VW)
        mixed, mix_pull = jax.vjp(gated_mix, gate_pre, retained)
        mixed_low = mixed.astype(jnp.bfloat16)
        attn_out = add_single(mixed_low, lax.all_gather(w_out, "fsdp", axis=0, tiled=True))
        hidden = rows_in + attn_out
        normed_two, norm_pull_two = jax.vjp(layer_norm, hidden, norm_gains[1], norm_biases[1])
        low_two = normed_two.astype(jnp.bfloat16)
        up_pre = add_single(low_two, lax.all_gather(w_up, "fsdp", axis=0, tiled=True))
        active, act_pull = jax.vjp(smooth_act, up_pre)
        active_low = active.astype(jnp.bfloat16)
        ffn_out = add_single(active_low, lax.all_gather(w_down, "fsdp", axis=0, tiled=True))
        out_list.append((hidden + ffn_out).astype(jnp.bfloat16))
        grad_ffn = grad_rows.astype(jnp.bfloat16)
        grad_act = back_rows(grad_ffn, lax.all_gather(w_down, "fsdp", axis=0, tiled=True))
        grad_up = act_pull(grad_act)[0].astype(jnp.bfloat16)
        grad_norm_two = back_rows(grad_up, lax.all_gather(w_up, "fsdp", axis=0, tiled=True))
        grad_hidden_ln, grad_gain_two, grad_bias_two = norm_pull_two(grad_norm_two)
        grad_hidden = grad_rows + grad_hidden_ln
        grad_attn = grad_hidden.astype(jnp.bfloat16)
        grad_mixed = back_rows(grad_attn, lax.all_gather(w_out, "fsdp", axis=0, tiled=True))
        grad_gate_f, grad_ret_f = mix_pull(grad_mixed)
        grad_gate = grad_gate_f.astype(jnp.bfloat16)
        ret_low = grad_ret_f.astype(jnp.bfloat16)
        ret_heads = ret_low.reshape(tok_rows, HEADS, DV)
        grad_attend = jnp.einsum(
            "thd,shd->hts", ret_heads, value_heads, preferred_element_type=jnp.float32
        )
        grad_scores = (grad_attend * table).astype(jnp.bfloat16)
        grad_query = (
            jnp.einsum("hts,shd->thd", grad_scores, key_heads, preferred_element_type=jnp.float32)
            .reshape(tok_rows, QW)
            .astype(jnp.bfloat16)
        )
        key_part = jnp.einsum(
            "hts,thd->shd", grad_scores, query_heads, preferred_element_type=jnp.float32
        ).reshape(tok_rows * lax.axis_size("ctx"), QW)
        value_part = jnp.einsum(
            "hts,thd->shd", attend, ret_heads, preferred_element_type=jnp.float32
        ).reshape(tok_rows * lax.axis_size("ctx"), VW)
        key_value_sum = lax.psum_scatter(
            jnp.concatenate([key_part, value_part], axis=1).astype(jnp.bfloat16),
            "ctx",
            scatter_dimension=0,
            tiled=True,
        ).astype(jnp.float32)
        grad_key = key_value_sum[:, :QW].astype(jnp.bfloat16)
        grad_value = key_value_sum[:, QW:].astype(jnp.bfloat16)
        term_now = (
            contract_rows(grad_query, lax.all_gather(w_query, "fsdp", axis=0, tiled=True))
            + contract_rows(grad_key, lax.all_gather(w_key, "fsdp", axis=0, tiled=True))
            + contract_rows(grad_value, lax.all_gather(w_value, "fsdp", axis=0, tiled=True))
            + contract_rows(grad_gate, lax.all_gather(w_gate, "fsdp", axis=0, tiled=True))
        )
        grad_rows_ln, grad_gain_one, grad_bias_one = norm_pull_one(term_now)
        grad_list.append(grad_hidden + grad_rows_ln)
        gain_sum = gain_sum + jnp.stack([grad_gain_one, grad_gain_two])
        bias_sum = bias_sum + jnp.stack([grad_bias_one, grad_bias_two])
        kept_now = (
            low_one,
            jnp.concatenate([grad_query, grad_key, grad_value, grad_gate], axis=1),
            low_two,
            grad_up,
            mixed_low,
            grad_attn,
            active_low,
            grad_ffn,
        )
        term_sum = lax.psum_scatter(
            weight_term(kept_now, share_rows * lax.axis_size(("ctx", "fsdp"))),
            ("ctx", "fsdp"),
            scatter_dimension=0,
            tiled=True,
        )
        weight_sum = term_sum if weight_sum is None else weight_sum + term_sum
    weight_sum = weight_sum * grad_scale
    bounds = [QW, 2 * QW, 2 * QW + VW, 2 * QW + 2 * VW, 2 * QW + 2 * VW + FF, 2 * QW + 3 * VW + FF]
    g_query, g_key, g_value, g_gate, g_up, g_out_flat, g_down_flat = jnp.split(
        weight_sum, bounds, axis=1
    )
    g_out = g_out_flat.reshape(share_rows * (VW // model_width), model_width)
    g_down = g_down_flat.reshape(share_rows * (FF // model_width), model_width)
    gain_grads, bias_grads = (
        lax.psum_scatter(gain_sum, ("ctx", "fsdp"), scatter_dimension=1, tiled=True),
        lax.psum_scatter(bias_sum, ("ctx", "fsdp"), scatter_dimension=1, tiled=True),
    )
    gain_grads = gain_grads * grad_scale
    bias_grads = bias_grads * grad_scale
    output = jnp.stack(out_list)[:, None]
    grad_tokens = jnp.stack(grad_list)[:, None]
    return (
        output,
        grad_tokens,
        g_query,
        g_key,
        g_value,
        g_gate,
        g_out,
        g_up,
        g_down,
        gain_grads,
        bias_grads,
    )


def xy_swap(x, bit):
    return lax.ppermute(x, "fsdp", [(i, i ^ bit) for i in range(lax.axis_size("fsdp"))])


def core_swap(x):
    return lax.ppermute(x, "ctx", [(i, i ^ 1) for i in range(lax.axis_size("ctx"))])


def after(x, *earlier):
    return lax.optimization_barrier((x,) + tuple(earlier))[0]


def place(shape, items):
    arrays = []
    for item in items:
        if not any(item[0] is a for a in arrays):
            arrays.append(item[0])
    slots = [[item[0] is a for a in arrays].index(True) for item in items]
    kind = arrays[0].dtype

    def kernel(*refs):
        out = refs[len(arrays)]
        rank = lax.axis_index("fsdp")
        core = lax.axis_index("ctx") % 2
        for number, (array, start, rows, row, column) in enumerate(items):
            width = array.shape[1]
            step = min(rows, 64)
            source = refs[slots[number]]
            base = row(rank, core) if callable(row) else row

            def copy(first, width=width, step=step, source=source, base=base, start=start, rows=rows):
                def one(turn, carry):
                    place_in = pl.multiple_of(start + turn * step, step)
                    place_out = pl.multiple_of(base + turn * step, step)
                    out[pl.ds(place_out, step), first : first + width] = source[
                        pl.ds(place_in, step), :
                    ]
                    return carry

                lax.fori_loop(0, rows // step, one, 0)

            if callable(column):
                for which in range(2):
                    pl.when(core == which)(lambda which=which: copy(column(rank, which)))
            else:
                copy(column)

    size = shape[0] * shape[1] * jnp.dtype(kind).itemsize
    return pl.pallas_call(
        kernel,
        out_shape=jax.ShapeDtypeStruct(shape, kind),
        cost_estimate=pl.CostEstimate(flops=0, bytes_accessed=2 * size, transcendentals=0),
    )(*arrays)


def gather_first(x):
    return xy_swap(x, 1), xy_swap(x, 2)


def gather_second(first, second):
    half = first.shape[0] // 2
    return xy_swap(first[:half], 2), xy_swap(second[half:], 1)


def by_offset(x, first, second, low_part, high_part):
    rows, half = x.shape[0], x.shape[0] // 2
    return place(
        (4 * rows, x.shape[1]),
        [
            (x, 0, rows, 0, 0),
            (first, 0, rows, rows, 0),
            (low_part, 0, half, 2 * rows, 0),
            (high_part, 0, half, 2 * rows + half, 0),
            (second, 0, rows, 3 * rows, 0),
        ],
    )


def by_rank(x, first, second, low_part, high_part):
    rows, half = x.shape[0], x.shape[0] // 2
    return place(
        (4 * rows, x.shape[1]),
        [
            (x, 0, rows, lambda f, c: f * rows, 0),
            (first, 0, rows, lambda f, c: (f ^ 1) * rows, 0),
            (low_part, 0, half, lambda f, c: (f ^ 3) * rows, 0),
            (high_part, 0, half, lambda f, c: (f ^ 3) * rows + half, 0),
            (second, 0, rows, lambda f, c: (f ^ 2) * rows, 0),
        ],
    )


def rows_first(part):
    rows, half = part.shape[0] // 4, part.shape[1] // 2
    return xy_swap(part[rows : 3 * rows, :half], 1), xy_swap(part[2 * rows :, half:], 2)


def rows_second(part, left_in, right_in):
    rows, half = part.shape[0] // 4, part.shape[1] // 2
    wide = lambda v: v.astype(jnp.float32)
    left_far = wide(part[3 * rows :, :half]) + wide(left_in[rows:])
    right_far = wide(part[rows : 2 * rows, half:]) + wide(right_in[:rows])
    left_last = xy_swap(left_far.astype(jnp.bfloat16), 2)
    right_last = xy_swap(right_far.astype(jnp.bfloat16), 1)
    left = wide(part[:rows, :half]) + wide(left_in[:rows]) + wide(left_last)
    right = wide(part[:rows, half:]) + wide(right_in[rows:]) + wide(right_last)
    return jnp.concatenate([left, right], axis=1)


def reduce_first(blocks):
    half = blocks[0].shape[-1] // 2
    left_in = xy_swap(jnp.stack([blocks[1][..., :half], blocks[3][..., :half]]), 1)
    right_in = xy_swap(jnp.stack([blocks[2][..., half:], blocks[3][..., half:]]), 2)
    return left_in, right_in


def reduce_second(blocks, left_in, right_in):
    half = blocks[0].shape[-1] // 2
    wide = lambda v: v.astype(jnp.float32)
    left_far = wide(blocks[2][..., :half]) + wide(left_in[1])
    right_far = wide(blocks[1][..., half:]) + wide(right_in[1])
    left_last = xy_swap(left_far.astype(jnp.bfloat16), 2)
    right_last = xy_swap(right_far.astype(jnp.bfloat16), 1)
    left = wide(blocks[0][..., :half]) + wide(left_in[0]) + wide(left_last)
    right = wide(blocks[0][..., half:]) + wide(right_in[0]) + wide(right_last)
    return jnp.concatenate([left, right], axis=-1)


def sum_over(x, axis):
    size = lax.axis_size(axis)
    bit = 1
    while bit < size:
        x = x + lax.ppermute(x, axis, [(i, i ^ bit) for i in range(size)])
        bit *= 2
    return x


def in_rank_order(blocks, rank):
    odd = (rank % 2) == 1
    upper = (rank // 2) == 1
    one = [
        jnp.where(odd, blocks[1], blocks[0]),
        jnp.where(odd, blocks[0], blocks[1]),
        jnp.where(odd, blocks[3], blocks[2]),
        jnp.where(odd, blocks[2], blocks[3]),
    ]
    return [
        jnp.where(upper, one[2], one[0]),
        jnp.where(upper, one[3], one[1]),
        jnp.where(upper, one[0], one[2]),
        jnp.where(upper, one[1], one[3]),
    ]


def pick(x, index, size, axis):
    return lax.dynamic_slice_in_dim(x, index * size, size, axis)


def head_columns(w_query, w_key, w_value, w_gate, ctx_rank):
    return jnp.concatenate(
        [
            pick(w_query, ctx_rank, DK, 1),
            pick(w_key, ctx_rank, DK, 1),
            pick(w_value, ctx_rank, DV, 1),
            pick(w_gate, ctx_rank, DV, 1),
        ],
        axis=1,
    )


def out_pieces(w_out, ctx_rank, fsdp_rank, fsdp_size):
    rows = DV // fsdp_size
    start = (ctx_rank % 2) * DV
    return [
        lax.dynamic_slice_in_dim(w_out, start + (fsdp_rank ^ bit) * rows, rows, 0)
        for bit in range(fsdp_size)
    ]


def scatter_quarters(cuts, ctx_size, fsdp_size):
    parts = [cuts[0]]
    for bit in range(1, fsdp_size):
        pairs = [
            (c * fsdp_size + c // 2, c * fsdp_size + ((c // 2) ^ bit)) for c in range(ctx_size)
        ]
        parts.append(lax.ppermute(cuts[bit], ("ctx", "fsdp"), pairs))
    return parts


def choose_quarter(parts, ctx_rank, fsdp_rank):
    quarter = parts[0]
    for bit in range(1, len(parts)):
        quarter = jnp.where((fsdp_rank ^ (ctx_rank // 2)) == bit, parts[bit], quarter)
    return quarter


def copy_block(target, row, column, source, row_in, column_in, rows, width):
    step = min(rows, 64)

    def one(turn, carry):
        place_in = pl.multiple_of(row_in + turn * step, step)
        place_out = pl.multiple_of(row + turn * step, step)
        taken = source[pl.ds(place_in, step), pl.ds(column_in, width)]
        target[pl.ds(place_out, step), pl.ds(column, width)] = taken
        return carry

    lax.fori_loop(0, rows // step, one, 0)


def cut_ffn(w_up, w_down):
    ctx_size, fsdp_size = lax.axis_size("ctx"), lax.axis_size("fsdp")
    rows, width = w_up.shape[0], w_down.shape[1]
    unit, half = FF // (ctx_size * fsdp_size), ctx_size // 2
    wide = half * unit
    fourth = width // 4

    def kernel(up, down, *outs):
        rank = lax.axis_index("fsdp")
        core = lax.axis_index("ctx") % 2
        for number in range(fsdp_size - 1):
            other = rank ^ (number + 1)
            for i in range(half):
                column = pl.multiple_of(((core * half + i) * fsdp_size + other) * unit, unit)
                copy_block(outs[number], 0, i * unit, up, 0, column, rows, unit)
            for i in range(2):
                for q in range(2):
                    column = pl.multiple_of(core * 2 * fourth + q * fourth, fourth)
                    row = (i * fsdp_size + other) * unit
                    copy_block(
                        outs[number], (2 * i + q) * unit, wide, down, row, column, unit, fourth
                    )

    kind = jax.ShapeDtypeStruct((rows, wide + fourth), w_up.dtype)
    return list(pl.pallas_call(kernel, out_shape=[kind] * (fsdp_size - 1))(w_up, w_down))


def join_ffn(w_up, w_down, mine, other):
    ctx_size, fsdp_size = lax.axis_size("ctx"), lax.axis_size("fsdp")
    rows, width = w_up.shape[0], w_down.shape[1]
    unit, half = FF // (ctx_size * fsdp_size), ctx_size // 2
    wide = half * unit
    fourth = width // 4

    def kernel(up, down, *refs):
        up_out, down_out = refs[2 * len(mine) :]
        rank = lax.axis_index("fsdp")
        core = lax.axis_index("ctx") % 2
        for i in range(ctx_size):
            column = pl.multiple_of((i * fsdp_size + rank) * unit, unit)
            copy_block(up_out, rank * rows, i * unit, up, 0, column, rows, unit)
        for i in range(2):
            copy_block(
                down_out, (2 * rank + i) * unit, 0, down, (i * fsdp_size + rank) * unit, 0, unit, width
            )
        for number in range(2 * len(mine)):
            source = rank ^ (number % len(mine) + 1)
            part = core if number < len(mine) else 1 - core
            column = pl.multiple_of(part * wide, wide)
            copy_block(up_out, source * rows, column, refs[number], 0, 0, rows, wide)
            for i in range(2):
                for q in range(2):
                    column = pl.multiple_of(part * 2 * fourth + q * fourth, fourth)
                    row = (2 * source + i) * unit
                    copy_block(
                        down_out, row, column, refs[number], (2 * i + q) * unit, wide, unit, fourth
                    )

    shapes = [
        jax.ShapeDtypeStruct((fsdp_size * rows, FF // fsdp_size), w_up.dtype),
        jax.ShapeDtypeStruct((FF // fsdp_size, width), w_up.dtype),
    ]
    return pl.pallas_call(kernel, out_shape=shapes)(w_up, w_down, *mine, *other)


def smooth_parts(values):
    share = 0.5 + 0.5 * lax.erf(values * (0.5**0.5))
    density = jnp.exp(-0.5 * values * values) * ((0.5 / jnp.pi) ** 0.5)
    return values * share, share + values * density


def one_table(pos, doc, rate, scaling):
    keeping = (pos[:, None] >= pos[None, :]) & (doc[:, None] == doc[None, :])
    spacing = jnp.where(keeping, (pos[:, None] - pos[None, :]).astype(jnp.float32), 0.0)
    return jnp.where(keeping, jnp.exp(rate * spacing) * scaling, 0.0)


def ctx_sum(x):
    return lax.psum_scatter(x, "ctx", scatter_dimension=0, tiled=True)


def body_heads(
    tokens,
    cotangent,
    w_query,
    w_key,
    w_value,
    w_gate,
    w_out,
    w_up,
    w_down,
    norm_gains,
    norm_biases,
    block_deal,
    doc_lengths,
):
    low = jnp.bfloat16
    ctx_size = lax.axis_size("ctx")
    fsdp_size = lax.axis_size("fsdp")
    tok_rows = tokens.shape[2]
    full_length = tok_rows * ctx_size
    width = tokens.shape[3]
    share = width // (ctx_size * fsdp_size)
    grad_scale = float(MICRO * fsdp_size * full_length) ** (-0.5)
    ctx_rank = lax.axis_index("ctx")
    fsdp_rank = lax.axis_index("fsdp")
    pos = stored_positions(block_deal, full_length, BLOCK)
    rate = jnp.log1p(-jnp.exp2(-5.0 - ctx_rank.astype(jnp.float32)))
    scaling = DK ** (-0.5)

    own_in = head_columns(w_query, w_key, w_value, w_gate, ctx_rank)
    tokens = after(tokens, own_in)
    rows_in = []
    norm_one = []
    x_own = []
    for m in range(MICRO):
        rows_in.append(after(tokens[m, 0], *x_own[-1:]).astype(jnp.float32))
        norm_one.append(jax.vjp(layer_norm, rows_in[m], norm_gains[0], norm_biases[0]))
        x_own.append(norm_one[m][0].astype(low))
    grad_rows = [cotangent[m, 0].astype(jnp.float32) for m in range(MICRO)]
    x_all = [lax.all_gather(x, "ctx", axis=0, tiled=True) for x in x_own]
    in_first = gather_first(own_in)
    ffn_cut = cut_ffn(w_up, w_down)
    out_cut = out_pieces(w_out, ctx_rank, fsdp_rank, fsdp_size)
    in_first = lax.optimization_barrier(tuple(in_first) + tuple(ffn_cut) + tuple(out_cut))[:2]
    in_second = gather_second(*in_first)
    w_in = by_rank(own_in, *in_first, *in_second)
    out_cut = lax.optimization_barrier(tuple(out_cut) + tuple(in_first))[: len(out_cut)]
    out_parts = scatter_quarters(out_cut, ctx_size, fsdp_size)

    def mix(m, x_now, *earlier):
        doc = document_ids(pos, doc_lengths[m, 0])
        table = one_table(pos, doc, rate, scaling)
        joint = jnp.dot(x_now, w_in[:, : 2 * DK + DV], preferred_element_type=jnp.float32).astype(low)
        joint = after(joint, *earlier)
        gate_pre = jnp.dot(x_now, w_in[:, 2 * DK + DV :], preferred_element_type=jnp.float32)
        query, key, value = joint[:, :DK], joint[:, DK : 2 * DK], joint[:, 2 * DK :]
        attend = (contract_rows(query, key) * table).astype(low)
        retained = add_single(attend, value)
        mixed, mix_pull = jax.vjp(gated_mix, gate_pre, retained)
        return table, query, key, value, attend, mix_pull, mixed.astype(low)

    kept = [mix(0, x_all[0])]
    out_parts = lax.optimization_barrier(tuple(out_parts) + (kept[0][4],))[:-1]
    quarter = choose_quarter(out_parts, ctx_rank, fsdp_rank)
    out_first = gather_first(quarter)
    out_second = gather_second(*out_first)
    w_head = by_rank(quarter, *out_first, *out_second)
    cot_own = after(cotangent.reshape(MICRO * tok_rows, width), *out_first)
    cot_first = gather_first(cot_own)
    ffn_cut = lax.optimization_barrier(tuple(ffn_cut) + tuple(out_second))[: len(ffn_cut)]
    ffn_mine = [xy_swap(ffn_cut[bit - 1], bit) for bit in range(1, fsdp_size)]
    part = add_single(kept[0][6], w_head).astype(low)
    attn_out = [ctx_sum(after(part, *x_all[1:], *cot_first))]
    for m in range(1, MICRO):
        kept.append(mix(m, after(x_all[m], *cot_first), *ffn_mine[:1]))
        part = add_single(kept[m][6], w_head).astype(low)
        attn_out.append(ctx_sum(after(part, *ffn_mine)))
    cot_second = gather_second(*cot_first)
    def enter(m):
        hidden = rows_in[m] + attn_out[m].astype(jnp.float32)
        normed_two, pull_two = jax.vjp(layer_norm, hidden, norm_gains[1], norm_biases[1])
        two_own = normed_two.astype(low)
        return hidden, pull_two, two_own, gather_first(two_own)

    ffn_other = [core_swap(x) for x in ffn_mine]
    attn_out[0] = after(attn_out[0], *ffn_other, *cot_second)
    entered = [enter(0)]
    up_own, down_own = join_ffn(w_up, w_down, ffn_mine, ffn_other)
    cot_all = [
        place(
            (fsdp_size * tok_rows, width),
            [
                (cot_own, m * tok_rows, tok_rows, 0, 0),
                (cot_first[0], m * tok_rows, tok_rows, tok_rows, 0),
                (cot_second[m], 0, tok_rows, 2 * tok_rows, 0),
                (cot_first[1], m * tok_rows, tok_rows, 3 * tok_rows, 0),
            ],
        )
        for m in range(MICRO)
    ]

    outs = [None] * MICRO
    grad_attn = []
    grad_hidden = []
    ffn_kept = []
    norm_two_terms = []

    for m in range(MICRO):
        hidden, pull_two, two_own, two_first = entered[m]
        if m == 0:
            two_first = lax.optimization_barrier(tuple(two_first) + (up_own, down_own))[:2]
            two_second = gather_second(*two_first)
        two_second = lax.optimization_barrier(tuple(two_second) + (cot_all[m],))[:2]
        two_all = by_offset(two_own, *two_first, *two_second)
        active, slope = smooth_parts(add_single(two_all, up_own))
        active_low, slope = lax.optimization_barrier((active.astype(low), slope))
        grad_up = (back_rows(cot_all[m], down_own) * slope).astype(low)
        norm_part = back_rows(grad_up, up_own).astype(low)
        sent = rows_first(norm_part)
        later = ()
        if m + 1 < MICRO:
            attn_out[m + 1] = after(attn_out[m + 1], *sent)
            entered.append(enter(m + 1))
            sent = lax.optimization_barrier(tuple(sent) + (entered[m + 1][2],))[:2]
            two_second = gather_second(*entered[m + 1][3])
            later = two_second
        grad_norm_two = after(rows_second(norm_part, *sent), *grad_attn[-1:], *later)
        grad_ln, gain_two, bias_two = pull_two(grad_norm_two)
        norm_two_terms.append((gain_two, bias_two))
        total = grad_rows[m] + grad_ln
        grad_hidden.append(total)
        grad_attn.append(total.astype(low))
        ffn_kept.append((two_all, grad_up, active_low, hidden))

    grad_all = [lax.all_gather(grad_attn[m], "ctx", axis=0, tiled=True) for m in range(MICRO)]

    def unmix(m, grad_now):
        table, query, key, value, attend, mix_pull, mixed_low = kept[m]
        grad_mixed = back_rows(grad_now, w_head)
        grad_gate, grad_ret = mix_pull(grad_mixed)
        ret_low = grad_ret.astype(low)
        grad_scores = (contract_rows(ret_low, value) * table).astype(low)
        grad_query = add_single(grad_scores, key).astype(low)
        grad_key = contract_cols(grad_scores, query).astype(low)
        grad_value = contract_cols(attend, ret_low).astype(low)
        return jnp.concatenate([grad_query, grad_key, grad_value, grad_gate.astype(low)], axis=1)

    terms = []
    sums = []
    fill = ()
    for m in range(MICRO):
        grad_now = after(grad_all[m], *(grad_attn[1:] if m == 0 else terms[-1:]), *fill)
        grad_in = unmix(m, grad_now)
        part = back_rows(grad_in, w_in).astype(low)
        terms.append(part)
        sums.append(ctx_sum(after(part, *grad_all[m + 1 :], *sums[-1:])))
        x_now, grad_in = lax.optimization_barrier((x_all[m], grad_in, part))[:2]
        in_now = contract_cols(x_now, grad_in)
        if m == 0:
            in_term = in_now
            sums[m] = after(sums[m], in_term)
            ready = [after(ffn_kept[n][2], part, grad_attn[n]) for n in range(MICRO)]
            fill = tuple(add_single(ready[n], down_own).astype(low) for n in range(MICRO))
        else:
            in_term = (in_term + in_now).astype(low)
    in_view = in_term.reshape(ctx_size, fsdp_size, share, -1)
    in_blocks_out = [pick(in_view, fsdp_rank ^ j, 1, 1)[:, 0] for j in range(fsdp_size)]
    in_sent = reduce_first(in_blocks_out)
    up_grad = sum(contract_cols(k[0], after(k[1], in_term)) for k in ffn_kept).astype(low)
    down_grad = sum(
        contract_cols(after(ready[n], up_grad), cot_all[n]) for n in range(MICRO)
    ).astype(low)
    sums[-1] = after(sums[-1], up_grad, down_grad, *in_sent)
    up_sum = ctx_sum(after(up_grad, sums[-1]))
    down_sum = ctx_sum(after(down_grad, sums[-1]))
    in_sum = reduce_second(in_blocks_out, *in_sent).astype(low)
    out_term = sum(
        contract_cols(after(kept[m][6], down_grad), grad_all[m]) for m in range(MICRO)
    ).astype(low)

    grad_tokens = []
    norm_one_terms = []
    for m in range(MICRO):
        grad_ln, gain_one, bias_one = norm_one[m][1](sums[m].astype(jnp.float32))
        norm_one_terms.append((gain_one, bias_one))
        grad_tokens.append(grad_hidden[m] + grad_ln)

    gain_rows = [sum(t[0] for t in norm_one_terms), sum(t[0] for t in norm_two_terms)]
    bias_rows = [sum(t[1] for t in norm_one_terms), sum(t[1] for t in norm_two_terms)]
    norm_lines = sum_over(jnp.stack(gain_rows + bias_rows), "ctx")
    in_mine = lax.all_to_all(
        after(in_sum, norm_lines), "ctx", split_axis=0, concat_axis=0, tiled=True
    )
    norm_sums = sum_over(norm_lines, "fsdp")
    for n in range(MICRO):
        ffn_part = after(fill[n], in_sum, norm_sums)
        outs[n] = (ffn_kept[n][3] + rows_second(ffn_part, *rows_first(ffn_part))).astype(low)
    out_term = after(out_term, in_sum, norm_sums)
    rows = DV // fsdp_size
    out_blocks = [pick(out_term, fsdp_rank ^ j, rows, 0) for j in range(fsdp_size)]
    g_out = reduce_second(out_blocks, *reduce_first(out_blocks))

    up_view = up_sum.reshape(fsdp_size, share, -1)
    pieces = [lax.dynamic_index_in_dim(up_view, fsdp_rank, 0, keepdims=False)]
    for bit in range(1, fsdp_size):
        pieces.append(
            xy_swap(lax.dynamic_index_in_dim(up_view, fsdp_rank ^ bit, 0, keepdims=False), bit)
        )
    in_mine = after(in_mine, norm_sums)
    def by_head(first, size):
        part = in_mine[:, :, first : first + size].transpose(1, 0, 2)
        return part.reshape(share, -1).astype(jnp.float32) * grad_scale

    g_query = by_head(0, DK)
    g_key = by_head(DK, DK)
    g_value = by_head(2 * DK, DV)
    g_gate = by_head(2 * DK + DV, DV)

    pieces = [p.reshape(share, ctx_size, -1) for p in in_rank_order(pieces, fsdp_rank)]
    g_up = jnp.stack(pieces, axis=2).reshape(share, FF).astype(jnp.float32) * grad_scale
    down_sum = after(down_sum, g_query, g_key, g_value, g_gate, g_up)

    norm_sums = pick(norm_sums, ctx_rank * fsdp_size + fsdp_rank, share, 1) * grad_scale
    return (
        jnp.stack(outs)[:, None],
        jnp.stack(grad_tokens)[:, None],
        g_query,
        g_key,
        g_value,
        g_gate,
        g_out * grad_scale,
        g_up,
        down_sum.astype(jnp.float32) * grad_scale,
        norm_sums[:2],
        norm_sums[2:],
    )


def solution(mesh):
    in_specs = (
        P(None, "fsdp", "ctx", None),
        P(None, "fsdp", "ctx", None),
        P("fsdp", None),
        P("fsdp", None),
        P("fsdp", None),
        P("fsdp", None),
        P("fsdp", None),
        P("fsdp", None),
        P("fsdp", None),
        P(),
        P(),
        P(),
        P(None, "fsdp", None),
    )
    out_specs = (
        P(None, "fsdp", "ctx", None),
        P(None, "fsdp", "ctx", None),
        P(("ctx", "fsdp"), None),
        P(("ctx", "fsdp"), None),
        P(("ctx", "fsdp"), None),
        P(("ctx", "fsdp"), None),
        P(("ctx", "fsdp"), None),
        P(("ctx", "fsdp"), None),
        P(("ctx", "fsdp"), None),
        P(None, ("ctx", "fsdp")),
        P(None, ("ctx", "fsdp")),
    )
    by_heads = mesh.shape["ctx"] == HEADS and mesh.shape["fsdp"] == 4
    chosen = body_heads if by_heads else body
    return jax.shard_map(chosen, mesh=mesh, in_specs=in_specs, out_specs=out_specs, check_vma=False)
```

```python
import jax
import jax.numpy as jnp
from jax import lax
from jax.experimental import pallas as pl
from jax.sharding import PartitionSpec as P

HEADS = 8
DK = 256
DV = 512
FF = 4096
MICRO = 2
QW = 2048
VW = 4096
BLOCK = 64


epsilon = 1e-05
group_floor = 1.0


def layer_norm(values, gain_row, offset):
    center = jnp.mean(values, axis=-1, keepdims=True)
    centred = values - center
    spread = jnp.mean(centred * centred, axis=-1, keepdims=True)
    return centred * lax.rsqrt(spread + epsilon) * gain_row + offset


def gated_mix(gate_pre, retained):
    number = retained.shape[0]
    grouped = retained.reshape(number, -1, DV)
    center = jnp.mean(grouped, axis=-1, keepdims=True)
    centred = grouped - center
    spread = jnp.mean(centred * centred, axis=-1, keepdims=True)
    normed = (centred * lax.rsqrt(spread + group_floor)).reshape(number, -1)
    return jax.nn.silu(gate_pre) * normed


def smooth_act(values):
    return jax.nn.gelu(values, approximate=False)


def stored_positions(block_deal, full_length, block_size):
    stored = jnp.arange(full_length, dtype=jnp.int32)
    block_ids = stored // block_size
    slots_all = jnp.arange(block_deal.shape[0], dtype=jnp.int32)
    picked = jnp.sum(
        jnp.where(block_ids[:, None] == slots_all[None, :], block_deal[None, :], 0),
        axis=1,
        dtype=jnp.int32,
    )
    return picked * block_size + stored % block_size


def document_ids(positions, doc_sizes):
    starts = jnp.cumsum(doc_sizes, dtype=jnp.int32) - doc_sizes
    return (
        jnp.sum((positions[:, None] >= starts[None, :]).astype(jnp.int32), axis=1, dtype=jnp.int32)
        - 1
    )


def decay_table(query_pos, query_doc, key_pos, key_doc, decay_log, scaling):
    keeping = (query_pos[:, None] >= key_pos[None, :]) & (query_doc[:, None] == key_doc[None, :])
    spacing = jnp.where(keeping, (query_pos[:, None] - key_pos[None, :]).astype(jnp.float32), 0.0)
    factor = jnp.exp(decay_log[:, None, None] * spacing[None])
    return jnp.where(keeping[None], factor * scaling, 0.0)


def contract_rows(left, right):
    return lax.dot_general(
        left, right, (((1,), (1,)), ((), ())), preferred_element_type=jnp.float32
    )


def contract_cols(left, right):
    return lax.dot_general(
        left, right, (((0,), (0,)), ((), ())), preferred_element_type=jnp.float32
    )


def add_single(left, weight_piece):
    return jnp.dot(left, weight_piece, preferred_element_type=jnp.float32)


def back_rows(left, weight_piece):
    return contract_rows(left, weight_piece)


def weight_term(kept_acts, number):
    normed_one, grads_in, normed_two, grads_up, mixed_all, grads_attn, active_all, grads_ffn = (
        kept_acts
    )
    pieces = [
        contract_cols(normed_one, grads_in),
        contract_cols(normed_two, grads_up),
        contract_cols(mixed_all, grads_attn).reshape(number, -1),
        contract_cols(active_all, grads_ffn).reshape(number, -1),
    ]
    return jnp.concatenate(pieces, axis=1)


def body(
    tokens,
    cotangent,
    w_query,
    w_key,
    w_value,
    w_gate,
    w_out,
    w_up,
    w_down,
    norm_gains,
    norm_biases,
    block_deal,
    doc_lengths,
):
    ctx_size = lax.axis_size("ctx")
    tok_rows = tokens.shape[2]
    full_length = tok_rows * ctx_size
    model_width = tokens.shape[3]
    share_rows = model_width // lax.axis_size(("ctx", "fsdp"))
    grad_scale = float(MICRO * lax.axis_size("fsdp") * full_length) ** (-0.5)
    own_start = lax.axis_index("ctx") * tok_rows
    key_pos = stored_positions(block_deal, full_length, BLOCK)
    query_pos = lax.dynamic_slice_in_dim(key_pos, own_start, tok_rows)
    decay_log = jnp.log1p(-jnp.exp2(-5.0 - jnp.arange(HEADS).astype(jnp.float32)))
    scaling = DK ** (-0.5)
    out_list = []
    grad_list = []
    weight_sum = None
    gain_sum = jnp.zeros((2, model_width), jnp.float32)
    bias_sum = jnp.zeros((2, model_width), jnp.float32)
    for batch_index in range(MICRO):
        rows_in = tokens[batch_index, 0].astype(jnp.float32)
        grad_rows = cotangent[batch_index, 0].astype(jnp.float32)
        key_doc = document_ids(key_pos, doc_lengths[batch_index, 0])
        query_doc = lax.dynamic_slice_in_dim(key_doc, own_start, tok_rows)
        table = decay_table(query_pos, query_doc, key_pos, key_doc, decay_log, scaling)
        normed_one, norm_pull_one = jax.vjp(layer_norm, rows_in, norm_gains[0], norm_biases[0])
        low_one = normed_one.astype(jnp.bfloat16)
        pieces = (
            lax.all_gather(w_query, "fsdp", axis=0, tiled=True),
            lax.all_gather(w_key, "fsdp", axis=0, tiled=True),
            lax.all_gather(w_value, "fsdp", axis=0, tiled=True),
            lax.all_gather(w_gate, "fsdp", axis=0, tiled=True),
        )
        query_f, key_f, value_f, gate_pre = tuple(
            (
                jnp.dot(low_one, weight_piece, preferred_element_type=jnp.float32)
                for weight_piece in pieces
            )
        )
        query_low = query_f.astype(jnp.bfloat16)
        key_low = key_f.astype(jnp.bfloat16)
        value_low = value_f.astype(jnp.bfloat16)
        keys_all, values_all = (
            lax.all_gather(key_low, "ctx", axis=0, tiled=True),
            lax.all_gather(value_low, "ctx", axis=0, tiled=True),
        )
        query_heads = query_low.reshape(tok_rows, HEADS, DK)
        key_heads = keys_all.reshape(full_length, HEADS, DK)
        value_heads = values_all.reshape(full_length, HEADS, DV)
        scores = jnp.einsum(
            "thd,shd->hts", query_heads, key_heads, preferred_element_type=jnp.float32
        )
        attend = (scores * table).astype(jnp.bfloat16)
        retained = jnp.einsum(
            "hts,shd->thd", attend, value_heads, preferred_element_type=jnp.float32
        ).reshape(tok_rows, VW)
        mixed, mix_pull = jax.vjp(gated_mix, gate_pre, retained)
        mixed_low = mixed.astype(jnp.bfloat16)
        attn_out = add_single(mixed_low, lax.all_gather(w_out, "fsdp", axis=0, tiled=True))
        hidden = rows_in + attn_out
        normed_two, norm_pull_two = jax.vjp(layer_norm, hidden, norm_gains[1], norm_biases[1])
        low_two = normed_two.astype(jnp.bfloat16)
        up_pre = add_single(low_two, lax.all_gather(w_up, "fsdp", axis=0, tiled=True))
        active, act_pull = jax.vjp(smooth_act, up_pre)
        active_low = active.astype(jnp.bfloat16)
        ffn_out = add_single(active_low, lax.all_gather(w_down, "fsdp", axis=0, tiled=True))
        out_list.append((hidden + ffn_out).astype(jnp.bfloat16))
        grad_ffn = grad_rows.astype(jnp.bfloat16)
        grad_act = back_rows(grad_ffn, lax.all_gather(w_down, "fsdp", axis=0, tiled=True))
        grad_up = act_pull(grad_act)[0].astype(jnp.bfloat16)
        grad_norm_two = back_rows(grad_up, lax.all_gather(w_up, "fsdp", axis=0, tiled=True))
        grad_hidden_ln, grad_gain_two, grad_bias_two = norm_pull_two(grad_norm_two)
        grad_hidden = grad_rows + grad_hidden_ln
        grad_attn = grad_hidden.astype(jnp.bfloat16)
        grad_mixed = back_rows(grad_attn, lax.all_gather(w_out, "fsdp", axis=0, tiled=True))
        grad_gate_f, grad_ret_f = mix_pull(grad_mixed)
        grad_gate = grad_gate_f.astype(jnp.bfloat16)
        ret_low = grad_ret_f.astype(jnp.bfloat16)
        ret_heads = ret_low.reshape(tok_rows, HEADS, DV)
        grad_attend = jnp.einsum(
            "thd,shd->hts", ret_heads, value_heads, preferred_element_type=jnp.float32
        )
        grad_scores = (grad_attend * table).astype(jnp.bfloat16)
        grad_query = (
            jnp.einsum("hts,shd->thd", grad_scores, key_heads, preferred_element_type=jnp.float32)
            .reshape(tok_rows, QW)
            .astype(jnp.bfloat16)
        )
        key_part = jnp.einsum(
            "hts,thd->shd", grad_scores, query_heads, preferred_element_type=jnp.float32
        ).reshape(tok_rows * lax.axis_size("ctx"), QW)
        value_part = jnp.einsum(
            "hts,thd->shd", attend, ret_heads, preferred_element_type=jnp.float32
        ).reshape(tok_rows * lax.axis_size("ctx"), VW)
        key_value_sum = lax.psum_scatter(
            jnp.concatenate([key_part, value_part], axis=1).astype(jnp.bfloat16),
            "ctx",
            scatter_dimension=0,
            tiled=True,
        ).astype(jnp.float32)
        grad_key = key_value_sum[:, :QW].astype(jnp.bfloat16)
        grad_value = key_value_sum[:, QW:].astype(jnp.bfloat16)
        term_now = (
            contract_rows(grad_query, lax.all_gather(w_query, "fsdp", axis=0, tiled=True))
            + contract_rows(grad_key, lax.all_gather(w_key, "fsdp", axis=0, tiled=True))
            + contract_rows(grad_value, lax.all_gather(w_value, "fsdp", axis=0, tiled=True))
            + contract_rows(grad_gate, lax.all_gather(w_gate, "fsdp", axis=0, tiled=True))
        )
        grad_rows_ln, grad_gain_one, grad_bias_one = norm_pull_one(term_now)
        grad_list.append(grad_hidden + grad_rows_ln)
        gain_sum = gain_sum + jnp.stack([grad_gain_one, grad_gain_two])
        bias_sum = bias_sum + jnp.stack([grad_bias_one, grad_bias_two])
        kept_now = (
            low_one,
            jnp.concatenate([grad_query, grad_key, grad_value, grad_gate], axis=1),
            low_two,
            grad_up,
            mixed_low,
            grad_attn,
            active_low,
            grad_ffn,
        )
        term_sum = lax.psum_scatter(
            weight_term(kept_now, share_rows * lax.axis_size(("ctx", "fsdp"))),
            ("ctx", "fsdp"),
            scatter_dimension=0,
            tiled=True,
        )
        weight_sum = term_sum if weight_sum is None else weight_sum + term_sum
    weight_sum = weight_sum * grad_scale
    bounds = [QW, 2 * QW, 2 * QW + VW, 2 * QW + 2 * VW, 2 * QW + 2 * VW + FF, 2 * QW + 3 * VW + FF]
    g_query, g_key, g_value, g_gate, g_up, g_out_flat, g_down_flat = jnp.split(
        weight_sum, bounds, axis=1
    )
    g_out = g_out_flat.reshape(share_rows * (VW // model_width), model_width)
    g_down = g_down_flat.reshape(share_rows * (FF // model_width), model_width)
    gain_grads, bias_grads = (
        lax.psum_scatter(gain_sum, ("ctx", "fsdp"), scatter_dimension=1, tiled=True),
        lax.psum_scatter(bias_sum, ("ctx", "fsdp"), scatter_dimension=1, tiled=True),
    )
    gain_grads = gain_grads * grad_scale
    bias_grads = bias_grads * grad_scale
    output = jnp.stack(out_list)[:, None]
    grad_tokens = jnp.stack(grad_list)[:, None]
    return (
        output,
        grad_tokens,
        g_query,
        g_key,
        g_value,
        g_gate,
        g_out,
        g_up,
        g_down,
        gain_grads,
        bias_grads,
    )


def xy_swap(x, bit):
    return lax.ppermute(x, "fsdp", [(i, i ^ bit) for i in range(lax.axis_size("fsdp"))])


def core_swap(x):
    return lax.ppermute(x, "ctx", [(i, i ^ 1) for i in range(lax.axis_size("ctx"))])


def after(x, *earlier):
    return lax.optimization_barrier((x,) + tuple(earlier))[0]


def place(shape, items):
    arrays = []
    for item in items:
        if not any(item[0] is a for a in arrays):
            arrays.append(item[0])
    slots = [[item[0] is a for a in arrays].index(True) for item in items]
    kind = arrays[0].dtype

    def kernel(*refs):
        out = refs[len(arrays)]
        rank = lax.axis_index("fsdp")
        core = lax.axis_index("ctx") % 2
        for number, (array, start, rows, row, column) in enumerate(items):
            width = array.shape[1]
            step = min(rows, 64)
            source = refs[slots[number]]
            base = row(rank, core) if callable(row) else row

            def copy(first, width=width, step=step, source=source, base=base, start=start, rows=rows):
                def one(turn, carry):
                    place_in = pl.multiple_of(start + turn * step, step)
                    place_out = pl.multiple_of(base + turn * step, step)
                    out[pl.ds(place_out, step), first : first + width] = source[
                        pl.ds(place_in, step), :
                    ]
                    return carry

                lax.fori_loop(0, rows // step, one, 0)

            if callable(column):
                for which in range(2):
                    pl.when(core == which)(lambda which=which: copy(column(rank, which)))
            else:
                copy(column)

    size = shape[0] * shape[1] * jnp.dtype(kind).itemsize
    return pl.pallas_call(
        kernel,
        out_shape=jax.ShapeDtypeStruct(shape, kind),
        cost_estimate=pl.CostEstimate(flops=0, bytes_accessed=2 * size, transcendentals=0),
    )(*arrays)


def gather_first(x):
    return xy_swap(x, 1), xy_swap(x, 2)


def gather_second(first, second):
    half = first.shape[0] // 2
    return xy_swap(first[:half], 2), xy_swap(second[half:], 1)


def by_offset(x, first, second, low_part, high_part):
    rows, half = x.shape[0], x.shape[0] // 2
    return place(
        (4 * rows, x.shape[1]),
        [
            (x, 0, rows, 0, 0),
            (first, 0, rows, rows, 0),
            (low_part, 0, half, 2 * rows, 0),
            (high_part, 0, half, 2 * rows + half, 0),
            (second, 0, rows, 3 * rows, 0),
        ],
    )


def by_rank(x, first, second, low_part, high_part):
    rows, half = x.shape[0], x.shape[0] // 2
    return place(
        (4 * rows, x.shape[1]),
        [
            (x, 0, rows, lambda f, c: f * rows, 0),
            (first, 0, rows, lambda f, c: (f ^ 1) * rows, 0),
            (low_part, 0, half, lambda f, c: (f ^ 3) * rows, 0),
            (high_part, 0, half, lambda f, c: (f ^ 3) * rows + half, 0),
            (second, 0, rows, lambda f, c: (f ^ 2) * rows, 0),
        ],
    )


def rows_first(part):
    rows, half = part.shape[0] // 4, part.shape[1] // 2
    return xy_swap(part[rows : 3 * rows, :half], 1), xy_swap(part[2 * rows :, half:], 2)


def rows_second(part, left_in, right_in):
    rows, half = part.shape[0] // 4, part.shape[1] // 2
    wide = lambda v: v.astype(jnp.float32)
    left_far = wide(part[3 * rows :, :half]) + wide(left_in[rows:])
    right_far = wide(part[rows : 2 * rows, half:]) + wide(right_in[:rows])
    left_last = xy_swap(left_far.astype(jnp.bfloat16), 2)
    right_last = xy_swap(right_far.astype(jnp.bfloat16), 1)
    left = wide(part[:rows, :half]) + wide(left_in[:rows]) + wide(left_last)
    right = wide(part[:rows, half:]) + wide(right_in[rows:]) + wide(right_last)
    return jnp.concatenate([left, right], axis=1)


def reduce_first(blocks):
    half = blocks[0].shape[-1] // 2
    left_in = xy_swap(jnp.stack([blocks[1][..., :half], blocks[3][..., :half]]), 1)
    right_in = xy_swap(jnp.stack([blocks[2][..., half:], blocks[3][..., half:]]), 2)
    return left_in, right_in


def reduce_second(blocks, left_in, right_in):
    half = blocks[0].shape[-1] // 2
    wide = lambda v: v.astype(jnp.float32)
    left_far = wide(blocks[2][..., :half]) + wide(left_in[1])
    right_far = wide(blocks[1][..., half:]) + wide(right_in[1])
    left_last = xy_swap(left_far.astype(jnp.bfloat16), 2)
    right_last = xy_swap(right_far.astype(jnp.bfloat16), 1)
    left = wide(blocks[0][..., :half]) + wide(left_in[0]) + wide(left_last)
    right = wide(blocks[0][..., half:]) + wide(right_in[0]) + wide(right_last)
    return jnp.concatenate([left, right], axis=-1)


def sum_over(x, axis):
    size = lax.axis_size(axis)
    bit = 1
    while bit < size:
        x = x + lax.ppermute(x, axis, [(i, i ^ bit) for i in range(size)])
        bit *= 2
    return x


def in_rank_order(blocks, rank):
    odd = (rank % 2) == 1
    upper = (rank // 2) == 1
    one = [
        jnp.where(odd, blocks[1], blocks[0]),
        jnp.where(odd, blocks[0], blocks[1]),
        jnp.where(odd, blocks[3], blocks[2]),
        jnp.where(odd, blocks[2], blocks[3]),
    ]
    return [
        jnp.where(upper, one[2], one[0]),
        jnp.where(upper, one[3], one[1]),
        jnp.where(upper, one[0], one[2]),
        jnp.where(upper, one[1], one[3]),
    ]


def pick(x, index, size, axis):
    return lax.dynamic_slice_in_dim(x, index * size, size, axis)


def head_columns(w_query, w_key, w_value, w_gate, ctx_rank):
    return jnp.concatenate(
        [
            pick(w_query, ctx_rank, DK, 1),
            pick(w_key, ctx_rank, DK, 1),
            pick(w_value, ctx_rank, DV, 1),
            pick(w_gate, ctx_rank, DV, 1),
        ],
        axis=1,
    )


def out_pieces(w_out, ctx_rank, fsdp_rank, fsdp_size):
    rows = DV // fsdp_size
    start = (ctx_rank % 2) * DV
    return [
        lax.dynamic_slice_in_dim(w_out, start + (fsdp_rank ^ bit) * rows, rows, 0)
        for bit in range(fsdp_size)
    ]


def scatter_quarters(cuts, ctx_size, fsdp_size):
    parts = [cuts[0]]
    for bit in range(1, fsdp_size):
        pairs = [
            (c * fsdp_size + c // 2, c * fsdp_size + ((c // 2) ^ bit)) for c in range(ctx_size)
        ]
        parts.append(lax.ppermute(cuts[bit], ("ctx", "fsdp"), pairs))
    return parts


def choose_quarter(parts, ctx_rank, fsdp_rank):
    quarter = parts[0]
    for bit in range(1, len(parts)):
        quarter = jnp.where((fsdp_rank ^ (ctx_rank // 2)) == bit, parts[bit], quarter)
    return quarter


def copy_block(target, row, column, source, row_in, column_in, rows, width):
    step = min(rows, 64)

    def one(turn, carry):
        place_in = pl.multiple_of(row_in + turn * step, step)
        place_out = pl.multiple_of(row + turn * step, step)
        taken = source[pl.ds(place_in, step), pl.ds(column_in, width)]
        target[pl.ds(place_out, step), pl.ds(column, width)] = taken
        return carry

    lax.fori_loop(0, rows // step, one, 0)


def cut_ffn(w_up, w_down):
    ctx_size, fsdp_size = lax.axis_size("ctx"), lax.axis_size("fsdp")
    rows, width = w_up.shape[0], w_down.shape[1]
    unit, half = FF // (ctx_size * fsdp_size), ctx_size // 2
    wide = half * unit
    fourth = width // 4

    def kernel(up, down, *outs):
        rank = lax.axis_index("fsdp")
        core = lax.axis_index("ctx") % 2
        for number in range(fsdp_size - 1):
            other = rank ^ (number + 1)
            for i in range(half):
                column = pl.multiple_of(((core * half + i) * fsdp_size + other) * unit, unit)
                copy_block(outs[number], 0, i * unit, up, 0, column, rows, unit)
            for i in range(2):
                for q in range(2):
                    column = pl.multiple_of(core * 2 * fourth + q * fourth, fourth)
                    row = (i * fsdp_size + other) * unit
                    copy_block(
                        outs[number], (2 * i + q) * unit, wide, down, row, column, unit, fourth
                    )

    kind = jax.ShapeDtypeStruct((rows, wide + fourth), w_up.dtype)
    return list(pl.pallas_call(kernel, out_shape=[kind] * (fsdp_size - 1))(w_up, w_down))


def join_ffn(w_up, w_down, mine, other):
    ctx_size, fsdp_size = lax.axis_size("ctx"), lax.axis_size("fsdp")
    rows, width = w_up.shape[0], w_down.shape[1]
    unit, half = FF // (ctx_size * fsdp_size), ctx_size // 2
    wide = half * unit
    fourth = width // 4

    def kernel(up, down, *refs):
        up_out, down_out = refs[2 * len(mine) :]
        rank = lax.axis_index("fsdp")
        core = lax.axis_index("ctx") % 2
        for i in range(ctx_size):
            column = pl.multiple_of((i * fsdp_size + rank) * unit, unit)
            copy_block(up_out, rank * rows, i * unit, up, 0, column, rows, unit)
        for i in range(2):
            copy_block(
                down_out, (2 * rank + i) * unit, 0, down, (i * fsdp_size + rank) * unit, 0, unit, width
            )
        for number in range(2 * len(mine)):
            source = rank ^ (number % len(mine) + 1)
            part = core if number < len(mine) else 1 - core
            column = pl.multiple_of(part * wide, wide)
            copy_block(up_out, source * rows, column, refs[number], 0, 0, rows, wide)
            for i in range(2):
                for q in range(2):
                    column = pl.multiple_of(part * 2 * fourth + q * fourth, fourth)
                    row = (2 * source + i) * unit
                    copy_block(
                        down_out, row, column, refs[number], (2 * i + q) * unit, wide, unit, fourth
                    )

    shapes = [
        jax.ShapeDtypeStruct((fsdp_size * rows, FF // fsdp_size), w_up.dtype),
        jax.ShapeDtypeStruct((FF // fsdp_size, width), w_up.dtype),
    ]
    return pl.pallas_call(kernel, out_shape=shapes)(w_up, w_down, *mine, *other)


def smooth_parts(values):
    share = 0.5 + 0.5 * lax.erf(values * (0.5**0.5))
    density = jnp.exp(-0.5 * values * values) * ((0.5 / jnp.pi) ** 0.5)
    return values * share, share + values * density


def one_table(pos, doc, rate, scaling):
    keeping = (pos[:, None] >= pos[None, :]) & (doc[:, None] == doc[None, :])
    spacing = jnp.where(keeping, (pos[:, None] - pos[None, :]).astype(jnp.float32), 0.0)
    return jnp.where(keeping, jnp.exp(rate * spacing) * scaling, 0.0)


def ctx_sum(x):
    return lax.psum_scatter(x, "ctx", scatter_dimension=0, tiled=True)


def body_heads(
    tokens,
    cotangent,
    w_query,
    w_key,
    w_value,
    w_gate,
    w_out,
    w_up,
    w_down,
    norm_gains,
    norm_biases,
    block_deal,
    doc_lengths,
):
    low = jnp.bfloat16
    ctx_size = lax.axis_size("ctx")
    fsdp_size = lax.axis_size("fsdp")
    tok_rows = tokens.shape[2]
    full_length = tok_rows * ctx_size
    width = tokens.shape[3]
    share = width // (ctx_size * fsdp_size)
    grad_scale = float(MICRO * fsdp_size * full_length) ** (-0.5)
    ctx_rank = lax.axis_index("ctx")
    fsdp_rank = lax.axis_index("fsdp")
    pos = stored_positions(block_deal, full_length, BLOCK)
    rate = jnp.log1p(-jnp.exp2(-5.0 - ctx_rank.astype(jnp.float32)))
    scaling = DK ** (-0.5)

    own_in = head_columns(w_query, w_key, w_value, w_gate, ctx_rank)
    tokens = after(tokens, own_in)
    rows_in = []
    norm_one = []
    x_own = []
    for m in range(MICRO):
        rows_in.append(after(tokens[m, 0], *x_own[-1:]).astype(jnp.float32))
        norm_one.append(jax.vjp(layer_norm, rows_in[m], norm_gains[0], norm_biases[0]))
        x_own.append(norm_one[m][0].astype(low))
    grad_rows = [cotangent[m, 0].astype(jnp.float32) for m in range(MICRO)]
    x_all = [lax.all_gather(x, "ctx", axis=0, tiled=True) for x in x_own]
    in_first = gather_first(own_in)
    ffn_cut = cut_ffn(w_up, w_down)
    out_cut = out_pieces(w_out, ctx_rank, fsdp_rank, fsdp_size)
    in_first = lax.optimization_barrier(tuple(in_first) + tuple(ffn_cut) + tuple(out_cut))[:2]
    in_second = gather_second(*in_first)
    w_in = by_rank(own_in, *in_first, *in_second)
    out_cut = lax.optimization_barrier(tuple(out_cut) + tuple(in_first))[: len(out_cut)]
    out_parts = scatter_quarters(out_cut, ctx_size, fsdp_size)

    def mix(m, x_now, *earlier):
        doc = document_ids(pos, doc_lengths[m, 0])
        table = one_table(pos, doc, rate, scaling)
        joint = jnp.dot(x_now, w_in[:, : 2 * DK + DV], preferred_element_type=jnp.float32).astype(low)
        joint = after(joint, *earlier)
        gate_pre = jnp.dot(x_now, w_in[:, 2 * DK + DV :], preferred_element_type=jnp.float32)
        query, key, value = joint[:, :DK], joint[:, DK : 2 * DK], joint[:, 2 * DK :]
        attend = (contract_rows(query, key) * table).astype(low)
        retained = add_single(attend, value)
        mixed, mix_pull = jax.vjp(gated_mix, gate_pre, retained)
        return table, query, key, value, attend, mix_pull, mixed.astype(low)

    kept = [mix(0, x_all[0])]
    out_parts = lax.optimization_barrier(tuple(out_parts) + (kept[0][4],))[:-1]
    quarter = choose_quarter(out_parts, ctx_rank, fsdp_rank)
    out_first = gather_first(quarter)
    out_second = gather_second(*out_first)
    w_head = by_rank(quarter, *out_first, *out_second)
    cot_own = after(cotangent.reshape(MICRO * tok_rows, width), *out_first)
    cot_first = gather_first(cot_own)
    cot_second = gather_second(*cot_first)
    ffn_cut = lax.optimization_barrier(tuple(ffn_cut) + tuple(cot_second))[: len(ffn_cut)]
    ffn_mine = [xy_swap(ffn_cut[bit - 1], bit) for bit in range(1, fsdp_size)]
    part = add_single(kept[0][6], w_head).astype(low)
    attn_out = [ctx_sum(after(part, *x_all[1:], *cot_first))]
    for m in range(1, MICRO):
        kept.append(mix(m, after(x_all[m], *cot_first), *cot_second))
        part = add_single(kept[m][6], w_head).astype(low)
        attn_out.append(ctx_sum(after(part, *ffn_mine)))
    def enter(m):
        hidden = rows_in[m] + attn_out[m].astype(jnp.float32)
        normed_two, pull_two = jax.vjp(layer_norm, hidden, norm_gains[1], norm_biases[1])
        two_own = normed_two.astype(low)
        return hidden, pull_two, two_own, gather_first(two_own)

    ffn_other = [core_swap(x) for x in ffn_mine]
    entered = [enter(0)]
    up_own, down_own = join_ffn(w_up, w_down, ffn_mine, ffn_other)
    cot_all = [
        place(
            (fsdp_size * tok_rows, width),
            [
                (cot_own, m * tok_rows, tok_rows, 0, 0),
                (cot_first[0], m * tok_rows, tok_rows, tok_rows, 0),
                (cot_second[m], 0, tok_rows, 2 * tok_rows, 0),
                (cot_first[1], m * tok_rows, tok_rows, 3 * tok_rows, 0),
            ],
        )
        for m in range(MICRO)
    ]

    outs = [None] * MICRO
    grad_attn = []
    grad_hidden = []
    ffn_kept = []
    norm_two_terms = []

    for m in range(MICRO):
        hidden, pull_two, two_own, two_first = entered[m]
        if m == 0:
            two_first = lax.optimization_barrier(tuple(two_first) + (up_own, down_own))[:2]
            two_second = gather_second(*two_first)
        two_second = lax.optimization_barrier(tuple(two_second) + (cot_all[m],))[:2]
        two_all = by_offset(two_own, *two_first, *two_second)
        active, slope = smooth_parts(add_single(two_all, up_own))
        active_low, slope = lax.optimization_barrier((active.astype(low), slope))
        grad_up = (back_rows(cot_all[m], down_own) * slope).astype(low)
        norm_part = back_rows(grad_up, up_own).astype(low)
        sent = rows_first(norm_part)
        later = ()
        if m + 1 < MICRO:
            attn_out[m + 1] = after(attn_out[m + 1], *sent)
            entered.append(enter(m + 1))
            sent = lax.optimization_barrier(tuple(sent) + (entered[m + 1][2],))[:2]
            two_second = gather_second(*entered[m + 1][3])
            later = two_second
        grad_norm_two = after(rows_second(norm_part, *sent), *grad_attn[-1:], *later)
        grad_ln, gain_two, bias_two = pull_two(grad_norm_two)
        norm_two_terms.append((gain_two, bias_two))
        total = grad_rows[m] + grad_ln
        grad_hidden.append(total)
        grad_attn.append(total.astype(low))
        ffn_kept.append((two_all, grad_up, active_low, hidden))

    grad_all = [lax.all_gather(grad_attn[m], "ctx", axis=0, tiled=True) for m in range(MICRO)]

    def unmix(m, grad_now):
        table, query, key, value, attend, mix_pull, mixed_low = kept[m]
        grad_mixed = back_rows(grad_now, w_head)
        grad_gate, grad_ret = mix_pull(grad_mixed)
        ret_low = grad_ret.astype(low)
        grad_scores = (contract_rows(ret_low, value) * table).astype(low)
        grad_query = add_single(grad_scores, key).astype(low)
        grad_key = contract_cols(grad_scores, query).astype(low)
        grad_value = contract_cols(attend, ret_low).astype(low)
        return jnp.concatenate([grad_query, grad_key, grad_value, grad_gate.astype(low)], axis=1)

    terms = []
    sums = []
    fill = ()
    for m in range(MICRO):
        grad_now = after(grad_all[m], *(grad_attn[1:] if m == 0 else terms[-1:]), *fill)
        grad_in = unmix(m, grad_now)
        part = back_rows(grad_in, w_in).astype(low)
        terms.append(part)
        sums.append(ctx_sum(after(part, *grad_all[m + 1 :], *sums[-1:])))
        x_now, grad_in = lax.optimization_barrier((x_all[m], grad_in, part))[:2]
        in_now = contract_cols(x_now, grad_in)
        if m == 0:
            in_term = in_now
            sums[m] = after(sums[m], in_term)
            ready = [after(ffn_kept[n][2], part, grad_attn[n]) for n in range(MICRO)]
            fill = tuple(add_single(ready[n], down_own).astype(low) for n in range(MICRO))
        else:
            in_term = (in_term + in_now).astype(low)
    in_view = in_term.reshape(ctx_size, fsdp_size, share, -1)
    in_blocks_out = [pick(in_view, fsdp_rank ^ j, 1, 1)[:, 0] for j in range(fsdp_size)]
    in_sent = reduce_first(in_blocks_out)
    up_grad = sum(contract_cols(k[0], after(k[1], in_term)) for k in ffn_kept).astype(low)
    down_grad = sum(
        contract_cols(after(ready[n], up_grad), cot_all[n]) for n in range(MICRO)
    ).astype(low)
    sums[-1] = after(sums[-1], up_grad, down_grad, *in_sent)
    up_sum = ctx_sum(after(up_grad, sums[-1]))
    down_sum = ctx_sum(after(down_grad, sums[-1]))
    in_sum = reduce_second(in_blocks_out, *in_sent).astype(low)
    out_term = sum(
        contract_cols(after(kept[m][6], down_grad), grad_all[m]) for m in range(MICRO)
    ).astype(low)

    grad_tokens = []
    norm_one_terms = []
    for m in range(MICRO):
        grad_ln, gain_one, bias_one = norm_one[m][1](sums[m].astype(jnp.float32))
        norm_one_terms.append((gain_one, bias_one))
        grad_tokens.append(grad_hidden[m] + grad_ln)

    gain_rows = [sum(t[0] for t in norm_one_terms), sum(t[0] for t in norm_two_terms)]
    bias_rows = [sum(t[1] for t in norm_one_terms), sum(t[1] for t in norm_two_terms)]
    norm_lines = sum_over(jnp.stack(gain_rows + bias_rows), "ctx")
    in_mine = lax.all_to_all(
        after(in_sum, norm_lines), "ctx", split_axis=0, concat_axis=0, tiled=True
    )
    norm_sums = sum_over(norm_lines, "fsdp")
    for n in range(MICRO):
        ffn_part = after(fill[n], in_sum, norm_sums)
        outs[n] = (ffn_kept[n][3] + rows_second(ffn_part, *rows_first(ffn_part))).astype(low)
    out_term = after(out_term, in_sum, norm_sums)
    rows = DV // fsdp_size
    out_blocks = [pick(out_term, fsdp_rank ^ j, rows, 0) for j in range(fsdp_size)]
    g_out = reduce_second(out_blocks, *reduce_first(out_blocks))

    up_view = up_sum.reshape(fsdp_size, share, -1)
    pieces = [lax.dynamic_index_in_dim(up_view, fsdp_rank, 0, keepdims=False)]
    for bit in range(1, fsdp_size):
        pieces.append(
            xy_swap(lax.dynamic_index_in_dim(up_view, fsdp_rank ^ bit, 0, keepdims=False), bit)
        )
    in_mine = after(in_mine, norm_sums)
    def by_head(first, size):
        part = in_mine[:, :, first : first + size].transpose(1, 0, 2)
        return part.reshape(share, -1).astype(jnp.float32) * grad_scale

    g_query = by_head(0, DK)
    g_key = by_head(DK, DK)
    g_value = by_head(2 * DK, DV)
    g_gate = by_head(2 * DK + DV, DV)

    pieces = [p.reshape(share, ctx_size, -1) for p in in_rank_order(pieces, fsdp_rank)]
    g_up = jnp.stack(pieces, axis=2).reshape(share, FF).astype(jnp.float32) * grad_scale
    down_sum = after(down_sum, g_query, g_key, g_value, g_gate, g_up)

    norm_sums = pick(norm_sums, ctx_rank * fsdp_size + fsdp_rank, share, 1) * grad_scale
    return (
        jnp.stack(outs)[:, None],
        jnp.stack(grad_tokens)[:, None],
        g_query,
        g_key,
        g_value,
        g_gate,
        g_out * grad_scale,
        g_up,
        down_sum.astype(jnp.float32) * grad_scale,
        norm_sums[:2],
        norm_sums[2:],
    )


def solution(mesh):
    in_specs = (
        P(None, "fsdp", "ctx", None),
        P(None, "fsdp", "ctx", None),
        P("fsdp", None),
        P("fsdp", None),
        P("fsdp", None),
        P("fsdp", None),
        P("fsdp", None),
        P("fsdp", None),
        P("fsdp", None),
        P(),
        P(),
        P(),
        P(None, "fsdp", None),
    )
    out_specs = (
        P(None, "fsdp", "ctx", None),
        P(None, "fsdp", "ctx", None),
        P(("ctx", "fsdp"), None),
        P(("ctx", "fsdp"), None),
        P(("ctx", "fsdp"), None),
        P(("ctx", "fsdp"), None),
        P(("ctx", "fsdp"), None),
        P(("ctx", "fsdp"), None),
        P(("ctx", "fsdp"), None),
        P(None, ("ctx", "fsdp")),
        P(None, ("ctx", "fsdp")),
    )
    by_heads = mesh.shape["ctx"] == HEADS and mesh.shape["fsdp"] == 4
    chosen = body_heads if by_heads else body
    return jax.shard_map(chosen, mesh=mesh, in_specs=in_specs, out_specs=out_specs, check_vma=False)
```
